32 devices in a mesh: row: 4 (over x, core), col: 8 (over z, y).
Axes of the slice: x: 2, y: 2, z: 4, core: 2. Of those that a mesh axis runs over, the one named last changes fastest.
Arguments:
- latents: bfloat16 [8200, 1536], P('col', 'row'), may hold values from -30 to 30
- conditioning: bfloat16 [1040, 1536], P('col', 'row'), may hold values from -6 to 6
- teacher: bfloat16 [8200, 1536], P('col', 'row'), may hold values from -46 to 46
- gain_attn: float32 [1536], P('row'), may hold values from 0.5 to 1.5
- bias_attn: float32 [1536], P('row'), may hold values from -0.3 to 0.3
- gain_cross: float32 [1536], P('row'), may hold values from 0.5 to 1.5
- bias_cross: float32 [1536], P('row'), may hold values from -1.8 to 1.8
- gain_mlp: float32 [1536], P('row'), may hold values from 0.5 to 1.5
- bias_mlp: float32 [1536], P('row'), may hold values from -1.8 to 1.8
- w_query: bfloat16 [1536, 1536], P('col', 'row'), may hold values from -0.15625 to 0.15625
- w_key: bfloat16 [1536, 1536], P('col', 'row'), may hold values from -0.15625 to 0.15625
- w_value: bfloat16 [1536, 1536], P('col', 'row'), may hold values from -0.15625 to 0.15625
- w_out: bfloat16 [1536, 1536], P('row', 'col'), may hold values from -3 to 3
- w_cross_query: bfloat16 [1536, 1536], P('col', 'row'), may hold values from -0.15625 to 0.15625
- w_cross_key: bfloat16 [1536, 1536], P('col', 'row'), may hold values from -0.15625 to 0.15625
- w_cross_value: bfloat16 [1536, 1536], P('col', 'row'), may hold values from -0.15625 to 0.15625
- w_cross_out: bfloat16 [1536, 1536], P('row', 'col'), may hold values from -1 to 1
- w_gate: bfloat16 [1536, 6144], P('col', 'row'), may hold values from -0.15625 to 0.15625
- w_up: bfloat16 [1536, 6144], P('col', 'row'), may hold values from -0.15625 to 0.15625
- w_down: bfloat16 [6144, 1536], P('row', 'col'), may hold values from -0.078125 to 0.078125
Outputs:
- outputs: bfloat16 [8200, 1536], P('col', 'row')
- loss: float32 [], replicated
- grad_latents: bfloat16 [8200, 1536], P('col', 'row')
- grad_conditioning: bfloat16 [1040, 1536], P('col', 'row')
- grad_w_query: float32 [1536, 1536], P('col', 'row')
- grad_w_key: float32 [1536, 1536], P('col', 'row')
- grad_w_value: float32 [1536, 1536], P('col', 'row')
- grad_w_out: float32 [1536, 1536], P('row', 'col')
- grad_w_cross_query: float32 [1536, 1536], P('col', 'row')
- grad_w_cross_key: float32 [1536, 1536], P('col', 'row')
- grad_w_cross_value: float32 [1536, 1536], P('col', 'row')
- grad_w_cross_out: float32 [1536, 1536], P('row', 'col')
- grad_w_gate: float32 [1536, 6144], P('col', 'row')
- grad_w_up: float32 [1536, 6144], P('col', 'row')
- grad_w_down: float32 [6144, 1536], P('row', 'col')
- grad_gain_attn: float32 [1536], P(('row', 'col'))
- grad_bias_attn: float32 [1536], P(('row', 'col'))
- grad_gain_cross: float32 [1536], P(('row', 'col'))
- grad_bias_cross: float32 [1536], P(('row', 'col'))
- grad_gain_mlp: float32 [1536], P(('row', 'col'))
- grad_bias_mlp: float32 [1536], P(('row', 'col'))
The draws below stay inside these ranges and needn't reach their ends.
All inputs are finite; a program needn't handle non-finite values.
Results may differ from the reference program's by a relative error of at most 0.017.
Values may be sent and summed in bfloat16 or wider, within the bound.
A program may use at most 192 MiB of HBM per device.

```python
import math
import jax
import jax.numpy as jnp
from jax import lax

D = 1536
HEADS = 24
HEAD = 64
ROT = 32
FF = 6144
LEN = 1025
CLEN = 130
CLIPS = 8
TOKENS = 8200
CTOKENS = 1040


def draw_latents(key, part):
    key_feature, key_token, key_base = jax.random.split(key, 3)
    feature_scale = jnp.exp(jax.random.uniform(key_feature, (1, D), jnp.float32, math.log(0.3), math.log(3.0)))
    token_scale = jnp.exp(jax.random.uniform(key_token, (TOKENS, 1), jnp.float32, math.log(0.5), math.log(2.0)))
    base = jnp.clip(jax.random.normal(key_base, (TOKENS, D), jnp.float32), -5.0, 5.0)
    return (base * feature_scale * token_scale).astype(jnp.bfloat16)


def draw_teacher(key, part):
    clip_place = (jnp.arange(TOKENS) // LEN).astype(jnp.float32) / max(CLIPS - 1, 1)
    feature_place = jnp.arange(D).astype(jnp.float32) / max(D - 1, 1)
    scale = (1.0 + 2.0 * clip_place)[:, None] * (1.0 + 2.0 * feature_place)[None, :]
    base = jnp.clip(jax.random.normal(key, (TOKENS, D), jnp.float32), -5.0, 5.0)
    return (base * scale).astype(jnp.bfloat16)


def block_levels(rng, shape, cuts, low, top_value):
    loudness, own = 1.0, jax.random.fold_in(rng, 6)
    for axis_at, parts in cuts:
        steps = jnp.exp(jax.random.uniform(jax.random.fold_in(own, axis_at), (parts,), jnp.float32, low / len(cuts), top_value / len(cuts)))
        loudness = loudness * jnp.repeat(steps, shape[axis_at] // parts).reshape([-1 if axis == axis_at else 1 for axis in range(len(shape))])
    return loudness


def bell_draw(stream_key, dims, scale, bound, cuts=(), kind=jnp.bfloat16):
    entries = jax.random.normal(stream_key, dims, jnp.float32) * scale
    if len(cuts) > 0:
        entries = block_levels(stream_key, dims, cuts, -0.22, 0.18) * entries
    return jnp.clip(entries, min=-bound, max=bound).astype(kind)


def setup_inputs(seed: int = 0) -> dict:
    streams_of = jax.random.split(jax.random.key(seed), 21)
    return {
        "latents": draw_latents(jax.random.fold_in(streams_of[20], 71), 0),
        "conditioning": bell_draw(streams_of[1], (CTOKENS, D), 1.0, 6.0, ((0, 8), (1, 4))),
        "teacher": draw_teacher(jax.random.fold_in(streams_of[20], 71), 0),
        "gain_attn": jnp.clip(1.0 + 0.1 * jax.random.normal(streams_of[3], (D,), jnp.float32), 0.5, 1.5),
        "bias_attn": bell_draw(streams_of[4], (D,), 0.05, 0.3, ((0, 4),), jnp.float32),
        "gain_cross": jnp.clip(1.0 + 0.1 * jax.random.normal(streams_of[5], (D,), jnp.float32), 0.5, 1.5),
        "bias_cross": bell_draw(streams_of[6], (D,), 0.3, 1.8, ((0, 4),), jnp.float32),
        "gain_mlp": jnp.clip(1.0 + 0.1 * jax.random.normal(streams_of[7], (D,), jnp.float32), 0.5, 1.5),
        "bias_mlp": bell_draw(streams_of[8], (D,), 0.3, 1.8, ((0, 4),), jnp.float32),
        "w_query": bell_draw(streams_of[9], (D, D), D ** -0.5, 0.15625, ((0, 8), (1, 4))),
        "w_key": bell_draw(streams_of[10], (D, D), D ** -0.5, 0.15625, ((0, 8), (1, 4))),
        "w_value": bell_draw(streams_of[11], (D, D), D ** -0.5, 0.15625, ((0, 8), (1, 4))),
        "w_out": bell_draw(streams_of[12], (D, D), (max(1, 3 * D // LEN)) ** -0.5, 3.0, ((0, 4), (1, 8))),
        "w_cross_query": bell_draw(streams_of[13], (D, D), D ** -0.5, 0.15625, ((0, 8), (1, 4))),
        "w_cross_key": bell_draw(streams_of[14], (D, D), D ** -0.5, 0.15625, ((0, 8), (1, 4))),
        "w_cross_value": bell_draw(streams_of[15], (D, D), D ** -0.5, 0.15625, ((0, 8), (1, 4))),
        "w_cross_out": bell_draw(streams_of[16], (D, D), (max(1, 3 * D // CLEN)) ** -0.5, 1.0, ((0, 4), (1, 8))),
        "w_gate": bell_draw(streams_of[17], (D, FF), D ** -0.5, 0.15625, ((0, 8), (1, 4))),
        "w_up": bell_draw(streams_of[18], (D, FF), D ** -0.5, 0.15625, ((0, 8), (1, 4))),
        "w_down": bell_draw(streams_of[19], (FF, D), FF ** -0.5, 0.078125, ((0, 4), (1, 8))),
    }


HIGHEST = lax.Precision.HIGHEST
EPSILON = 1e-06

@jax.custom_vjp
def low(v):
    return lax.optimization_barrier(v.astype(jnp.bfloat16)).astype(jnp.float32)

@jax.custom_vjp
def low_back(v):
    return v

def low_keep(v):
    return (low(v), None)

def low_pass(kept, grad):
    return (grad,)

def back_keep(v):
    return (v, None)

def back_low(kept, grad):
    return (low(grad),)
low.defvjp(low_keep, low_pass)
low_back.defvjp(back_keep, back_low)

def matmul(left, right):
    return jnp.dot(left, right, precision=HIGHEST)

def layer_norm(stream, norm_gain, norm_shift):
    average = lax.optimization_barrier(jnp.mean(stream, axis=1, keepdims=True))
    centered = stream - average
    variance = lax.optimization_barrier(jnp.mean(centered * centered, axis=1, keepdims=True))
    return centered * lax.rsqrt(variance + EPSILON) * norm_gain + norm_shift

def rotary_tables(length, rotated):
    half_size = rotated // 2
    position = jnp.arange(length, dtype=jnp.float32)
    frequency = jnp.exp(jnp.arange(half_size, dtype=jnp.float32) * (-2.0 * math.log(10000.0) / rotated))
    angles = position[:, None] * frequency[None, :]
    return (jnp.cos(angles)[:, None, :], jnp.sin(angles)[:, None, :])

def rotate(tensor, cosine, sine):
    half_size = ROT // 2
    front_half = tensor[..., :half_size]
    back_half = tensor[..., half_size:ROT]
    untouched = tensor[..., ROT:]
    return jnp.concatenate([front_half * cosine - back_half * sine, back_half * cosine + front_half * sine, untouched], axis=-1)

def split_heads(matrix, length):
    return matrix.reshape(matrix.shape[0] // length, length, HEADS, HEAD)

def attend_clip(group):
    queries, key_rows, value_rows = group
    scaling = HEAD ** (-0.5)
    raw_scores = low_back(jnp.einsum('qhd,khd->hqk', queries, key_rows, precision=HIGHEST))
    weights = low(jax.nn.softmax(raw_scores * scaling, axis=-1))
    return jnp.einsum('hqk,khd->qhd', weights, value_rows, precision=HIGHEST)

def forward(latents, conditioning, gain_attn, bias_attn, gain_cross, bias_cross, gain_mlp, bias_mlp, w_query, w_key, w_value, w_out, w_cross_query, w_cross_key, w_cross_value, w_cross_out, w_gate, w_up, w_down):
    cosine, sine = rotary_tables(LEN, ROT)
    rows_total = latents.shape[0]
    attend_all = jax.checkpoint(attend_clip)
    first_rows = low(layer_norm(latents, gain_attn, bias_attn))
    queries = low(rotate(split_heads(low_back(matmul(first_rows, w_query)), LEN), cosine, sine))
    key_rows = low(rotate(split_heads(low_back(matmul(first_rows, w_key)), LEN), cosine, sine))
    value_rows = low(split_heads(low_back(matmul(first_rows, w_value)), LEN))
    mixed_self = lax.map(attend_all, (queries, key_rows, value_rows)).reshape(rows_total, D)
    mixed_self = low(low_back(mixed_self))
    stream_one = latents + low_back(matmul(mixed_self, w_out))
    second_rows = low(layer_norm(stream_one, gain_cross, bias_cross))
    cross_queries = low(split_heads(low_back(matmul(second_rows, w_cross_query)), LEN))
    cross_keys = low(split_heads(low_back(matmul(conditioning, w_cross_key)), CLEN))
    cross_values = low(split_heads(low_back(matmul(conditioning, w_cross_value)), CLEN))
    mixed_cross = lax.map(attend_all, (cross_queries, cross_keys, cross_values)).reshape(rows_total, D)
    mixed_cross = low(low_back(mixed_cross))
    stream_two = stream_one + low_back(matmul(mixed_cross, w_cross_out))
    third_rows = low(layer_norm(stream_two, gain_mlp, bias_mlp))
    gate_values = low_back(matmul(third_rows, w_gate))
    up_values = low_back(matmul(third_rows, w_up))
    hidden = low(jax.nn.silu(gate_values) * up_values)
    return stream_two + low_back(matmul(hidden, w_down))

def reference(latents, conditioning, teacher, gain_attn, bias_attn, gain_cross, bias_cross, gain_mlp, bias_mlp, w_query, w_key, w_value, w_out, w_cross_query, w_cross_key, w_cross_value, w_cross_out, w_gate, w_up, w_down):
    inputs = (latents, conditioning, gain_attn, bias_attn, gain_cross, bias_cross, gain_mlp, bias_mlp, w_query, w_key, w_value, w_out, w_cross_query, w_cross_key, w_cross_value, w_cross_out, w_gate, w_up, w_down)
    floats = tuple((item.astype(jnp.float32) for item in inputs))
    final, pullback = jax.vjp(forward, *floats)
    residual = final - teacher.astype(jnp.float32)
    loss = jnp.sum(residual * residual) / (TOKENS * D)
    grads = pullback(residual)
    grad_latents, grad_conditioning, grad_gain_attn, grad_bias_attn, grad_gain_cross, grad_bias_cross, grad_gain_mlp, grad_bias_mlp, grad_w_query, grad_w_key, grad_w_value, grad_w_out, grad_w_cross_query, grad_w_cross_key, grad_w_cross_value, grad_w_cross_out, grad_w_gate, grad_w_up, grad_w_down = grads
    return (final.astype(jnp.bfloat16), loss, grad_latents.astype(jnp.bfloat16), grad_conditioning.astype(jnp.bfloat16), grad_w_query, grad_w_key, grad_w_value, grad_w_out, grad_w_cross_query, grad_w_cross_key, grad_w_cross_value, grad_w_cross_out, grad_w_gate, grad_w_up, grad_w_down, grad_gain_attn, grad_bias_attn, grad_gain_cross, grad_bias_cross, grad_gain_mlp, grad_bias_mlp)
```

```python
import functools
import math

import jax, jax.numpy as jnp
from jax import lax
from jax.sharding import PartitionSpec as P
from jax.experimental import pallas as pl
from jax.experimental.pallas import tpu as pltpu

BF, F32 = jnp.bfloat16, jnp.float32
MESH = pl.DeviceIdType.MESH
TP = 1040
LEN = 1025
CLEN = 130
CP = 144
HEAD = 64
ROT = 32
EPSILON = 1e-06
CH = 208
NCH = TP // CH
SUB = 16


def nt(a, b):
    return lax.dot_general(a, b, (((1,), (1,)), ((), ())), preferred_element_type=F32)


def remote(src, dst, ssem, rsem, dev):
    return pltpu.make_async_remote_copy(src_ref=src, dst_ref=dst, send_sem=ssem, recv_sem=rsem, device_id=dev, device_id_type=MESH)


def ar_kernel(mode, wide, *refs):
    n_in = {"fwd": 5, "out": 4, "bwd": 5}[mode]
    n_out = {"fwd": 2, "out": 4, "bwd": 3}[mode]
    ins, outs, scr = refs[:n_in], refs[n_in:n_in + n_out], refs[n_in + n_out:]
    (ybuf, wbuf, acc, send_a, recv_a, p1, p2, buf1, buf2, low, lsem, s_a, r_a, s_b, r_b, s_c, r_c, s_d, r_d) = scr
    half = wide // 2
    r, col = lax.axis_index("row"), lax.axis_index("col")
    c = lax.rem(r, 2)
    o = 1 - c
    sib = (r + 1 - 2 * c, col)
    xi = lax.div(r, 2)
    par = (r + 2 - 4 * xi, col)

    y_hbm, w_hbm = ins[0], ins[1]
    ycp = pltpu.make_async_copy(y_hbm, ybuf, lsem.at[0])
    wcp = pltpu.make_async_copy(w_hbm, wbuf, lsem.at[1])
    ycp.start()
    wcp.start()
    b1 = pltpu.make_async_copy(ins[2], buf1, lsem.at[2])
    b1.start()
    if mode in ("out", "bwd"):
        b2 = pltpu.make_async_copy(ins[3], buf2, lsem.at[3])
        b2.start()

    barrier = pltpu.get_barrier_semaphore()
    pl.semaphore_signal(barrier, inc=1, device_id=sib, device_id_type=MESH)
    pl.semaphore_signal(barrier, inc=1, device_id=par, device_id_type=MESH)
    pl.semaphore_wait(barrier, 2)
    ycp.wait()
    wcp.wait()

    def rows_of(i):
        return pl.ds(pl.multiple_of(i * CH, 16), CH)

    def copy_a(i):
        return remote(send_a.at[rows_of(i)], recv_a.at[rows_of(i)], s_a.at[i], r_a.at[i], sib)

    def copy_b(i):
        return remote(p1.at[c, rows_of(i)], p2.at[c, rows_of(i)], s_b.at[i], r_b.at[i], par)

    def copy_c(i):
        return remote(p1.at[c, rows_of(i)], p1.at[c, rows_of(i)], s_c.at[i], r_c.at[i], sib)

    def copy_d(i):
        return remote(p2.at[c, rows_of(i)], p2.at[c, rows_of(i)], s_d.at[i], r_d.at[i], sib)

    w_mine = pl.ds(pl.multiple_of(c * half, 128), half)
    w_other = pl.ds(pl.multiple_of(o * half, 128), half)

    def step_b(i):
        copy_a(i).wait_recv()
        p1[c, rows_of(i)] = (acc[rows_of(i)] + recv_a[rows_of(i)].astype(F32)).astype(BF)
        copy_b(i).start()
        copy_c(i).start()

    def first(i, carry):
        yc = ybuf[rows_of(i)]
        send_a[rows_of(i)] = nt(yc, wbuf[w_other]).astype(BF)
        copy_a(i).start()
        acc[rows_of(i)] = nt(yc, wbuf[w_mine])

        @pl.when(i > 0)
        def _():
            step_b(i - 1)

        return carry

    lax.fori_loop(0, NCH, first, 0)
    step_b(NCH - 1)
    b1.wait()
    if mode in ("out", "bwd"):
        b2.wait()

    gain = ins[{"fwd": 3, "out": 0, "bwd": 4}[mode]]
    if mode == "bwd":
        outs[2][...] = jnp.zeros_like(outs[2])
    if mode == "out":
        outs[3][...] = jnp.zeros_like(outs[3])

    def block(k, carry):
        rs = pl.ds(pl.multiple_of(k * SUB, SUB), SUB)
        tot = jnp.concatenate(
            [p1[0, rs].astype(F32) + p2[0, rs].astype(F32), p1[1, rs].astype(F32) + p2[1, rs].astype(F32)], axis=1
        )
        if mode == "fwd":
            x = buf1[rs] + tot
            buf1[rs] = x
            xc = x - jnp.sum(x, axis=1, keepdims=True) * (1.0 / wide)
            inv = lax.rsqrt(jnp.sum(xc * xc, axis=1, keepdims=True) * (1.0 / wide) + EPSILON)
            low[rs] = (xc * inv * gain[...] + ins[4][...]).astype(BF)
        if mode == "out":
            y = buf1[rs] + tot
            pos = k * SUB + lax.broadcasted_iota(jnp.int32, (SUB, wide), 0)
            res = jnp.where(pos < LEN, y - buf2[rs].astype(F32), 0.0)
            buf1[rs] = res
            low[rs] = res.astype(BF)
            send_a_full[rs] = y.astype(BF)
            sq = res * res
            outs[3][...] += sq[:8] + sq[8:]
        if mode == "bwd":
            x = buf2[rs]
            xc = x - jnp.sum(x, axis=1, keepdims=True) * (1.0 / wide)
            inv = lax.rsqrt(jnp.sum(xc * xc, axis=1, keepdims=True) * (1.0 / wide) + EPSILON)
            xh = xc * inv
            e = tot * gain[...]
            m1 = jnp.sum(e, axis=1, keepdims=True) * (1.0 / wide)
            m2 = jnp.sum(e * xh, axis=1, keepdims=True) * (1.0 / wide)
            gnew = buf1[rs] + inv * (e - m1 - xh * m2)
            buf1[rs] = gnew
            low[rs] = gnew.astype(BF)
            dx = tot * xh
            outs[2][0] += dx[:8] + dx[8:]
            outs[2][1] += tot[:8] + tot[8:]
        return carry

    per = CH // SUB
    send_a_full = ybuf if mode == "out" else None

    def out_copies(i):
        cps = [
            pltpu.make_async_copy(buf1.at[rows_of(i)], outs[0].at[rows_of(i)], lsem.at[4 + 2 * i]),
            pltpu.make_async_copy(low.at[rows_of(i)], outs[1].at[rows_of(i)], lsem.at[5 + 2 * i]),
        ]
        return cps

    def second(i, carry):
        copy_b(i).wait_recv()
        copy_d(i).start()

        @pl.when(i > 0)
        def _():
            finish(i - 1)

        return carry

    def finish(i):
        remote(p1.at[o, rows_of(i)], p1.at[o, rows_of(i)], s_c.at[i], r_c.at[i], sib).wait_recv()
        remote(p2.at[o, rows_of(i)], p2.at[o, rows_of(i)], s_d.at[i], r_d.at[i], sib).wait_recv()
        lax.fori_loop(i * per, (i + 1) * per, block, 0)
        for cp in out_copies(i):
            cp.start()

    lax.fori_loop(0, NCH, second, 0)
    finish(NCH - 1)

    def drain(i, carry):
        copy_a(i).wait_send()
        copy_b(i).wait_send()
        copy_c(i).wait_send()
        copy_d(i).wait_send()
        for cp in out_copies(i):
            cp.wait()
        return carry

    lax.fori_loop(0, NCH, drain, 0)
    if mode == "out":
        width = wide // 4
        cp = pltpu.make_async_copy(
            ybuf.at[:, pl.ds(pl.multiple_of(r * width, 128), width)], outs[2], lsem.at[0]
        )
        cp.start()
        cp.wait()


def ar_call(mode, cid, args, k, wide):
    vm = pl.BlockSpec(memory_space=pltpu.VMEM)
    hb = pl.BlockSpec(memory_space=pl.ANY)
    sd = jax.ShapeDtypeStruct
    outs = [sd((TP, wide), F32), sd((TP, wide), BF)]
    ospec = [hb, hb]
    if mode == "out":
        outs += [sd((TP, wide // 4), BF), sd((8, wide), F32)]
        ospec += [hb, vm]
    if mode == "bwd":
        outs += [sd((2, 8, wide), F32)]
        ospec += [vm]
    ispec = {"fwd": [hb, hb, hb, vm, vm], "out": [hb, hb, hb, hb], "bwd": [hb, hb, hb, hb, vm]}[mode]
    half = wide // 2
    ncopies = pltpu.SemaphoreType.DMA((NCH,))
    return pl.pallas_call(
        functools.partial(ar_kernel, mode, wide),
        out_shape=outs,
        in_specs=ispec,
        out_specs=ospec,
        scratch_shapes=[
            pltpu.VMEM((TP, k), BF),
            pltpu.VMEM((wide, k), BF),
            pltpu.VMEM((TP, half), F32),
            pltpu.VMEM((TP, half), BF),
            pltpu.VMEM((TP, half), BF),
            pltpu.VMEM((2, TP, half), BF),
            pltpu.VMEM((2, TP, half), BF),
            pltpu.VMEM((TP, wide), F32),
            pltpu.VMEM((TP, wide), BF if mode == "out" else F32) if mode != "fwd" else pltpu.VMEM((8, 128), F32),
            pltpu.VMEM((TP, wide), BF),
            pltpu.SemaphoreType.DMA((4 + 2 * NCH,)),
        ] + [ncopies] * 8,
        compiler_params=pltpu.CompilerParams(collective_id=cid, has_side_effects=True, vmem_limit_bytes=60 << 20),
        name=f"ar_{mode}_{cid}",
    )(*args)


NEG = -1e30


def nn(a, b):
    return jnp.dot(a, b, preferred_element_type=F32)


def lanes(shape):
    return lax.broadcasted_iota(jnp.int32, shape, len(shape) - 1)


def head_mask(value, which):
    lane = lanes(value.shape)
    keep = (lane < HEAD) if which == 0 else (lane >= HEAD)
    return jnp.where(keep, value, jnp.zeros_like(value))


def attend_rows(q_ref, q_off, k_ref, k_off, v_ref, v_off, keys, valid, out_ref, lse_ref, heads):
    def rows_step(i, carry):
        rows = pl.ds(pl.multiple_of(i * CH, 16), CH)
        lse = jnp.zeros((CH, 128), F32)
        for pair in range(heads // 2):
            qp = q_ref[rows, q_off + 128 * pair:q_off + 128 * (pair + 1)]
            kp = k_ref[:, k_off + 128 * pair:k_off + 128 * (pair + 1)]
            vp = v_ref[:, v_off + 128 * pair:v_off + 128 * (pair + 1)]
            mixed = []
            for which in range(2):
                s = nt(head_mask(qp, which), kp)
                s = jnp.where(lanes((1, keys)) < valid, s, NEG)
                top = jnp.max(s, axis=1, keepdims=True)
                e = jnp.exp(s - top)
                total = jnp.sum(e, axis=1, keepdims=True)
                mixed.append(nn(e.astype(BF), vp) / total)
                lse = jnp.where(lanes(lse.shape) == 2 * pair + which, top + jnp.log(total), lse)
            both = jnp.where(lanes(mixed[0].shape) < HEAD, mixed[0], mixed[1])
            out_ref[rows, 128 * pair:128 * (pair + 1)] = both.astype(BF)
        lse_ref[rows] = lse
        return carry

    lax.fori_loop(0, TP // CH, rows_step, 0)


def attend_back(q_ref, q_off, k_ref, k_off, v_ref, v_off, keys, kblock, valid, do_ref, out_ref, lse_ref, lse_t, delta_t, dqt, emit_q, emit_kv, heads):
    queries = q_ref.shape[0]
    lse_t[...] = lse_ref[...].T
    delta = jnp.zeros((queries, 128), F32)
    for pair in range(heads // 2):
        cols = slice(128 * pair, 128 * (pair + 1))
        prod = do_ref[:, cols].astype(F32) * out_ref[:, cols].astype(F32)
        for which in range(2):
            one = jnp.sum(head_mask(prod, which), axis=1, keepdims=True)
            delta = jnp.where(lanes(delta.shape) == 2 * pair + which, one, delta)
    delta_t[...] = delta.T
    for pair in range(heads // 2):
        qc = slice(q_off + 128 * pair, q_off + 128 * (pair + 1))
        kc = slice(k_off + 128 * pair, k_off + 128 * (pair + 1))
        vc = slice(v_off + 128 * pair, v_off + 128 * (pair + 1))
        oc = slice(128 * pair, 128 * (pair + 1))
        dqt[...] = jnp.zeros_like(dqt)

        def keys_step(j, carry):
            rows = pl.ds(pl.multiple_of(j * kblock, 16), kblock)
            kb, vb = k_ref[rows, kc], v_ref[rows, vc]
            dks, dvs = [], []
            for which in range(2):
                h = 2 * pair + which
                km = head_mask(kb, which)
                p = jnp.exp(nt(km, q_ref[:, qc]) - lse_t[h:h + 1])
                if keys != valid:
                    pos = j * kblock + lax.broadcasted_iota(jnp.int32, (kblock, 1), 0)
                    p = jnp.where(pos < valid, p, 0.0)
                dp = nt(head_mask(vb, which), do_ref[:, oc])
                ds = (p * (dp - delta_t[h:h + 1])).astype(BF)
                dvs.append(nn(p.astype(BF), do_ref[:, oc]))
                dks.append(nn(ds, q_ref[:, qc]))
                dqt[...] += nn(km.T, ds)
            low = lanes(dks[0].shape) < HEAD
            emit_kv(pair, rows, jnp.where(low, dks[0], dks[1]), jnp.where(low, dvs[0], dvs[1]))
            return carry

        lax.fori_loop(0, keys // kblock, keys_step, 0)
        emit_q(pair, dqt[...].T)


def rotate_lanes(u, cos, sin_low, sin_high):
    width = u.shape[-1]
    return u * cos + pltpu.roll(u, width - ROT // 2, u.ndim - 1) * sin_low + pltpu.roll(u, ROT // 2, u.ndim - 1) * sin_high


def qkv_kernel(wide, f, x_ref, g_ref, b_ref, w_ref, cos_ref, lo_ref, hi_ref, h_ref, x0_ref, qkv_ref, a_ref, lse_ref):
    def norm(i, carry):
        rows = pl.ds(pl.multiple_of(i * SUB, SUB), SUB)
        x = x_ref[rows].astype(F32)
        x0_ref[rows] = x
        xc = x - jnp.sum(x, axis=1, keepdims=True) * (1.0 / wide)
        inv = lax.rsqrt(jnp.sum(xc * xc, axis=1, keepdims=True) * (1.0 / wide) + EPSILON)
        h_ref[rows] = (xc * inv * g_ref[...] + b_ref[...]).astype(BF)
        return carry

    lax.fori_loop(0, TP // SUB, norm, 0)

    def project(i, carry):
        rows = pl.ds(pl.multiple_of(i * CH, 16), CH)
        cos, lo, hi = cos_ref[rows], lo_ref[rows], hi_ref[rows]
        valid = i * CH + lax.broadcasted_iota(jnp.int32, (CH, 1), 0) < LEN
        res = nn(h_ref[rows], w_ref[...])
        for part in range(3):
            for pair in range(f // 128):
                at = slice(part * f + pair * 128, part * f + (pair + 1) * 128)
                u = res[:, at]
                if part < 2:
                    u = rotate_lanes(u, cos, lo, hi).astype(BF)
                else:
                    u = u.astype(BF)
                if part == 0:
                    u = u * HEAD ** (-0.5)
                qkv_ref[rows, at] = u
        return carry

    lax.fori_loop(0, TP // CH, project, 0)
    attend_rows(qkv_ref, 0, qkv_ref, f, qkv_ref, 2 * f, TP, LEN, a_ref, lse_ref, f // HEAD)


def vspec():
    return pl.BlockSpec(memory_space=pltpu.VMEM)


def qkv_call(x, g, b, w, tables):
    wide, f = x.shape[1], w.shape[1] // 3
    sd = jax.ShapeDtypeStruct
    return pl.pallas_call(
        functools.partial(qkv_kernel, wide, f),
        out_shape=[sd((TP, wide), BF), sd((TP, wide), F32), sd((TP, 3 * f), BF), sd((TP, f), BF), sd((TP, 128), F32)],
        in_specs=[vspec()] * 7,
        out_specs=[vspec()] * 5,
        compiler_params=pltpu.CompilerParams(vmem_limit_bytes=60 << 20),
        name="qkv_attend",
    )(x, g, b, w, *tables)


def self_back_kernel(f, do_ref, w_ref, qkv_ref, a_ref, lse_ref, cos_ref, lo_ref, hi_ref, out_ref, da, lse_t, delta_t, dqt):
    da[...] = nn(do_ref[...], w_ref[...]).astype(BF)

    def emit_q(pair, dq):
        out_ref[:, 128 * pair:128 * (pair + 1)] = rotate_lanes(dq * HEAD ** (-0.5), cos_ref[...], -lo_ref[...], -hi_ref[...]).astype(BF)

    def emit_kv(pair, rows, dk, dv):
        out_ref[rows, f + 128 * pair:f + 128 * (pair + 1)] = rotate_lanes(dk, cos_ref[rows], -lo_ref[rows], -hi_ref[rows]).astype(BF)
        out_ref[rows, 2 * f + 128 * pair:2 * f + 128 * (pair + 1)] = dv.astype(BF)

    attend_back(qkv_ref, 0, qkv_ref, f, qkv_ref, 2 * f, TP, CH, LEN, da, a_ref, lse_ref, lse_t, delta_t, dqt, emit_q, emit_kv, f // HEAD)


def self_back_call(do, w, qkv, a, lse, tables):
    f = a.shape[1]
    return pl.pallas_call(
        functools.partial(self_back_kernel, f),
        out_shape=jax.ShapeDtypeStruct((TP, 3 * f), BF),
        in_specs=[vspec()] * 8,
        out_specs=vspec(),
        scratch_shapes=[pltpu.VMEM((TP, f), BF), pltpu.VMEM((128, TP), F32), pltpu.VMEM((128, TP), F32), pltpu.VMEM((128, TP), F32)],
        compiler_params=pltpu.CompilerParams(vmem_limit_bytes=60 << 20),
        name="self_back",
    )(do, w, qkv, a, lse, *tables)


def cross_kernel(f, h_ref, cond_ref, wq_ref, wkv_ref, cq_ref, ckv_ref, c_ref, lse_ref):
    ckv_ref[...] = nn(cond_ref[...], wkv_ref[...]).astype(BF)

    def project(i, carry):
        rows = pl.ds(pl.multiple_of(i * CH, 16), CH)
        cq_ref[rows] = nn(h_ref[rows], wq_ref[...]).astype(BF) * HEAD ** (-0.5)
        return carry

    lax.fori_loop(0, TP // CH, project, 0)
    attend_rows(cq_ref, 0, ckv_ref, 0, ckv_ref, f, CP, CLEN, c_ref, lse_ref, f // HEAD)


def cross_call(h, cond, wq, wkv):
    f = wq.shape[1]
    sd = jax.ShapeDtypeStruct
    return pl.pallas_call(
        functools.partial(cross_kernel, f),
        out_shape=[sd((TP, f), BF), sd((CP, 2 * f), BF), sd((TP, f), BF), sd((TP, 128), F32)],
        in_specs=[vspec()] * 4,
        out_specs=[vspec()] * 4,
        compiler_params=pltpu.CompilerParams(vmem_limit_bytes=60 << 20),
        name="cross_attend",
    )(h, cond, wq, wkv)


def cross_back_kernel(f, do_ref, w_ref, cq_ref, ckv_ref, c_ref, lse_ref, dq_ref, dkv_ref, dc, lse_t, delta_t, dqt):
    dc[...] = nn(do_ref[...], w_ref[...]).astype(BF)

    def emit_q(pair, dq):
        dq_ref[:, 128 * pair:128 * (pair + 1)] = (dq * HEAD ** (-0.5)).astype(BF)

    def emit_kv(pair, rows, dk, dv):
        dkv_ref[rows, 128 * pair:128 * (pair + 1)] = dk.astype(BF)
        dkv_ref[rows, f + 128 * pair:f + 128 * (pair + 1)] = dv.astype(BF)

    attend_back(cq_ref, 0, ckv_ref, 0, ckv_ref, f, CP, CP, CLEN, dc, c_ref, lse_ref, lse_t, delta_t, dqt, emit_q, emit_kv, f // HEAD)


def cross_back_call(do, w, cq, ckv, c, lse):
    f = c.shape[1]
    sd = jax.ShapeDtypeStruct
    return pl.pallas_call(
        functools.partial(cross_back_kernel, f),
        out_shape=[sd((TP, f), BF), sd((CP, 2 * f), BF)],
        in_specs=[vspec()] * 6,
        out_specs=[vspec()] * 2,
        scratch_shapes=[pltpu.VMEM((TP, f), BF), pltpu.VMEM((128, TP), F32), pltpu.VMEM((128, TP), F32), pltpu.VMEM((128, TP), F32)],
        compiler_params=pltpu.CompilerParams(vmem_limit_bytes=60 << 20),
        name="cross_back",
    )(do, w, cq, ckv, c, lse)


def tn(left, right):
    return lax.dot_general(left, right, (((0,), (0,)), ((), ())), preferred_element_type=F32)


def rotary_lanes():
    half_size = ROT // 2
    position = jnp.arange(TP, dtype=F32)
    frequency = jnp.exp(jnp.arange(half_size, dtype=F32) * (-2.0 * math.log(10000.0) / ROT))
    angles = position[:, None] * frequency[None, :]
    cos, sin = jnp.cos(angles), jnp.sin(angles)
    one, zero = jnp.ones((TP, HEAD - ROT), F32), jnp.zeros((TP, half_size), F32)
    rest = jnp.zeros((TP, HEAD - ROT), F32)
    tile = lambda *xs: jnp.concatenate(xs + xs, axis=1)
    return tile(cos, cos, one), tile(-sin, zero, rest), tile(zero, sin, rest)


def gather_cols(block):
    return lax.all_gather(block, "row", axis=1, tiled=True)


def own_cols(full, width):
    return lax.dynamic_slice_in_dim(full, lax.axis_index("row") * width, width, axis=1)


def pad_rows(block, rows):
    return jnp.pad(block, ((0, rows - block.shape[0]), (0, 0)))


def body(
    latents,
    conditioning,
    teacher,
    gain_attn,
    bias_attn,
    gain_cross,
    bias_cross,
    gain_mlp,
    bias_mlp,
    w_query,
    w_key,
    w_value,
    w_out,
    w_cross_query,
    w_cross_key,
    w_cross_value,
    w_cross_out,
    w_gate,
    w_up,
    w_down,
):

    wide = latents.shape[1] * lax.axis_size("row")
    F = latents.shape[1]
    FFL = w_gate.shape[1]
    small = jnp.stack([gain_attn, bias_attn, gain_cross, bias_cross, gain_mlp, bias_mlp])
    g1, b1, g2, b2, g3, b3 = jnp.split(gather_cols(small), 6, axis=0)
    x0_low = gather_cols(pad_rows(latents, TP))
    cond_full = gather_cols(pad_rows(conditioning, CP))
    teacher_full = gather_cols(pad_rows(teacher, TP))
    tables = rotary_lanes()
    gather_w = lambda *ws: lax.all_gather(jnp.concatenate(ws, axis=1), "col", axis=0, tiled=True)
    w1 = gather_w(w_query, w_key, w_value)
    w2 = gather_w(w_out.T, w_cross_query, w_cross_key, w_cross_value, w_cross_out.T)
    w3 = gather_w(w_gate, w_up, w_down.T)
    full_out, full_cquery, full_ckv, full_cout = w2[:, :F], w2[:, F:2 * F], w2[:, 2 * F:4 * F], w2[:, 4 * F:]
    full_gate_up, full_down = w3[:, :2 * FFL], w3[:, 2 * FFL:]

    h1, x0, qkv, a, lse1 = qkv_call(x0_low, g1, b1, w1, tables)
    x1, h2 = ar_call("fwd", 0, (a, full_out, x0, g2, b2), F, wide)
    cq, ckv, c, lse2 = cross_call(h2, cond_full, full_cquery, full_ckv)
    x2, h3 = ar_call("fwd", 1, (c, full_cout, x1, g3, b3), F, wide)
    gate_values = nn(h3, full_gate_up[:, :FFL])
    up_values = nn(h3, full_gate_up[:, FFL:])
    hidden = (jax.nn.silu(gate_values) * up_values).astype(BF)
    res, dm, outputs, squares = ar_call("out", 2, (hidden, full_down, x2, teacher_full), FFL, wide)
    count = LEN * wide * lax.axis_size("col")
    loss_part = jnp.sum(squares) / count
    grad_hidden = nn(dm, full_down)
    sigmoid_gate = jax.nn.sigmoid(gate_values)
    grad_gate = (
        grad_hidden * up_values * sigmoid_gate * (1.0 + gate_values * (1.0 - sigmoid_gate))
    ).astype(BF)
    grad_up = (grad_hidden * gate_values * sigmoid_gate).astype(BF)
    grad_gu = jnp.concatenate([grad_gate, grad_up], axis=1)
    scatter_w = lambda *gs: lax.psum_scatter(
        jnp.concatenate([g.astype(BF) for g in gs], axis=1), "col", scatter_dimension=0, tiled=True
    ).astype(F32)
    r3 = scatter_w(tn(h3, grad_gu), tn(dm, hidden))
    gs2, dco, sums3 = ar_call("bwd", 3, (grad_gu, full_gate_up, res, x2, g3), 2 * FFL, wide)
    grad_cq, grad_ckv = cross_back_call(dco, full_cout, cq, ckv, c, lse2)
    grad_conditioning = lax.psum_scatter(
        nt(grad_ckv, full_ckv)[:CLEN].astype(BF), "row", scatter_dimension=1, tiled=True
    )
    gs1, do, sums2 = ar_call("bwd", 4, (grad_cq, full_cquery, gs2, x1, g2), F, wide)
    r2 = scatter_w(tn(do, a), tn(h2, grad_cq), tn(cond_full, grad_ckv), tn(dco, c))
    grad_qkv = self_back_call(do, full_out, qkv, a, lse1, tables)
    r1 = scatter_w(tn(h1, grad_qkv))
    _, glat, sums1 = ar_call("bwd", 5, (grad_qkv, w1, gs1, x0, g1), 3 * F, wide)
    grad_latents = own_cols(glat, F)[:LEN]
    sums = jnp.concatenate([sums1, sums2, sums3]).sum(axis=1)
    sums, loss = lax.psum((own_cols(sums, F), loss_part), "col")
    width = F // lax.axis_size("col")
    vectors = lax.dynamic_slice_in_dim(sums, lax.axis_index("col") * width, width, axis=1)
    gq, gk, gv = jnp.split(r1, 3, axis=1)
    go, gcq, gck, gcv, gco = jnp.split(r2, 5, axis=1)
    ggate, gup, gdown = jnp.split(r3, 3, axis=1)
    return (
        outputs[:LEN], loss, grad_latents, grad_conditioning, gq, gk, gv, go.T, gcq, gck, gcv, gco.T,
        ggate, gup, gdown.T, vectors[0], vectors[1], vectors[2], vectors[3], vectors[4], vectors[5],
    )


def solution(mesh):
    in_specs = (
        P("col", "row"),
        P("col", "row"),
        P("col", "row"),
        P("row"),
        P("row"),
        P("row"),
        P("row"),
        P("row"),
        P("row"),
        P("col", "row"),
        P("col", "row"),
        P("col", "row"),
        P("row", "col"),
        P("col", "row"),
        P("col", "row"),
        P("col", "row"),
        P("row", "col"),
        P("col", "row"),
        P("col", "row"),
        P("row", "col"),
    )
    out_specs = (
        P("col", "row"),
        P(),
        P("col", "row"),
        P("col", "row"),
        P("col", "row"),
        P("col", "row"),
        P("col", "row"),
        P("row", "col"),
        P("col", "row"),
        P("col", "row"),
        P("col", "row"),
        P("row", "col"),
        P("col", "row"),
        P("col", "row"),
        P("row", "col"),
        P(("row", "col")),
        P(("row", "col")),
        P(("row", "col")),
        P(("row", "col")),
        P(("row", "col")),
        P(("row", "col")),
    )
    return jax.shard_map(body, mesh=mesh, in_specs=in_specs, out_specs=out_specs, check_vma=False)
```

```python
import functools
import math

import jax, jax.numpy as jnp
from jax import lax
from jax.sharding import PartitionSpec as P
from jax.experimental import pallas as pl
from jax.experimental.pallas import tpu as pltpu

BF, F32 = jnp.bfloat16, jnp.float32
MESH = pl.DeviceIdType.MESH
TP = 1040
LEN = 1025
CLEN = 130
CP = 144
HEAD = 64
ROT = 32
EPSILON = 1e-06
CH = 208
NCH = TP // CH
SUB = 16


def nt(a, b):
    return lax.dot_general(a, b, (((1,), (1,)), ((), ())), preferred_element_type=F32)


def remote(src, dst, ssem, rsem, dev):
    return pltpu.make_async_remote_copy(src_ref=src, dst_ref=dst, send_sem=ssem, recv_sem=rsem, device_id=dev, device_id_type=MESH)


def tn(left, right):
    return lax.dot_general(left, right, (((0,), (0,)), ((), ())), preferred_element_type=F32)


def row_stats(x, wide):
    xc = x - jnp.sum(x, axis=1, keepdims=True) * (1.0 / wide)
    inv = lax.rsqrt(jnp.sum(xc * xc, axis=1, keepdims=True) * (1.0 / wide) + EPSILON)
    return xc * inv, inv


def rotate_lanes(u, cos, sin_low, sin_high):
    width = u.shape[-1]
    return u * cos + pltpu.roll(u, width - ROT // 2, u.ndim - 1) * sin_low + pltpu.roll(u, ROT // 2, u.ndim - 1) * sin_high


def vspec():
    return pl.BlockSpec(memory_space=pltpu.VMEM)


def hspec():
    return pl.BlockSpec(memory_space=pl.ANY)


class Place:
    def __init__(self, n):
        self.n, self.outer = n, n // 2
        self.r, self.col = lax.axis_index("row"), lax.axis_index("col")
        self.c = lax.rem(self.r, 2)
        self.o = 1 - self.c
        self.xi = lax.div(self.r, 2)
        self.sib = (self.r + 1 - 2 * self.c, self.col)
        self.par = (self.r + 2 - 4 * self.xi, self.col)
        self.diag = (self.par[0] + 1 - 2 * self.c, self.col)
        self.zo, self.yi = lax.div(self.col, 2), lax.rem(self.col, 2)
        self.ypar = (self.r, self.col + 1 - 2 * self.yi)

    def zpeer(self, step):
        return lax.rem(self.zo + step, self.outer)

    def near(self, z):
        gap = z - self.zo
        return jnp.logical_and(gap < 3, gap > -3)

    def enter(self, with_cols, diagonal=False):
        barrier = pltpu.get_barrier_semaphore()
        pl.semaphore_signal(barrier, inc=1, device_id=self.sib, device_id_type=MESH)
        pl.semaphore_signal(barrier, inc=1, device_id=self.par, device_id_type=MESH)
        count = 2
        if diagonal:
            pl.semaphore_signal(barrier, inc=1, device_id=self.diag, device_id_type=MESH)
            count += 1
        if with_cols:
            pl.semaphore_signal(barrier, inc=1, device_id=self.ypar, device_id_type=MESH)

            def greet(step, carry):
                pl.semaphore_signal(barrier, inc=1, device_id=(self.r, 2 * self.zpeer(step) + self.yi), device_id_type=MESH)
                return carry

            lax.fori_loop(1, self.outer, greet, 0)
            count += self.outer
        pl.semaphore_wait(barrier, count)


class ColGather:
    def __init__(self, place, pieces, ahead, ssem, rsem, lsem):
        self.at, self.pieces, self.ahead, self.ssem, self.rsem, self.lsem = place, pieces, ahead, ssem, rsem, lsem
        self.line = place.outer == 4

    def rows(self, p, j):
        size = self.pieces[p][0].shape[0]
        return self.pieces[p][1].at[pl.ds(pl.multiple_of(j * size, 16), size)]

    def local(self, p):
        return pltpu.make_async_copy(self.pieces[p][0], self.rows(p, self.at.col), self.lsem.at[p])

    def send(self, p, slot, j, to, own=False):
        src = self.pieces[p][0] if own else self.rows(p, j)
        return remote(src, self.rows(p, j), self.ssem.at[p, slot], self.rsem.at[p, j], to)

    def across(self, p):
        return self.send(p, 0, self.at.col, self.at.ypar, own=True)

    def outward(self, p, step):
        at = self.at
        return self.send(p, step, at.col, (at.r, 2 * at.zpeer(step) + at.yi), own=True)

    def onward(self, p, step):
        at = self.at
        return self.send(p, at.outer - 1 + step, 2 * at.zpeer(at.outer - step) + at.yi, at.ypar)

    def steps(self, fn, source, far=False):
        at = self.at
        if far and not self.line:
            return

        def one(step):
            if not self.line:
                fn(step)
                return
            near = at.near(at.zpeer(at.outer - step) if source else at.zpeer(step))
            pl.when(jnp.logical_not(near) if far else near)(lambda: fn(step))

        each(1, at.outer, one)

    def relay(self, p, act):
        if not self.line:
            return
        at = self.at
        for mine, source, end in ((2, 0, 3), (1, 3, 0)):
            pl.when(at.zo == mine)(lambda: act(self.send(p, at.n - 1, 2 * source + at.yi, (at.r, 2 * end + at.yi))))

    def start(self, p):
        if p < len(self.pieces):
            self.local(p).start()
            self.across(p).start()
            self.steps(lambda step: self.outward(p, step).start(), False)

    def pass_on(self, p, far):
        def one(step):
            cp = self.onward(p, step)
            cp.wait_recv()
            cp.start()

        self.steps(one, True, far)

    def begin(self):
        for p in range(self.ahead):
            self.start(p)

    def advance(self, p):
        self.pass_on(p, False)
        self.relay(p, lambda cp: cp.start())
        self.start(p + self.ahead)
        if p > 0:
            self.pass_on(p - 1, True)
        if p == len(self.pieces) - 1:
            self.pass_on(p, True)

    def finish(self, p):
        at = self.at
        self.local(p).wait()
        self.across(p).wait_send()
        self.steps(lambda step: self.outward(p, step).wait_send(), False)
        each(0, at.outer, lambda z: self.send(p, 0, 2 * z + 1 - at.yi, at.ypar).wait_recv())
        self.steps(lambda step: self.onward(p, step).wait_send(), True)
        self.steps(lambda step: self.onward(p, step).wait_send(), True, far=True)
        self.relay(p, lambda cp: cp.wait_send())


def gather_sems(pieces, n):
    return [pltpu.SemaphoreType.DMA((pieces, n)), pltpu.SemaphoreType.DMA((pieces, n)), pltpu.SemaphoreType.DMA((pieces,))]


class ColScatter:
    def __init__(self, place, pieces, ahead, slots, bufs, sems):
        self.at, self.pieces, self.ahead, self.slots = place, pieces, ahead, slots
        self.ry, self.hb, self.rz, self.rl, self.ob, self.obt = bufs
        self.ls, self.sy, self.ryr, self.sz, self.rzr, self.rlr, self.os, self.credit = sems
        self.line = place.outer == 4
        self.size = self.hb.shape[2]

    def rows(self, p, j):
        return self.pieces[p][0].at[pl.ds(pl.multiple_of(j * self.size, 16), self.size)]

    def across(self, p, z):
        at = self.at
        return remote(
            self.rows(p, 2 * z + 1 - at.yi), self.ry.at[p % self.slots, z], self.sy.at[p, z], self.ryr.at[p, z], at.ypar
        )

    def own(self, p, z):
        return pltpu.make_async_copy(self.rows(p, 2 * z + self.at.yi), self.hb.at[p % self.slots, z], self.ls.at[p, z])

    def outward(self, p, z):
        at, s = self.at, p % self.slots
        return remote(self.hb.at[s, z], self.rz.at[s, at.zo], self.sz.at[p, z], self.rzr.at[p, at.zo], (at.r, 2 * z + at.yi))

    def detour(self, p, z):
        at, s = self.at, p % self.slots
        via = lax.div(at.zo, 3) + 1
        return remote(self.hb.at[s, z], self.rl.at[s], self.sz.at[p, z], self.rlr.at[p], (at.r, 2 * via + at.yi))

    def merging(self, z):
        zo = self.at.zo
        return jnp.logical_or(jnp.logical_and(zo == 1, z == 3), jnp.logical_and(zo == 2, z == 0))

    def arrives(self, zs):
        return self.at.near(zs)

    def blocks(self, fn):
        each(0, self.size // 48, lambda k: fn(pl.ds(pl.multiple_of(k * 48, 16), 48)))

    def begin(self):
        for p in range(self.ahead):
            self.start(p)

    def start(self, p):
        if p >= len(self.pieces):
            return
        if p >= self.slots:
            pl.semaphore_wait(self.credit.at[p - self.slots], self.at.outer)

        def one(z):
            self.across(p, z).start()
            self.own(p, z).start()

        each(0, self.at.outer, one)

    def reduce(self, p):
        at, s = self.at, p % self.slots

        def one(step):
            z = at.zpeer(step)
            self.own(p, z).wait()
            self.across(p, z).wait_recv()

            def add(rs):
                self.hb[s, z, rs] = (self.hb[s, z, rs].astype(F32) + self.ry[s, z, rs].astype(F32)).astype(BF)

            self.blocks(add)

            @pl.when(z != at.zo)
            def _():
                if not self.line:
                    self.outward(p, z).start()
                    return
                near = at.near(z)
                pl.when(jnp.logical_not(near))(lambda: self.detour(p, z).start())
                pl.when(jnp.logical_and(near, jnp.logical_not(self.merging(z))))(lambda: self.outward(p, z).start())

        each(1, at.outer + 1, one)

    def merge(self, p):
        if not self.line:
            return
        at, s = self.at, p % self.slots
        for mine, z, origin in ((1, 3, 0), (2, 0, 3)):
            @pl.when(at.zo == mine)
            def _():
                remote(self.rl.at[s], self.rl.at[s], self.sz.at[p, z], self.rlr.at[p], at.ypar).wait_recv()

                def add(rs):
                    self.hb[s, z, rs] = (self.hb[s, z, rs].astype(F32) + self.rl[s, rs].astype(F32)).astype(BF)

                self.blocks(add)
                self.outward(p, z).start()

    def result(self, p):
        flip = self.pieces[p][2]
        src = self.obt if flip else self.ob
        return pltpu.make_async_copy(src.at[p % 2], self.pieces[p][1], self.os.at[p])

    def finish(self, p):
        at, s = self.at, p % self.slots
        flip = self.pieces[p][2]
        if p >= 2:
            self.result(p - 2).wait()

        def first(rs):
            self.ob[p % 2, rs] = self.hb[s, at.zo, rs].astype(F32)

        self.blocks(first)

        def one(step):
            zs = at.zpeer(at.outer - step)

            def take():
                remote(self.rz.at[s, zs], self.rz.at[s, zs], self.sz.at[p, zs], self.rzr.at[p, zs], at.ypar).wait_recv()

                def add(rs):
                    self.ob[p % 2, rs] += self.rz[s, zs, rs].astype(F32)

                self.blocks(add)

            if self.line:
                pl.when(at.near(zs))(take)
            else:
                take()

        each(1, at.outer, one)
        if flip:
            self.obt[p % 2] = self.ob[p % 2].T
        self.result(p).start()

        def sent(z):
            self.across(p, z).wait_send()

            @pl.when(z != at.zo)
            def _():
                self.outward(p, z).wait_send()

        each(0, at.outer, sent)
        if p + self.slots < len(self.pieces):
            pl.semaphore_signal(self.credit.at[p], inc=1, device_id=at.ypar, device_id_type=MESH)
            each(
                1,
                at.outer,
                lambda step: pl.semaphore_signal(
                    self.credit.at[p], inc=1, device_id=(at.r, 2 * at.zpeer(step) + at.yi), device_id_type=MESH
                ),
            )

    def advance(self, p):
        if p < len(self.pieces):
            self.reduce(p)
        if 0 <= p - 1 < len(self.pieces):
            self.merge(p - 1)
        if 0 <= p - 2 < len(self.pieces):
            self.finish(p - 2)
        self.start(p + self.ahead)

    def complete(self):
        count = len(self.pieces)
        self.advance(count)
        self.advance(count + 1)
        for p in range(max(0, count - 2), count):
            self.result(p).wait()


def scatter_scratch(pieces, slots, n, f, rows):
    size, outer = rows // n, n // 2
    dma = pltpu.SemaphoreType.DMA
    block = lambda *lead: pltpu.VMEM(lead + (size, f), BF)
    return [
        block(slots, outer), block(slots, outer), block(slots, outer), block(slots),
        pltpu.VMEM((2, size, f), F32), pltpu.VMEM((2, f, size), F32),
    ], [
        dma((pieces, outer)), dma((pieces, outer)), dma((pieces, outer)), dma((pieces, outer)), dma((pieces, outer)),
        dma((pieces,)), dma((pieces,)), pltpu.SemaphoreType.REGULAR((pieces,)),
    ]


class RowGather:
    def __init__(self, place, pieces, ssem, rsem, lsem):
        self.at, self.pieces, self.ssem, self.rsem, self.lsem = place, pieces, ssem, rsem, lsem

    def cols(self, p, j):
        size = self.pieces[p][0].shape[1]
        return self.pieces[p][1].at[:, pl.ds(pl.multiple_of(j * size, 128), size)]

    def copies(self, p):
        at = self.at
        src, mine = self.pieces[p][0], self.cols(p, at.r)
        theirs = self.cols(p, at.par[0])
        return (
            pltpu.make_async_copy(src, mine, self.lsem.at[p]),
            remote(src, mine, self.ssem.at[p, 0], self.rsem.at[p, 0], at.sib),
            remote(src, mine, self.ssem.at[p, 1], self.rsem.at[p, 1], at.par),
            remote(theirs, theirs, self.ssem.at[p, 2], self.rsem.at[p, 2], at.sib),
        )

    def start(self, p):
        for cp in self.copies(p)[:3]:
            cp.start()

    def forward(self, p):
        local, near, far, on = self.copies(p)
        far.wait_recv()
        on.start()

    def finish(self, p):
        local, near, far, on = self.copies(p)
        local.wait()
        near.wait_recv()
        on.wait_recv()
        near.wait_send()
        far.wait_send()
        on.wait_send()


class RowReduce:
    def __init__(self, at, send_a, recv_a, acc, p1, p2, sems):
        self.at, self.send_a, self.recv_a, self.acc, self.p1, self.p2 = at, send_a, recv_a, acc, p1, p2
        self.s_a, self.r_a, self.s_b, self.r_b, self.s_c, self.r_c, self.s_d, self.r_d = sems
        self.half = p1.shape[2]

    def copy_a(self, i):
        rows = rows_of(i)
        return remote(self.send_a.at[rows], self.recv_a.at[rows], self.s_a.at[i], self.r_a.at[i], self.at.sib)

    def copy_b(self, i):
        rows, c = rows_of(i), self.at.c
        return remote(self.p1.at[c, rows], self.p2.at[c, rows], self.s_b.at[i], self.r_b.at[i], self.at.par)

    def copy_c(self, i, side):
        rows = rows_of(i)
        return remote(self.p1.at[side, rows], self.p1.at[side, rows], self.s_c.at[i], self.r_c.at[i], self.at.sib)

    def copy_d(self, i, side):
        rows = rows_of(i)
        return remote(self.p2.at[side, rows], self.p2.at[side, rows], self.s_d.at[i], self.r_d.at[i], self.at.sib)

    def partial(self, i, value, w):
        c, o, half = self.at.c, self.at.o, self.half
        self.send_a[rows_of(i)] = nt(value, w[pl.ds(pl.multiple_of(o * half, 128), half)]).astype(BF)
        self.copy_a(i).start()
        self.acc[lax.rem(i, 2)] = nt(value, w[pl.ds(pl.multiple_of(c * half, 128), half)])

    def swap(self, i):
        self.copy_a(i).wait_recv()
        self.p1[self.at.c, rows_of(i)] = (self.acc[lax.rem(i, 2)] + self.recv_a[rows_of(i)].astype(F32)).astype(BF)
        self.copy_b(i).start()
        self.copy_c(i, self.at.c).start()

    def share(self, i):
        self.copy_b(i).wait_recv()
        self.copy_d(i, self.at.c).start()

    def ready(self, i):
        self.copy_c(i, self.at.o).wait_recv()
        self.copy_d(i, self.at.o).wait_recv()

    def total(self, rs):
        p1, p2 = self.p1, self.p2
        return jnp.concatenate(
            [p1[0, rs].astype(F32) + p2[0, rs].astype(F32), p1[1, rs].astype(F32) + p2[1, rs].astype(F32)], axis=1
        )

    def drain(self, i):
        self.copy_a(i).wait_send()
        self.copy_b(i).wait_send()
        self.copy_c(i, self.at.c).wait_send()
        self.copy_d(i, self.at.c).wait_send()


def reduce_scratch(wide, both):
    half = wide // 2
    out = [
        pltpu.VMEM((TP, half), BF), pltpu.VMEM((TP, half), BF), pltpu.VMEM((2, CH, half), F32),
        pltpu.VMEM((2, TP, half), BF), pltpu.VMEM((2, TP, half), BF),
    ]
    if both:
        out.append(pltpu.VMEM((2, TP, half), BF))
    return out + [pltpu.SemaphoreType.DMA((NCH,))] * (16 if both else 8)


def rows_of(i):
    return pl.ds(pl.multiple_of(i * CH, 16), CH)


def each(low, high, fn):
    def body(i, carry):
        fn(i)
        return carry

    lax.fori_loop(low, high, body, 0)


def sub_blocks(i, fn):
    each(0, CH // SUB, lambda k: fn(k, pl.ds(pl.multiple_of(i * CH + k * SUB, SUB), SUB), pl.ds(pl.multiple_of(k * SUB, SUB), SUB)))


def mid_kernel(n, f, nbg, ahead, *refs):
    refs = list(refs)
    take = lambda count: [refs.pop(0) for _ in range(count)]
    a_hbm, x0_hbm, vecs, cond_ref, wo_hbm, wq_hbm, wk_hbm, wv_hbm, wc_hbm = take(9)
    bg_in = take(nbg)
    x1_out, h2_out, cq_ref, ckv_ref, c_ref, lse_ref, x2_out, h3_out = take(8)
    bg_out = take(nbg)
    a_buf, x0_buf, x_buf, low, wo, wq, wk, wv, wc, lsem, osem = take(11)
    send_a, recv_a, acc, p1, p2, p2b = take(6)
    sems = take(16)
    at = Place(n)
    wide = x_buf.shape[1]
    first = RowReduce(at, send_a, recv_a, acc, p1, p2, sems[:8])
    second = RowReduce(at, send_a, recv_a, acc, p1, p2b, sems[8:])
    gather = ColGather(at, list(zip(bg_in, bg_out)), ahead, *take(3)) if nbg else None
    loads = [
        pltpu.make_async_copy(src, dst, lsem.at[k])
        for k, (src, dst) in enumerate(
            ((a_hbm, a_buf), (wo_hbm, wo), (wk_hbm, wk), (wv_hbm, wv), (x0_hbm, x0_buf), (wq_hbm, wq), (wc_hbm, wc))
        )
    ]
    for cp in loads:
        cp.start()
    at.enter(nbg > 0)
    gather.begin()
    for cp in loads[:2]:
        cp.wait()

    def project(i):
        first.partial(i, a_buf[rows_of(i)], wo)
        pl.when(i > 0)(lambda: first.swap(i - 1))

    each(0, NCH, project)
    first.swap(NCH - 1)
    for cp in loads[2:]:
        cp.wait()
    ckv_ref[:, :f] = nn(cond_ref[...], wk[...]).astype(BF)
    ckv_ref[:, f:] = nn(cond_ref[...], wv[...]).astype(BF)

    def outs(i, main, lowest, which):
        return [
            pltpu.make_async_copy(x_buf.at[rows_of(i)], main.at[rows_of(i)], osem.at[which, 2 * i]),
            pltpu.make_async_copy(low.at[rows_of(i)], lowest.at[rows_of(i)], osem.at[which, 2 * i + 1]),
        ]

    def hook(slot):
        for k in range(nbg):
            pl.when(slot == k * 2 * NCH // nbg)(lambda: gather.advance(k))

    def cross(i):
        first.ready(i)

        def block(k, rs, ls):
            x = x0_buf[rs].astype(F32) + first.total(rs)
            x_buf[rs] = x
            low[rs] = (row_stats(x, wide)[0] * vecs[2:3] + vecs[3:4]).astype(BF)

        sub_blocks(i, block)
        for cp in outs(i, x1_out, h2_out, 0):
            cp.start()
        rows = rows_of(i)
        cq_ref[rows] = nn(low[rows], wq[...]).astype(BF) * HEAD ** (-0.5)
        attend_step(i, cq_ref, 0, ckv_ref, 0, ckv_ref, f, CP, CLEN, c_ref, lse_ref, f // HEAD)
        first.drain(i)
        second.partial(i, c_ref[rows], wc)
        pl.when(i > 0)(lambda: second.swap(i - 1))

    def step(i):
        first.share(i)
        pl.when(i > 0)(lambda: cross(i - 1))
        hook(i)

    each(0, NCH, step)
    cross(NCH - 1)
    second.swap(NCH - 1)

    def last(i):
        second.ready(i)
        for cp in outs(i, x1_out, h2_out, 0):
            cp.wait()

        def block(k, rs, ls):
            x = x_buf[rs] + second.total(rs)
            x_buf[rs] = x
            low[rs] = (row_stats(x, wide)[0] * vecs[4:5] + vecs[5:6]).astype(BF)

        sub_blocks(i, block)
        for cp in outs(i, x2_out, h3_out, 1):
            cp.start()

    def step_two(i):
        second.share(i)
        pl.when(i > 0)(lambda: last(i - 1))
        hook(NCH + i)

    each(0, NCH, step_two)
    last(NCH - 1)
    for k in range(nbg):
        gather.finish(k)

    def end(i):
        second.drain(i)
        for cp in outs(i, x2_out, h3_out, 1):
            cp.wait()

    each(0, NCH, end)


def mid_call(cid, n, a, x0, vecs, cond, wo, wq, wk, wv, wc, bg, ahead=4):
    f, wide, nbg = a.shape[1], x0.shape[1], len(bg)
    sd = jax.ShapeDtypeStruct
    dma = pltpu.SemaphoreType.DMA
    weight = lambda: pltpu.VMEM((wide, f), BF)
    return pl.pallas_call(
        functools.partial(mid_kernel, n, f, nbg, ahead),
        out_shape=[
            sd((TP, wide), F32), sd((TP, wide), BF), sd((TP, f), BF), sd((CP, 2 * f), BF), sd((TP, f), BF), sd((TP, 128), F32),
            sd((TP, wide), F32), sd((TP, wide), BF),
        ] + [sd((n * b.shape[0], b.shape[1]), BF) for b in bg],
        in_specs=[hspec()] * 2 + [vspec()] * 2 + [hspec()] * (5 + nbg),
        out_specs=[hspec()] * 2 + [vspec()] * 4 + [hspec()] * (2 + nbg),
        scratch_shapes=[
            pltpu.VMEM((TP, f), BF), pltpu.VMEM((TP, wide), BF), pltpu.VMEM((TP, wide), F32), pltpu.VMEM((TP, wide), BF),
            weight(), weight(), weight(), weight(), weight(), dma((7,)), dma((2, 2 * NCH)),
        ] + reduce_scratch(wide, True) + (gather_sems(nbg, n) if nbg else []),
        compiler_params=pltpu.CompilerParams(collective_id=cid, has_side_effects=True, vmem_limit_bytes=60 << 20),
        name="mid",
    )(a, x0, vecs, cond, wo, wq, wk, wv, wc, *bg)


NEG = -1e30


def nn(a, b):
    return jnp.dot(a, b, preferred_element_type=F32)


def lanes(shape):
    return lax.broadcasted_iota(jnp.int32, shape, len(shape) - 1)


def head_mask(value, which):
    lane = lanes(value.shape)
    keep = (lane < HEAD) if which == 0 else (lane >= HEAD)
    return jnp.where(keep, value, jnp.zeros_like(value))


def attend_step(i, q_ref, q_off, k_ref, k_off, v_ref, v_off, keys, valid, out_ref, lse_ref, heads, hook=None):
    rows = rows_of(i)
    lse = jnp.zeros((CH, 128), F32)
    for pair in range(heads // 2):
        qp = q_ref[rows, q_off + 128 * pair:q_off + 128 * (pair + 1)]
        kp = k_ref[:, k_off + 128 * pair:k_off + 128 * (pair + 1)]
        vp = v_ref[:, v_off + 128 * pair:v_off + 128 * (pair + 1)]
        mixed = []
        for which in range(2):
            s = nt(head_mask(qp, which), kp)
            s = jnp.where(lanes((1, keys)) < valid, s, NEG)
            top = jnp.max(s, axis=1, keepdims=True)
            e = jnp.exp(s - top)
            total = jnp.sum(e, axis=1, keepdims=True)
            mixed.append(nn(e.astype(BF), vp) / total)
            lse = jnp.where(lanes(lse.shape) == 2 * pair + which, top + jnp.log(total), lse)
        both = jnp.where(lanes(mixed[0].shape) < HEAD, mixed[0], mixed[1])
        out_ref[rows, 128 * pair:128 * (pair + 1)] = both.astype(BF)
        if hook is not None:
            hook(pair)
    lse_ref[rows] = lse


def attend_back(q_ref, q_off, k_ref, k_off, v_ref, v_off, keys, kblock, valid, do_ref, out_ref, lse_ref, lse_t, delta_t, dqt, emit_q, emit_kv, heads, hook=None):
    queries = q_ref.shape[0]
    lse_t[...] = lse_ref[...].T
    delta = jnp.zeros((queries, 128), F32)
    for pair in range(heads // 2):
        cols = slice(128 * pair, 128 * (pair + 1))
        prod = do_ref[:, cols].astype(F32) * out_ref[:, cols].astype(F32)
        for which in range(2):
            one = jnp.sum(head_mask(prod, which), axis=1, keepdims=True)
            delta = jnp.where(lanes(delta.shape) == 2 * pair + which, one, delta)
    delta_t[...] = delta.T
    for pair in range(heads // 2):
        qc = slice(q_off + 128 * pair, q_off + 128 * (pair + 1))
        kc = slice(k_off + 128 * pair, k_off + 128 * (pair + 1))
        vc = slice(v_off + 128 * pair, v_off + 128 * (pair + 1))
        oc = slice(128 * pair, 128 * (pair + 1))
        dqt[...] = jnp.zeros_like(dqt)

        def keys_step(j, carry):
            rows = pl.ds(pl.multiple_of(j * kblock, 16), kblock)
            kb, vb = k_ref[rows, kc], v_ref[rows, vc]
            dks, dvs = [], []
            for which in range(2):
                h = 2 * pair + which
                km = head_mask(kb, which)
                p = jnp.exp(nt(km, q_ref[:, qc]) - lse_t[h:h + 1])
                if keys != valid:
                    pos = j * kblock + lax.broadcasted_iota(jnp.int32, (kblock, 1), 0)
                    p = jnp.where(pos < valid, p, 0.0)
                dp = nt(head_mask(vb, which), do_ref[:, oc])
                ds = (p * (dp - delta_t[h:h + 1])).astype(BF)
                dvs.append(nn(p.astype(BF), do_ref[:, oc]))
                dks.append(nn(ds, q_ref[:, qc]))
                dqt[...] += nn(km.T, ds)
            low = lanes(dks[0].shape) < HEAD
            emit_kv(pair, rows, jnp.where(low, dks[0], dks[1]), jnp.where(low, dvs[0], dvs[1]))
            if hook is not None:
                hook(pair, j)
            return carry

        lax.fori_loop(0, keys // kblock, keys_step, 0)
        emit_q(pair, dqt[...].T)


def rotate_lanes(u, cos, sin_low, sin_high):
    width = u.shape[-1]
    return u * cos + pltpu.roll(u, width - ROT // 2, u.ndim - 1) * sin_low + pltpu.roll(u, ROT // 2, u.ndim - 1) * sin_high


def front_kernel(n, f, nbg, ahead, *refs):
    refs = list(refs)
    take = lambda count: [refs.pop(0) for _ in range(count)]
    lat, teach, cond, small = take(4)
    cos_ref, lo_ref, hi_ref = take(3)
    shards = take(3 + nbg)
    x_ref, h_ref, qkv_ref, a_ref, lse_ref, small_ref, teach_ref, cond_ref = take(8)
    fulls = take(3 + nbg)
    rows_sems, col_sems = take(3), take(3)
    at = Place(n)
    wide = x_ref.shape[1]
    rowg = RowGather(at, [(lat, x_ref), (small, small_ref), (cond, cond_ref), (teach, teach_ref)], *rows_sems)
    colg = ColGather(at, list(zip(shards, fulls)), ahead, *col_sems)
    at.enter(True)
    rowg.start(0)
    rowg.start(1)
    colg.begin()
    rowg.forward(0)
    rowg.forward(1)
    colg.advance(0)
    rowg.finish(0)
    rowg.finish(1)
    rowg.start(2)
    rowg.start(3)

    def norm(i, carry):
        rows = pl.ds(pl.multiple_of(i * SUB, SUB), SUB)
        h_ref[rows] = (row_stats(x_ref[rows].astype(F32), wide)[0] * small_ref[0:1] + small_ref[1:2]).astype(BF)
        return carry

    lax.fori_loop(0, TP // SUB, norm, 0)
    for k in (1, 2):
        colg.advance(k)
    rowg.forward(2)

    for part in range(3):
        colg.finish(part)
        if part > 0:
            colg.advance(part + 2)

        def project(i, carry):
            rows = pl.ds(pl.multiple_of(i * CH, 16), CH)
            cos, lo, hi = cos_ref[rows], lo_ref[rows], hi_ref[rows]
            res = nn(h_ref[rows], fulls[part][...])
            for pair in range(f // 128):
                u = res[:, pair * 128:(pair + 1) * 128]
                if part < 2:
                    u = rotate_lanes(u, cos, lo, hi).astype(BF)
                else:
                    u = u.astype(BF)
                if part == 0:
                    u = u * HEAD ** (-0.5)
                qkv_ref[rows, part * f + pair * 128:part * f + (pair + 1) * 128] = u
            return carry

        lax.fori_loop(0, TP // CH, project, 0)

    def attend(i):
        def hook(pair):
            for k in range(5, 3 + nbg):
                pl.when(i * 3 + pair == (k - 5) * 15 // (nbg - 2))(lambda: colg.advance(k))

        attend_step(i, qkv_ref, 0, qkv_ref, f, qkv_ref, 2 * f, TP, LEN, a_ref, lse_ref, f // HEAD, hook)

    each(0, NCH, attend)
    rowg.forward(3)
    for k in range(3, 3 + nbg):
        colg.finish(k)
    rowg.finish(2)
    rowg.finish(3)


def front_call(cid, n, lat, teach, cond, small, tables, shards, ahead=4):
    f, nbg = shards[0].shape[1], len(shards) - 3
    wide = 4 * f
    sd = jax.ShapeDtypeStruct
    fulls = [sd((n * s.shape[0], s.shape[1]), BF) for s in shards]
    return pl.pallas_call(
        functools.partial(front_kernel, n, f, nbg, ahead),
        out_shape=[
            sd((TP, wide), BF), sd((TP, wide), BF), sd((TP, 3 * f), BF), sd((TP, f), BF), sd((TP, 128), F32),
            sd((8, wide), F32), sd((TP, wide), BF), sd((CP, wide), BF),
        ] + fulls,
        in_specs=[hspec()] * 4 + [vspec()] * 3 + [hspec()] * len(shards),
        out_specs=[vspec()] * 6 + [hspec()] * 2 + [vspec()] * 3 + [hspec()] * nbg,
        scratch_shapes=[pltpu.SemaphoreType.DMA((4, 3)), pltpu.SemaphoreType.DMA((4, 3)), pltpu.SemaphoreType.DMA((4,))] + gather_sems(len(shards), n),
        compiler_params=pltpu.CompilerParams(collective_id=cid, has_side_effects=True, vmem_limit_bytes=60 << 20),
        name="front",
    )(lat, teach, cond, small, *tables, *shards)


def mlp_kernel(n, f, nbg, *refs):
    refs = list(refs)
    take = lambda count: [refs.pop(0) for _ in range(count)]
    parts = 4
    h_hbm, x_hbm, t_hbm = take(3)
    gates, ups = take(parts), take(parts)
    downs = take(parts - nbg)
    bg_in = take(nbg)
    res_out, y_out, sq_ref, dg_out, du_out, gw_out = take(6)
    (h, wg, wu, wd, hid, sg, tt, dm, acc, send_a, recv_a, p1, p2, xbuf, tbuf, rbuf, ybuf, stage) = take(18)
    (wsem, hsem, xsem, tsem, rsem, ysem, dsem, gsem, s_a, r_a, s_b, r_b, s_c, r_c, s_d, r_d) = take(16)
    at = Place(n)
    wide = h.shape[1]
    half = wide // 2
    c, o, sib, par = at.c, at.o, at.sib, at.par
    col = lambda k: slice(k * f, (k + 1) * f)
    gather = ColGather(at, [(b, wd.at[:, col(parts - nbg + k)]) for k, b in enumerate(bg_in)], nbg, *take(3)) if nbg else None

    hcp = pltpu.make_async_copy(h_hbm, h, hsem.at[0])
    hcp.start()
    loads = []
    for k in range(parts):
        loads.append(pltpu.make_async_copy(gates[k], wg.at[:, col(k)], wsem.at[k]))
        loads.append(pltpu.make_async_copy(ups[k], wu.at[:, col(k)], wsem.at[parts + k]))
    late = [pltpu.make_async_copy(d, wd.at[:, col(k)], wsem.at[2 * parts + k]) for k, d in enumerate(downs)]
    for cp in loads + late:
        cp.start()
    at.enter(nbg > 0)
    if nbg:
        gather.begin()
    hcp.wait()
    sq_ref[...] = jnp.zeros_like(sq_ref)

    def rows_of(i):
        return pl.ds(pl.multiple_of(i * CH, 16), CH)

    def slot_in(i):
        return [
            pltpu.make_async_copy(x_hbm.at[rows_of(i)], xbuf.at[lax.rem(i, 2)], xsem.at[lax.rem(i, 2)]),
            pltpu.make_async_copy(t_hbm.at[rows_of(i)], tbuf.at[lax.rem(i, 2)], tsem.at[lax.rem(i, 2)]),
        ]

    def copy_a(i):
        return remote(send_a.at[rows_of(i)], recv_a.at[rows_of(i)], s_a.at[i], r_a.at[i], sib)

    def copy_b(i):
        return remote(p1.at[c, rows_of(i)], p2.at[c, rows_of(i)], s_b.at[i], r_b.at[i], par)

    def copy_c(i, side):
        return remote(p1.at[side, rows_of(i)], p1.at[side, rows_of(i)], s_c.at[i], r_c.at[i], sib)

    def copy_d(i, side):
        return remote(p2.at[side, rows_of(i)], p2.at[side, rows_of(i)], s_d.at[i], r_d.at[i], sib)

    for k in range(parts):
        loads[2 * k].wait()
        loads[2 * k + 1].wait()

        def hidden(i, carry):
            rows = rows_of(i)
            gate = nn(h[rows], wg[:, col(k)])
            up = nn(h[rows], wu[:, col(k)])
            sig = jax.nn.sigmoid(gate)
            act = gate * sig
            hid[rows, col(k)] = (act * up).astype(BF)
            sg[rows, col(k)] = act.astype(BF)
            tt[rows, col(k)] = (up * sig * (1.0 + gate * (1.0 - sig))).astype(BF)
            return carry

        lax.fori_loop(0, NCH, hidden, 0)
    for cp in late:
        cp.wait()
    for k in range(nbg):
        gather.advance(k)
    for k in range(nbg):
        gather.finish(k)
    for i in range(2):
        for cp in slot_in(i):
            cp.start()

    w_mine = pl.ds(pl.multiple_of(c * half, 128), half)
    w_other = pl.ds(pl.multiple_of(o * half, 128), half)

    def step_b(i):
        copy_a(i).wait_recv()
        p1[c, rows_of(i)] = (acc[rows_of(i)] + recv_a[rows_of(i)].astype(F32)).astype(BF)
        copy_b(i).start()
        copy_c(i, c).start()

    def first(i, carry):
        yc = hid[rows_of(i)]
        send_a[rows_of(i)] = nt(yc, wd[w_other]).astype(BF)
        copy_a(i).start()
        acc[rows_of(i)] = nt(yc, wd[w_mine])

        @pl.when(i > 0)
        def _():
            step_b(i - 1)

        return carry

    lax.fori_loop(0, NCH, first, 0)
    step_b(NCH - 1)
    per = CH // SUB

    def outs_of(i):
        slot = lax.rem(i, 2)
        return [
            pltpu.make_async_copy(rbuf.at[slot], res_out.at[rows_of(i)], rsem.at[slot]),
            pltpu.make_async_copy(ybuf.at[slot], y_out.at[rows_of(i)], ysem.at[slot]),
        ]

    def grads_of(i):
        return [
            pltpu.make_async_copy(sg.at[rows_of(i)], du_out.at[rows_of(i)], dsem.at[2 * i]),
            pltpu.make_async_copy(tt.at[rows_of(i)], dg_out.at[rows_of(i)], dsem.at[2 * i + 1]),
        ]

    def finish(i):
        slot = lax.rem(i, 2)
        copy_c(i, o).wait_recv()
        copy_d(i, o).wait_recv()
        for cp in slot_in(i):
            cp.wait()

        @pl.when(i >= 2)
        def _():
            for cp in outs_of(i - 2):
                cp.wait()

        def block(k, carry):
            rs = pl.ds(pl.multiple_of(i * CH + k * SUB, SUB), SUB)
            ls = pl.ds(pl.multiple_of(k * SUB, SUB), SUB)
            tot = jnp.concatenate(
                [p1[0, rs].astype(F32) + p2[0, rs].astype(F32), p1[1, rs].astype(F32) + p2[1, rs].astype(F32)], axis=1
            )
            y = xbuf[slot, ls] + tot
            pos = i * CH + k * SUB + lax.broadcasted_iota(jnp.int32, (SUB, wide), 0)
            res = jnp.where(pos < LEN, y - tbuf[slot, ls].astype(F32), 0.0)
            rbuf[slot, ls] = res
            dm[rs] = res.astype(BF)
            ybuf[slot, ls] = y.astype(BF)
            sq = res * res
            sq_ref[...] += sq[:8] + sq[8:]
            return carry

        lax.fori_loop(0, per, block, 0)
        for cp in outs_of(i):
            cp.start()

        @pl.when(i < NCH - 2)
        def _():
            for cp in slot_in(i + 2):
                cp.start()

        for k in range(parts):
            dh = nn(dm[rows_of(i)], wd[:, col(k)])
            tt[rows_of(i), col(k)] = (dh * tt[rows_of(i), col(k)].astype(F32)).astype(BF)
            sg[rows_of(i), col(k)] = (dh * sg[rows_of(i), col(k)].astype(F32)).astype(BF)
        for cp in grads_of(i):
            cp.start()

    def second(i, carry):
        copy_b(i).wait_recv()
        copy_d(i, c).start()

        @pl.when(i > 0)
        def _():
            finish(i - 1)

        return carry

    lax.fori_loop(0, NCH, second, 0)
    finish(NCH - 1)

    block_rows = stage.shape[1]
    steps = wide // block_rows

    def stored(q, j):
        rows = pl.ds(pl.multiple_of(j * block_rows, 128), block_rows)
        slot = lax.rem(j, 2)
        return pltpu.make_async_copy(stage.at[slot], gw_out.at[rows, q * parts * f:(q + 1) * parts * f], gsem.at[slot])

    for q, (left, right) in enumerate(((h, tt), (h, sg), (dm, hid))):
        def grad(j, carry):
            at_cols = pl.ds(pl.multiple_of(j * block_rows, 128), block_rows)

            @pl.when(j >= 2)
            def _():
                stored(q, j - 2).wait()

            stage[lax.rem(j, 2)] = tn(left[:, at_cols], right[...]).astype(BF)
            stored(q, j).start()
            return carry

        lax.fori_loop(0, steps, grad, 0)
        stored(q, steps - 2).wait()
        stored(q, steps - 1).wait()

    def drain(i, carry):
        copy_a(i).wait_send()
        copy_b(i).wait_send()
        copy_c(i, c).wait_send()
        copy_d(i, c).wait_send()
        for cp in grads_of(i):
            cp.wait()
        return carry

    lax.fori_loop(0, NCH, drain, 0)
    for i in range(NCH - 2, NCH):
        for cp in outs_of(i):
            cp.wait()


def mlp_call(cid, n, h, x, teach, gates, ups, downs, bg):
    wide, f = h.shape[1], gates[0].shape[1]
    half, nbg = wide // 2, len(bg)
    sd = jax.ShapeDtypeStruct
    dma = pltpu.SemaphoreType.DMA
    full = lambda: pltpu.VMEM((TP, wide), BF)
    weight = lambda: pltpu.VMEM((wide, 4 * f), BF)
    scratch = [full(), weight(), weight(), weight(), full(), full(), full(), full()] + [
        pltpu.VMEM((TP, half), F32),
        pltpu.VMEM((TP, half), BF),
        pltpu.VMEM((TP, half), BF),
        pltpu.VMEM((2, TP, half), BF),
        pltpu.VMEM((2, TP, half), BF),
        pltpu.VMEM((2, CH, wide), F32),
        pltpu.VMEM((2, CH, wide), BF),
        pltpu.VMEM((2, CH, wide), F32),
        pltpu.VMEM((2, CH, wide), BF),
        pltpu.VMEM((2, 256, wide), BF),
        dma((12,)), dma((1,)), dma((2,)), dma((2,)), dma((2,)), dma((2,)), dma((2 * NCH,)), dma((2,)),
    ] + [dma((NCH,))] * 8
    if nbg:
        scratch += gather_sems(nbg, n)
    return pl.pallas_call(
        functools.partial(mlp_kernel, n, f, nbg),
        out_shape=[
            sd((TP, wide), F32), sd((TP, wide), BF), sd((8, wide), F32), sd((TP, 4 * f), BF), sd((TP, 4 * f), BF), sd((wide, 12 * f), BF),
        ],
        in_specs=[hspec()] * (3 + 8 + len(downs) + nbg),
        out_specs=[hspec(), hspec(), vspec(), hspec(), hspec(), hspec()],
        scratch_shapes=scratch,
        compiler_params=pltpu.CompilerParams(collective_id=cid, has_side_effects=True, vmem_limit_bytes=62 << 20),
        name="mlp",
    )(h, x, teach, *gates, *ups, *downs, *bg)


def norm_back(tot, x, prior, gain, wide):
    xh, inv = row_stats(x, wide)
    e = tot * gain
    m1 = jnp.sum(e, axis=1, keepdims=True) * (1.0 / wide)
    m2 = jnp.sum(e * xh, axis=1, keepdims=True) * (1.0 / wide)
    return prior + inv * (e - m1 - xh * m2), tot * xh


def fold(ref, at, value):
    ref[at] += value[:8] + value[8:]


def mid_back_kernel(n, f, npieces, ahead, slots, *refs):
    refs = list(refs)
    take = lambda count: [refs.pop(0) for _ in range(count)]
    dg_hbm, du_hbm, res_hbm, x2_hbm, x1_hbm, part_hbm, vecs, cq_ref, ckv_ref, c_ref, lse_ref, wc_hbm, wq_hbm = take(13)
    w_hbm = take(8)
    dco_out, dcq_ref, dckv_ref, g1_out, do_out, sums_ref = take(6)
    piece_out = take(2)
    ybuf, wbuf, g, low, xs, wc, wq, dkv, dc, lsem, wsem, xsem, osem = take(13)
    send_a, recv_a, acc, p1, p2, p2b = take(6)
    sems = take(16)
    bufs, rsems = take(6), take(8)
    at = Place(n)
    wide = g.shape[1]
    ffl = dg_hbm.shape[1]
    first = RowReduce(at, send_a, recv_a, acc, p1, p2, sems[:8])
    second = RowReduce(at, send_a, recv_a, acc, p1, p2b, sems[8:])
    made = [
        (part_hbm.at[:, k * f:(k + 1) * f], piece_out[k // 4].at[:, k % 4 * f:(k % 4 + 1) * f], False) for k in range(npieces)
    ]
    scatter = ColScatter(at, made, ahead, slots, bufs, rsems)
    loads = [
        pltpu.make_async_copy(dg_hbm, ybuf.at[:, :ffl], lsem.at[0]),
        pltpu.make_async_copy(du_hbm, ybuf.at[:, ffl:], lsem.at[1]),
    ] + [pltpu.make_async_copy(w_hbm[k], wbuf.at[:, k * f:(k + 1) * f], wsem.at[k]) for k in range(8)]
    rest = [
        pltpu.make_async_copy(src, dst, lsem.at[2 + k])
        for k, (src, dst) in enumerate(((res_hbm, g), (wc_hbm, wc), (wq_hbm, wq)))
    ]
    for cp in loads + rest:
        cp.start()

    def stream(src, i):
        slot = lax.rem(i, 2)
        return pltpu.make_async_copy(src.at[rows_of(i)], xs.at[slot], xsem.at[slot])

    stream(x2_hbm, 0).start()
    stream(x2_hbm, 1).start()
    at.enter(True)
    scatter.begin()
    for cp in loads:
        cp.wait()

    def project(i):
        first.partial(i, ybuf[rows_of(i)], wbuf)
        pl.when(i > 0)(lambda: first.swap(i - 1))

    each(0, NCH, project)
    first.swap(NCH - 1)
    for cp in rest:
        cp.wait()
    sums_ref[...] = jnp.zeros_like(sums_ref)
    dkv[...] = jnp.zeros_like(dkv)

    def hook(slot):
        for k in range(npieces):
            pl.when(slot == k * 2 * NCH // npieces + 1)(lambda: scatter.advance(k))

    def outs(i, which):
        lowest = (dco_out, do_out)[which]
        cps = [pltpu.make_async_copy(low.at[rows_of(i)], lowest.at[rows_of(i)], osem.at[which, i])]
        if which == 1:
            cps.append(pltpu.make_async_copy(g.at[rows_of(i)], g1_out.at[rows_of(i)], osem.at[2, i]))
        return cps

    def cross(i):
        first.ready(i)
        stream(x2_hbm, i).wait()
        slot = lax.rem(i, 2)

        def block(k, rs, ls):
            tot = first.total(rs)
            new, dx = norm_back(tot, xs[slot, ls], g[rs], vecs[4:5], wide)
            g[rs] = new
            low[rs] = new.astype(BF)
            fold(sums_ref, 0, dx)
            fold(sums_ref, 1, tot)

        sub_blocks(i, block)
        pl.when(i < NCH - 2)(lambda: stream(x2_hbm, i + 2).start())

        @pl.when(i >= NCH - 2)
        def _():
            pltpu.make_async_copy(x1_hbm.at[rows_of(i + 2 - NCH)], xs.at[slot], xsem.at[slot]).start()

        for cp in outs(i, 0):
            cp.start()
        rows = rows_of(i)
        dc[...] = nn(low[rows], wc[...]).astype(BF)
        lse_t = lse_ref[rows].T
        delta = jnp.zeros((CH, 128), F32)
        for pair in range(f // 128):
            cols = slice(128 * pair, 128 * (pair + 1))
            prod = dc[:, cols].astype(F32) * c_ref[rows, cols].astype(F32)
            for which in range(2):
                one = jnp.sum(head_mask(prod, which), axis=1, keepdims=True)
                delta = jnp.where(lanes(delta.shape) == 2 * pair + which, one, delta)
        delta_t = delta.T
        valid = lax.broadcasted_iota(jnp.int32, (CP, 1), 0) < CLEN
        for pair in range(f // 128):
            cols = slice(128 * pair, 128 * (pair + 1))
            vcols = slice(f + 128 * pair, f + 128 * (pair + 1))
            kb, vb, qc, doc = ckv_ref[:, cols], ckv_ref[:, vcols], cq_ref[rows, cols], dc[:, cols]
            dks, dvs, dqt = [], [], None
            for which in range(2):
                h = 2 * pair + which
                km = head_mask(kb, which)
                p = jnp.where(valid, jnp.exp(nt(km, qc) - lse_t[h:h + 1]), 0.0)
                dp = nt(head_mask(vb, which), doc)
                ds = (p * (dp - delta_t[h:h + 1])).astype(BF)
                dvs.append(nn(p.astype(BF), doc))
                dks.append(nn(ds, qc))
                part = nn(km.T, ds)
                dqt = part if dqt is None else dqt + part
            left = lanes(dks[0].shape) < HEAD
            dkv[:, cols] += jnp.where(left, dks[0], dks[1])
            dkv[:, vcols] += jnp.where(left, dvs[0], dvs[1])
            dcq_ref[rows, cols] = (dqt.T * HEAD ** (-0.5)).astype(BF)
        first.drain(i)
        second.partial(i, dcq_ref[rows], wq)
        pl.when(i > 0)(lambda: second.swap(i - 1))

    def step(i):
        first.share(i)
        pl.when(i > 0)(lambda: cross(i - 1))
        hook(i)

    each(0, NCH, step)
    cross(NCH - 1)
    second.swap(NCH - 1)
    dckv_ref[...] = dkv[...].astype(BF)

    def last(i):
        second.ready(i)
        slot = lax.rem(i + NCH, 2)
        cp = pltpu.make_async_copy(x1_hbm.at[rows_of(i)], xs.at[slot], xsem.at[slot])
        cp.wait()
        for cp in outs(i, 0):
            cp.wait()

        def block(k, rs, ls):
            tot = second.total(rs)
            new, dx = norm_back(tot, xs[slot, ls], g[rs], vecs[2:3], wide)
            g[rs] = new
            low[rs] = new.astype(BF)
            fold(sums_ref, 2, dx)
            fold(sums_ref, 3, tot)

        sub_blocks(i, block)

        @pl.when(i < NCH - 2)
        def _():
            pltpu.make_async_copy(x1_hbm.at[rows_of(i + 2)], xs.at[slot], xsem.at[slot]).start()

        for cp in outs(i, 1):
            cp.start()

    def step_two(i):
        second.share(i)
        pl.when(i > 0)(lambda: last(i - 1))
        hook(NCH + i)

    each(0, NCH, step_two)
    last(NCH - 1)
    scatter.complete()

    def end(i):
        second.drain(i)
        for cp in outs(i, 1):
            cp.wait()

    each(0, NCH, end)


def mid_back_call(cid, n, dg, du, res, x2, x1, part, vecs, cq, ckv, c, lse, wc, wq, ws, npieces=5, ahead=3, slots=5):
    wide, f, ffl = res.shape[1], cq.shape[1], dg.shape[1]
    size = wide // n
    sd = jax.ShapeDtypeStruct
    dma = pltpu.SemaphoreType.DMA
    bufs, sems = scatter_scratch(npieces, slots, n, f, wide)
    return pl.pallas_call(
        functools.partial(mid_back_kernel, n, f, npieces, ahead, slots),
        out_shape=[
            sd((TP, wide), BF), sd((TP, f), BF), sd((CP, 2 * f), BF), sd((TP, wide), F32), sd((TP, wide), BF), sd((4, 8, wide), F32),
            sd((size, ffl), F32), sd((size, (npieces - 4) * f), F32),
        ],
        in_specs=[hspec()] * 6 + [vspec()] * 5 + [hspec()] * 10,
        out_specs=[hspec(), vspec(), vspec(), hspec(), hspec(), vspec()] + [hspec()] * 2,
        scratch_shapes=[
            pltpu.VMEM((TP, 2 * ffl), BF), pltpu.VMEM((wide, 2 * ffl), BF), pltpu.VMEM((TP, wide), F32), pltpu.VMEM((TP, wide), BF),
            pltpu.VMEM((2, CH, wide), F32), pltpu.VMEM((wide, f), BF), pltpu.VMEM((wide, f), BF), pltpu.VMEM((CP, 2 * f), F32),
            pltpu.VMEM((CH, f), BF), dma((5,)), dma((8,)), dma((2,)), dma((3, NCH)),
        ] + reduce_scratch(wide, True) + bufs + sems,
        compiler_params=pltpu.CompilerParams(collective_id=cid, has_side_effects=True, vmem_limit_bytes=63 << 20),
        name="mid_back",
    )(dg, du, res, x2, x1, part, vecs, cq, ckv, c, lse, wc, wq, *ws)


def end_kernel(n, f, low, ahead, slots, *refs):
    refs = list(refs)
    take = lambda count: [refs.pop(0) for _ in range(count)]
    do_hbm, h1_hbm, h2_hbm, dco_hbm, x0_hbm, g1_hbm, part_hbm, vecs_hbm, sums_hbm = take(9)
    wo_hbm, wck_hbm, wcv_hbm = take(3)
    w1_hbm = take(3)
    qkv_ref, a_ref, lse_ref, cos_ref, lo_ref, hi_ref, c_ref, dcq_ref, dckv_ref, cond_ref, sq_ref = take(11)
    lat_ref, gcond_ref, vec_ref = take(3)
    up_out, down_out = take(2)
    square_out = take(8)
    (xa, xb, wt, w1, da, dqkv, lse_t, delta_t, dqt, gbuf, x0, xo, go, g1, tot, send_a, recv_a, acc, send_b, recv_b) = take(20)
    st, back, st_t, sx, cpart, crecv, vb, vr, vz, sums_own = take(10)
    lsem, wsem, s_a, r_a, s_b, r_b, s_x, r_x, s_c, r_c, s_v, r_v = take(12)
    bufs, rsems = take(6), take(8)
    at = Place(n)
    r, c, o = at.r, at.c, at.o
    wide = xa.shape[1]
    own = pl.ds(pl.multiple_of(r * f, 128), f)
    made = [(part_hbm.at[:, k * f:(k + 1) * f], up_out.at[:, (k - low) * f:(k - low + 1) * f], False) for k in range(low, 8)]
    made += [(part_hbm.at[:, k * f:(k + 1) * f], down_out.at[(k - 8) * f:(k - 7) * f], True) for k in range(8, 12)]
    flips = (True, True, False, False, False, False, False, False)
    made += [(gbuf.at[k], square_out[k], flips[k]) for k in range(8)]
    scatter = ColScatter(at, made, ahead, slots, bufs, rsems)
    load = lambda src, dst, k: pltpu.make_async_copy(src, dst, lsem.at[k])
    do_cp, h2_cp, wo_cp = load(do_hbm, xa, 0), load(h2_hbm, xb, 1), load(wo_hbm, wt, 2)
    others = [
        load(x0_hbm, x0, 3), load(x0_hbm.at[:, own], xo, 4), load(vecs_hbm.at[:, own], go, 5), load(g1_hbm.at[:, own], g1, 6),
        load(sums_hbm.at[:, :, own], sums_own, 7),
    ] + [pltpu.make_async_copy(w1_hbm[k], w1.at[:, k * f:(k + 1) * f], wsem.at[k]) for k in range(3)]
    for cp in [do_cp, wo_cp, h2_cp] + others:
        cp.start()
    at.enter(True, diagonal=True)
    scatter.begin()

    def weight_grad(slot, left, right):
        def one(j):
            cols = pl.ds(pl.multiple_of(j * 512, 128), 512)
            gbuf[slot, cols] = tn(left[:, cols], right).astype(BF)

        each(0, wide // 512, one)

    do_cp.wait()
    wo_cp.wait()
    each(0, NCH, lambda i: da.__setitem__(rows_of(i), nn(xa[rows_of(i)], wt[...]).astype(BF)))
    weight_grad(0, xa, a_ref[...])
    dco_cp, wck_cp = load(dco_hbm, xa, 0), load(wck_hbm, wt, 2)
    dco_cp.start()
    wck_cp.start()

    def emit_q(pair, dq):
        dqkv[:, 128 * pair:128 * (pair + 1)] = rotate_lanes(dq * HEAD ** (-0.5), cos_ref[...], -lo_ref[...], -hi_ref[...]).astype(BF)

    def emit_kv(pair, rows, dk, dv):
        dqkv[rows, f + 128 * pair:f + 128 * (pair + 1)] = rotate_lanes(dk, cos_ref[rows], -lo_ref[rows], -hi_ref[rows]).astype(BF)
        dqkv[rows, 2 * f + 128 * pair:2 * f + 128 * (pair + 1)] = dv.astype(BF)

    def hook(pair, j):
        pl.when(j == 4)(lambda: scatter.advance(pair))

    attend_back(qkv_ref, 0, qkv_ref, f, qkv_ref, 2 * f, TP, CH, LEN, da, a_ref, lse_ref, lse_t, delta_t, dqt, emit_q, emit_kv, f // HEAD, hook)
    step = f // 128

    dco_cp.wait()
    h2_cp.wait()
    weight_grad(1, xa, c_ref[...])
    weight_grad(2, xb, dcq_ref[...])
    h1_cp = load(h1_hbm, xb, 1)
    h1_cp.start()
    wck_cp.wait()
    dck, dcv = dckv_ref[:, :f], dckv_ref[:, f:]
    for j in range(4):
        cpart[j] = nt(dck, wt[j * f:(j + 1) * f])
    wcv_cp = load(wcv_hbm, wt, 2)
    wcv_cp.start()
    weight_grad(3, cond_ref, dck)
    weight_grad(4, cond_ref, dcv)
    scatter.advance(step)
    wcv_cp.wait()
    for j in range(4):
        crecv[j] = (cpart[j] + nt(dcv, wt[j * f:(j + 1) * f])).astype(BF)
    peers = (at.sib, at.par, at.diag)
    cond_cps = [
        remote(crecv.at[peers[k][0]], crecv.at[4 + k], s_c.at[k], r_c.at[k], peers[k]) for k in range(3)
    ]
    for cp in cond_cps:
        cp.start()
    h1_cp.wait()
    for k in range(3):
        weight_grad(5 + k, xb, dqkv[:, k * f:(k + 1) * f])
    for cp in others:
        cp.wait()
    scatter.advance(step + 1)

    wblock = lambda j: w1[pl.ds(pl.multiple_of(j * f, 128), f)]

    def copy_a(i):
        return remote(send_a.at[rows_of(i)], recv_a.at[rows_of(i)], s_a.at[i], r_a.at[i], at.sib)

    def copy_b(i):
        return remote(send_b.at[rows_of(i)], recv_b.at[rows_of(i)], s_b.at[i], r_b.at[i], at.par)

    def swap(i):
        copy_a(i).wait_recv()
        both = acc[lax.rem(i, 2)] + recv_a[rows_of(i)].astype(F32)
        left, right = both[:, :f], both[:, f:]
        tot[rows_of(i)] = jnp.where(at.xi == 0, left, right)
        send_b[rows_of(i)] = jnp.where(at.xi == 0, right, left).astype(BF)
        copy_b(i).start()

    def project(i):
        y = dqkv[rows_of(i)]
        send_a[rows_of(i), :f] = nt(y, wblock(o)).astype(BF)
        send_a[rows_of(i), f:] = nt(y, wblock(2 + o)).astype(BF)
        copy_a(i).start()
        acc[lax.rem(i, 2), :, :f] = nt(y, wblock(c))
        acc[lax.rem(i, 2), :, f:] = nt(y, wblock(2 + c))
        pl.when(i > 0)(lambda: swap(i - 1))

    each(0, NCH, project)
    swap(NCH - 1)
    vr[...] = jnp.zeros_like(vr)

    def sums_of(i):
        copy_b(i).wait_recv()

        def block(k, rs, ls):
            x = x0[rs].astype(F32)
            mean = jnp.sum(x, axis=1, keepdims=True) * (1.0 / wide)
            xc = x - mean
            inv = lax.rsqrt(jnp.sum(xc * xc, axis=1, keepdims=True) * (1.0 / wide) + EPSILON)
            t = tot[rs] + recv_b[rs].astype(F32)
            tot[rs] = t
            xh = (xo[rs].astype(F32) - mean) * inv
            e = t * go[0:1]
            dx = t * xh
            lane = lanes((SUB, 128))
            first = jnp.sum(e, axis=1, keepdims=True)
            cross = jnp.sum(e * xh, axis=1, keepdims=True)
            st[rs] = jnp.where(lane == 0, first, jnp.where(lane == 1, cross, jnp.where(lane == 2, mean, inv)))
            fold(vr, 0, dx)
            fold(vr, 1, t)

        sub_blocks(i, block)

    each(0, NCH, sums_of)
    st_t[...] = st[...].T
    sx[0] = st_t[:8]
    stat_cps = [remote(sx.at[0], sx.at[1 + k], s_x.at[k], r_x.at[k], peers[k]) for k in range(3)]
    for cp in stat_cps:
        cp.start()
    total = lambda x: jnp.sum(x, axis=0, keepdims=True)
    error = jnp.sum(total(sq_ref[...]), axis=1, keepdims=True)
    vb[0:1] = total(vr[0])
    vb[1:2] = total(vr[1])
    vb[2:3] = total(sums_own[2])
    vb[3:4] = total(sums_own[3])
    vb[4:5] = total(sums_own[0])
    vb[5:6] = total(sums_own[1])
    vb[6:8] = jnp.broadcast_to(error, (2, f))
    pair_cp = remote(vb, vz.at[at.outer], s_v.at[at.outer], r_v.at[at.outer], at.ypar)
    pair_cp.start()
    scatter.advance(step + 2)
    for cp in cond_cps:
        cp.wait_recv()
    gcond_ref[...] = (
        crecv[r].astype(F32) + crecv[4].astype(F32) + crecv[5].astype(F32) + crecv[6].astype(F32)
    ).astype(BF)
    for cp in stat_cps:
        cp.wait_recv()
    st_t[:8] = sx[0] + sx[1] + sx[2] + sx[3]
    pair_cp.wait()
    vz[at.zo] = vb[...] + vz[at.outer]

    def vec_out(step):
        return remote(vz.at[at.zo], vz.at[at.zo], s_v.at[step], r_v.at[at.zo], (r, 2 * at.zpeer(step) + at.yi))

    each(1, at.outer, lambda step: vec_out(step).start())
    back[...] = st_t[...].T

    def last(i):
        def block(k, rs, ls):
            e = tot[rs] * go[0:1]
            sums, own_stats = back[rs], st[rs]
            first, cross = sums[:, 0:1] * (1.0 / wide), sums[:, 1:2] * (1.0 / wide)
            mean, inv = own_stats[:, 2:3], own_stats[:, 3:4]
            xh = (xo[rs].astype(F32) - mean) * inv
            lat_ref[rs] = (g1[rs] + inv * (e - first - xh * cross)).astype(BF)

        sub_blocks(i, block)

    each(0, NCH, last)
    for p in range(step + 3, len(made)):
        scatter.advance(p)

    def vec_in(step):
        zs = at.zpeer(at.outer - step)
        remote(vz.at[zs], vz.at[zs], s_v.at[step], r_v.at[zs], at.ypar).wait_recv()
        vb[...] += vz[zs]

    vb[...] = vz[at.zo]
    each(1, at.outer, vec_in)
    vec_ref[...] = vb[...]
    each(1, at.outer, lambda step: vec_out(step).wait_send())
    scatter.complete()
    for cp in stat_cps + cond_cps:
        cp.wait_send()

    def drain(i):
        copy_a(i).wait_send()
        copy_b(i).wait_send()

    each(0, NCH, drain)


def end_call(cid, n, do, h1, h2, dco, x0, g1, part, vecs, sums, wo, wck, wcv, w1, qkv, a, lse, tables, c, dcq, dckv, cond, sq, low=5, ahead=3, slots=5):
    wide, f = do.shape[1], a.shape[1]
    size, outer = wide // n, n // 2
    sd = jax.ShapeDtypeStruct
    dma = pltpu.SemaphoreType.DMA
    pieces = 12 - low + 8
    bufs, sems = scatter_scratch(pieces, slots, n, f, wide)
    square = lambda flip: sd((f, size) if flip else (size, f), F32)
    return pl.pallas_call(
        functools.partial(end_kernel, n, f, low, ahead, slots),
        out_shape=[sd((TP, f), BF), sd((CP, f), BF), sd((8, f), F32), sd((size, (8 - low) * f), F32), sd((4 * f, size), F32)]
        + [square(k < 2) for k in range(8)],
        in_specs=[hspec()] * 15 + [vspec()] * 11,
        out_specs=[vspec()] * 3 + [hspec()] * 10,
        scratch_shapes=[
            pltpu.VMEM((TP, wide), BF), pltpu.VMEM((TP, wide), BF), pltpu.VMEM((wide, f), BF), pltpu.VMEM((wide, 3 * f), BF),
            pltpu.VMEM((TP, f), BF), pltpu.VMEM((TP, 3 * f), BF), pltpu.VMEM((128, TP), F32), pltpu.VMEM((128, TP), F32),
            pltpu.VMEM((128, TP), F32), pltpu.VMEM((8, wide, f), BF), pltpu.VMEM((TP, wide), BF), pltpu.VMEM((TP, f), BF),
            pltpu.VMEM((8, f), F32), pltpu.VMEM((TP, f), F32), pltpu.VMEM((TP, f), F32), pltpu.VMEM((TP, 2 * f), BF),
            pltpu.VMEM((TP, 2 * f), BF), pltpu.VMEM((2, CH, 2 * f), F32), pltpu.VMEM((TP, f), BF), pltpu.VMEM((TP, f), BF),
            pltpu.VMEM((TP, 128), F32), pltpu.VMEM((TP, 128), F32), pltpu.VMEM((128, TP), F32), pltpu.VMEM((4, 8, TP), F32),
            pltpu.VMEM((4, CP, f), F32), pltpu.VMEM((7, CP, f), BF), pltpu.VMEM((8, f), F32), pltpu.VMEM((2, 8, f), F32),
            pltpu.VMEM((outer + 1, 8, f), F32), pltpu.VMEM((4, 8, f), F32),
            dma((8,)), dma((3,)), dma((NCH,)), dma((NCH,)), dma((NCH,)), dma((NCH,)), dma((3,)), dma((3,)), dma((3,)), dma((3,)),
            dma((outer + 1,)), dma((outer + 1,)),
        ] + bufs + sems,
        compiler_params=pltpu.CompilerParams(collective_id=cid, has_side_effects=True, vmem_limit_bytes=63 << 20),
        name="end",
    )(do, h1, h2, dco, x0, g1, part, vecs, sums, wo, wck, wcv, *w1, qkv, a, lse, *tables, c, dcq, dckv, cond, sq)


def rotary_lanes():
    half_size = ROT // 2
    position = jnp.arange(TP, dtype=F32)
    frequency = jnp.exp(jnp.arange(half_size, dtype=F32) * (-2.0 * math.log(10000.0) / ROT))
    angles = position[:, None] * frequency[None, :]
    cos, sin = jnp.cos(angles), jnp.sin(angles)
    one, zero = jnp.ones((TP, HEAD - ROT), F32), jnp.zeros((TP, half_size), F32)
    rest = jnp.zeros((TP, HEAD - ROT), F32)
    tile = lambda *xs: jnp.concatenate(xs + xs, axis=1)
    return tile(cos, cos, one), tile(-sin, zero, rest), tile(zero, sin, rest)


def pad_rows(block, rows):
    return jnp.pad(block, ((0, rows - block.shape[0]), (0, 0)))


def body(
    latents,
    conditioning,
    teacher,
    gain_attn,
    bias_attn,
    gain_cross,
    bias_cross,
    gain_mlp,
    bias_mlp,
    w_query,
    w_key,
    w_value,
    w_out,
    w_cross_query,
    w_cross_key,
    w_cross_value,
    w_cross_out,
    w_gate,
    w_up,
    w_down,
):

    F = latents.shape[1]
    wide = F * lax.axis_size("row")
    n = lax.axis_size("col")
    FFL = w_gate.shape[1]
    small = jnp.stack([gain_attn, bias_attn, gain_cross, bias_cross, gain_mlp, bias_mlp])
    pieces = lambda w: [w[:, k:k + F] for k in range(0, FFL, F)]
    gates, ups, downs = pieces(w_gate), pieces(w_up), pieces(w_down.T)
    tables = rotary_lanes()
    early = [w_query, w_key, w_value, w_out.T, w_cross_query, w_cross_key, w_cross_value, w_cross_out.T, gates[0], ups[0]]
    late = [gates[1], ups[1], gates[2], ups[2], gates[3], ups[3]] + downs
    (x0, h1, qkv, a, lse1, vecs, teacher_full, cond_full, wq, wk, wv, wo, wcq, wck, wcv, wco, *gu0) = front_call(
        0, n, pad_rows(latents, TP), pad_rows(teacher, TP), pad_rows(conditioning, CP), pad_rows(small, 8), tables, early
    )
    x1, h2, cq, ckv, c, lse2, x2, h3, *gu1 = mid_call(1, n, a, x0, vecs, cond_full, wo, wcq, wck, wcv, wco, late[:8])
    gu = gu0 + gu1
    full_gate, full_up = [gu[0], gu[2], gu[4], gu[6]], [gu[1], gu[3], gu[5], gu[7]]
    res, y_low, squares, dgate, dup, part_mlp = mlp_call(2, n, h3, x2, teacher_full, full_gate, full_up, gu[8:], late[8:])
    dco, dcq, dckv, g1, do, sums, grad_gate, grad_up_a = mid_back_call(
        3, n, dgate, dup, res, x2, x1, part_mlp, vecs, cq, ckv, c, lse2, wco, wcq, full_gate + full_up
    )
    (glat, gcond, vec, grad_up_b, grad_down, go, gco, gcq, gck, gcv, gq, gk, gv) = end_call(
        4, n, do, h1, h2, dco, x0, g1, part_mlp, vecs, sums, wo, wck, wcv, [wq, wk, wv], qkv, a, lse1, tables, c, dcq, dckv,
        cond_full, squares,
    )
    outputs = lax.dynamic_slice_in_dim(y_low, lax.axis_index("row") * F, F, axis=1)[:LEN]
    loss = vec[6, 0] / (LEN * wide * n)
    width = F // n
    vectors = lax.dynamic_slice_in_dim(vec, lax.axis_index("col") * width, width, axis=1)
    return (
        outputs, loss, glat[:LEN], gcond[:CLEN], gq, gk, gv, go, gcq, gck, gcv, gco,
        grad_gate, jnp.concatenate([grad_up_a, grad_up_b], axis=1), grad_down,
        vectors[0], vectors[1], vectors[2], vectors[3], vectors[4], vectors[5],
    )


def solution(mesh):
    in_specs = (
        P("col", "row"),
        P("col", "row"),
        P("col", "row"),
        P("row"),
        P("row"),
        P("row"),
        P("row"),
        P("row"),
        P("row"),
        P("col", "row"),
        P("col", "row"),
        P("col", "row"),
        P("row", "col"),
        P("col", "row"),
        P("col", "row"),
        P("col", "row"),
        P("row", "col"),
        P("col", "row"),
        P("col", "row"),
        P("row", "col"),
    )
    out_specs = (
        P("col", "row"),
        P(),
        P("col", "row"),
        P("col", "row"),
        P("col", "row"),
        P("col", "row"),
        P("col", "row"),
        P("row", "col"),
        P("col", "row"),
        P("col", "row"),
        P("col", "row"),
        P("row", "col"),
        P("col", "row"),
        P("col", "row"),
        P("row", "col"),
        P(("row", "col")),
        P(("row", "col")),
        P(("row", "col")),
        P(("row", "col")),
        P(("row", "col")),
        P(("row", "col")),
    )
    return jax.shard_map(body, mesh=mesh, in_specs=in_specs, out_specs=out_specs, check_vma=False)
```

```python
import functools
import math

import jax
import jax.numpy as jnp
import numpy as np
from jax import lax
from jax.sharding import PartitionSpec as P
from jax.experimental import pallas as pl
from jax.experimental.pallas import tpu as pltpu

BF, F32 = jnp.bfloat16, jnp.float32
MESH = pl.DeviceIdType.MESH
TP = 1040
LEN = 1025
CLEN = 130
CP = 144
HEAD = 64
ROT = 32
EPSILON = 1e-06
CH = 208
NCH = TP // CH
SUB = 16


def nt(a, b):
    return lax.dot_general(a, b, (((1,), (1,)), ((), ())), preferred_element_type=F32)


def remote(src, dst, ssem, rsem, dev):
    return pltpu.make_async_remote_copy(src_ref=src, dst_ref=dst, send_sem=ssem, recv_sem=rsem, device_id=dev, device_id_type=MESH)


def tn(left, right):
    return lax.dot_general(left, right, (((0,), (0,)), ((), ())), preferred_element_type=F32)


def row_stats(x, wide):
    xc = x - jnp.sum(x, axis=1, keepdims=True) * (1.0 / wide)
    inv = lax.rsqrt(jnp.sum(xc * xc, axis=1, keepdims=True) * (1.0 / wide) + EPSILON)
    return xc * inv, inv


def rotate_lanes(u, cos, sin_low, sin_high):
    width = u.shape[-1]
    return u * cos + pltpu.roll(u, width - ROT // 2, u.ndim - 1) * sin_low + pltpu.roll(u, ROT // 2, u.ndim - 1) * sin_high


def vspec():
    return pl.BlockSpec(memory_space=pltpu.VMEM)


def hspec():
    return pl.BlockSpec(memory_space=pl.ANY)


class Place:
    def __init__(self, n):
        self.n, self.outer = n, n // 2
        self.r, self.col = lax.axis_index("row"), lax.axis_index("col")
        self.c = lax.rem(self.r, 2)
        self.o = 1 - self.c
        self.xi = lax.div(self.r, 2)
        self.sib = (self.r + 1 - 2 * self.c, self.col)
        self.par = (self.r + 2 - 4 * self.xi, self.col)
        self.diag = (self.par[0] + 1 - 2 * self.c, self.col)
        self.zo, self.yi = lax.div(self.col, 2), lax.rem(self.col, 2)
        self.ypar = (self.r, self.col + 1 - 2 * self.yi)

    def zpeer(self, step):
        return lax.rem(self.zo + step, self.outer)

    def near(self, z):
        gap = z - self.zo
        return jnp.logical_and(gap < 3, gap > -3)

    def enter(self, with_cols, diagonal=False):
        barrier = pltpu.get_barrier_semaphore()
        pl.semaphore_signal(barrier, inc=1, device_id=self.sib, device_id_type=MESH)
        pl.semaphore_signal(barrier, inc=1, device_id=self.par, device_id_type=MESH)
        count = 2
        if diagonal:
            pl.semaphore_signal(barrier, inc=1, device_id=self.diag, device_id_type=MESH)
            count += 1
        if with_cols:
            pl.semaphore_signal(barrier, inc=1, device_id=self.ypar, device_id_type=MESH)

            def greet(step, carry):
                pl.semaphore_signal(barrier, inc=1, device_id=(self.r, 2 * self.zpeer(step) + self.yi), device_id_type=MESH)
                return carry

            lax.fori_loop(1, self.outer, greet, 0)
            count += self.outer
        pl.semaphore_wait(barrier, count)


class ColGather:
    def __init__(self, place, pieces, ahead, ssem, rsem, lsem):
        self.at, self.pieces, self.ahead, self.ssem, self.rsem, self.lsem = place, pieces, ahead, ssem, rsem, lsem
        self.line = place.outer == 4

    def rows(self, p, j):
        size = self.pieces[p][0].shape[0]
        return self.pieces[p][1].at[pl.ds(pl.multiple_of(j * size, 16), size)]

    def local(self, p):
        return pltpu.make_async_copy(self.pieces[p][0], self.rows(p, self.at.col), self.lsem.at[p])

    def send(self, p, slot, j, to, own=False):
        src = self.pieces[p][0] if own else self.rows(p, j)
        return remote(src, self.rows(p, j), self.ssem.at[p, slot], self.rsem.at[p, j], to)

    def across(self, p):
        return self.send(p, 0, self.at.col, self.at.ypar, own=True)

    def outward(self, p, step):
        at = self.at
        return self.send(p, step, at.col, (at.r, 2 * at.zpeer(step) + at.yi), own=True)

    def onward(self, p, step):
        at = self.at
        return self.send(p, at.outer - 1 + step, 2 * at.zpeer(at.outer - step) + at.yi, at.ypar)

    def steps(self, fn, source, far=False):
        at = self.at
        if far and not self.line:
            return

        def one(step):
            if not self.line:
                fn(step)
                return
            near = at.near(at.zpeer(at.outer - step) if source else at.zpeer(step))
            pl.when(jnp.logical_not(near) if far else near)(lambda: fn(step))

        each(1, at.outer, one)

    def relay(self, p, act):
        if not self.line:
            return
        at = self.at
        for mine, source, end in ((2, 0, 3), (1, 3, 0)):
            pl.when(at.zo == mine)(lambda: act(self.send(p, at.n - 1, 2 * source + at.yi, (at.r, 2 * end + at.yi))))

    def start(self, p):
        if p < len(self.pieces):
            self.local(p).start()
            self.across(p).start()
            self.steps(lambda step: self.outward(p, step).start(), False)

    def pass_on(self, p, far):
        def one(step):
            cp = self.onward(p, step)
            cp.wait_recv()
            cp.start()

        self.steps(one, True, far)

    def begin(self):
        for p in range(self.ahead):
            self.start(p)

    def advance(self, p, flush=True):
        self.pass_on(p, False)
        self.relay(p, lambda cp: cp.start())
        self.start(p + self.ahead)
        if flush and p > 0:
            self.pass_on(p - 1, True)
        if p == len(self.pieces) - 1:
            self.pass_on(p, True)

    def finish(self, p):
        at = self.at
        self.local(p).wait()
        self.across(p).wait_send()
        self.steps(lambda step: self.outward(p, step).wait_send(), False)
        each(0, at.outer, lambda z: self.send(p, 0, 2 * z + 1 - at.yi, at.ypar).wait_recv())
        self.steps(lambda step: self.onward(p, step).wait_send(), True)
        self.steps(lambda step: self.onward(p, step).wait_send(), True, far=True)
        self.relay(p, lambda cp: cp.wait_send())


def gather_sems(pieces, n):
    return [pltpu.SemaphoreType.DMA((pieces, n)), pltpu.SemaphoreType.DMA((pieces, n)), pltpu.SemaphoreType.DMA((pieces,))]


class ColScatter:
    def __init__(self, place, pieces, ahead, slots, bufs, sems):
        self.at, self.pieces, self.ahead, self.slots = place, pieces, ahead, slots
        self.ry, self.hb, self.rz, self.rl, self.ob = bufs
        self.ls, self.sy, self.ryr, self.sz, self.rzr, self.rlr, self.os, self.credit = sems
        self.line = place.outer == 4
        self.size = self.hb.shape[2]

    def rows(self, p, j):
        return self.pieces[p][0].at[pl.ds(pl.multiple_of(j * self.size, 16), self.size)]

    def across(self, p, z):
        at = self.at
        return remote(
            self.rows(p, 2 * z + 1 - at.yi), self.ry.at[p % self.slots, z], self.sy.at[p, z], self.ryr.at[p, z], at.ypar
        )

    def own(self, p, z):
        return pltpu.make_async_copy(self.rows(p, 2 * z + self.at.yi), self.hb.at[p % self.slots, z], self.ls.at[p, z])

    def outward(self, p, z):
        at, s = self.at, p % self.slots
        return remote(self.hb.at[s, z], self.rz.at[s, at.zo], self.sz.at[p, z], self.rzr.at[p, at.zo], (at.r, 2 * z + at.yi))

    def detour(self, p, z):
        at, s = self.at, p % self.slots
        via = lax.div(at.zo, 3) + 1
        return remote(self.hb.at[s, z], self.rl.at[s], self.sz.at[p, z], self.rlr.at[p], (at.r, 2 * via + at.yi))

    def merging(self, z):
        zo = self.at.zo
        return jnp.logical_or(jnp.logical_and(zo == 1, z == 3), jnp.logical_and(zo == 2, z == 0))

    def arrives(self, zs):
        return self.at.near(zs)

    def blocks(self, fn):
        each(0, self.size // 48, lambda k: fn(pl.ds(pl.multiple_of(k * 48, 16), 48)))

    def begin(self):
        for p in range(self.ahead):
            self.start(p)

    def start(self, p):
        if p >= len(self.pieces):
            return
        if p >= self.slots:
            pl.semaphore_wait(self.credit.at[p - self.slots], self.at.outer)

        def one(z):
            self.across(p, z).start()
            self.own(p, z).start()

        each(0, self.at.outer, one)

    def reduce(self, p):
        at, s = self.at, p % self.slots

        def one(step):
            z = at.zpeer(step)
            self.own(p, z).wait()
            self.across(p, z).wait_recv()

            def add(rs):
                self.hb[s, z, rs] = (self.hb[s, z, rs].astype(F32) + self.ry[s, z, rs].astype(F32)).astype(BF)

            self.blocks(add)

            @pl.when(z != at.zo)
            def _():
                if not self.line:
                    self.outward(p, z).start()
                    return
                near = at.near(z)
                pl.when(jnp.logical_not(near))(lambda: self.detour(p, z).start())
                pl.when(jnp.logical_and(near, jnp.logical_not(self.merging(z))))(lambda: self.outward(p, z).start())

        each(1, at.outer + 1, one)

    def merge(self, p):
        if not self.line:
            return
        at, s = self.at, p % self.slots
        for mine, z, origin in ((1, 3, 0), (2, 0, 3)):
            @pl.when(at.zo == mine)
            def _():
                remote(self.rl.at[s], self.rl.at[s], self.sz.at[p, z], self.rlr.at[p], at.ypar).wait_recv()

                def add(rs):
                    self.hb[s, z, rs] = (self.hb[s, z, rs].astype(F32) + self.rl[s, rs].astype(F32)).astype(BF)

                self.blocks(add)
                self.outward(p, z).start()

    def result(self, p):
        return pltpu.make_async_copy(self.ob.at[p % 2], self.pieces[p][1], self.os.at[p])

    def finish(self, p):
        at, s = self.at, p % self.slots
        if p >= 2:
            self.result(p - 2).wait()

        def first(rs):
            self.ob[p % 2, rs] = self.hb[s, at.zo, rs].astype(F32)

        self.blocks(first)

        def one(step):
            zs = at.zpeer(at.outer - step)

            def take():
                remote(self.rz.at[s, zs], self.rz.at[s, zs], self.sz.at[p, zs], self.rzr.at[p, zs], at.ypar).wait_recv()

                def add(rs):
                    self.ob[p % 2, rs] += self.rz[s, zs, rs].astype(F32)

                self.blocks(add)

            if self.line:
                pl.when(at.near(zs))(take)
            else:
                take()

        each(1, at.outer, one)
        self.result(p).start()

        def sent(z):
            self.across(p, z).wait_send()

            @pl.when(z != at.zo)
            def _():
                self.outward(p, z).wait_send()

        each(0, at.outer, sent)
        if p + self.slots < len(self.pieces):
            pl.semaphore_signal(self.credit.at[p], inc=1, device_id=at.ypar, device_id_type=MESH)
            each(
                1,
                at.outer,
                lambda step: pl.semaphore_signal(
                    self.credit.at[p], inc=1, device_id=(at.r, 2 * at.zpeer(step) + at.yi), device_id_type=MESH
                ),
            )

    def advance(self, p):
        if p < len(self.pieces):
            self.reduce(p)
        if 0 <= p - 1 < len(self.pieces):
            self.merge(p - 1)
        if 0 <= p - 2 < len(self.pieces):
            self.finish(p - 2)
        self.start(p + self.ahead)

    def complete(self):
        count = len(self.pieces)
        self.advance(count)
        self.advance(count + 1)
        for p in range(max(0, count - 2), count):
            self.result(p).wait()


def scatter_scratch(pieces, slots, n, f, rows):
    size, outer = rows // n, n // 2
    dma = pltpu.SemaphoreType.DMA
    block = lambda *lead: pltpu.VMEM(lead + (size, f), BF)
    return [
        block(slots, outer), block(slots, outer), block(slots, outer), block(slots),
        pltpu.VMEM((2, size, f), F32),
    ], [
        dma((pieces, outer)), dma((pieces, outer)), dma((pieces, outer)), dma((pieces, outer)), dma((pieces, outer)),
        dma((pieces,)), dma((pieces,)), pltpu.SemaphoreType.REGULAR((pieces,)),
    ]


class RowGather:
    def __init__(self, place, pieces, ssem, rsem, lsem):
        self.at, self.pieces, self.ssem, self.rsem, self.lsem = place, pieces, ssem, rsem, lsem

    def cols(self, p, j):
        size = self.pieces[p][0].shape[1]
        return self.pieces[p][1].at[:, pl.ds(pl.multiple_of(j * size, 128), size)]

    def copies(self, p):
        at = self.at
        src, mine = self.pieces[p][0], self.cols(p, at.r)
        theirs = self.cols(p, at.par[0])
        return (
            pltpu.make_async_copy(src, mine, self.lsem.at[p]),
            remote(src, mine, self.ssem.at[p, 0], self.rsem.at[p, 0], at.sib),
            remote(src, mine, self.ssem.at[p, 1], self.rsem.at[p, 1], at.par),
            remote(theirs, theirs, self.ssem.at[p, 2], self.rsem.at[p, 2], at.sib),
        )

    def start(self, p):
        for cp in self.copies(p)[:3]:
            cp.start()

    def forward(self, p):
        local, near, far, on = self.copies(p)
        far.wait_recv()
        on.start()

    def finish(self, p):
        local, near, far, on = self.copies(p)
        local.wait()
        near.wait_recv()
        on.wait_recv()
        near.wait_send()
        far.wait_send()
        on.wait_send()


class RowReduce:
    def __init__(self, at, send_a, recv_a, acc, p1, p2, sems, free, prior):
        self.free, self.prior = free, prior
        self.at, self.send_a, self.recv_a, self.acc, self.p1, self.p2 = at, send_a, recv_a, acc, p1, p2
        self.s_a, self.r_a, self.s_b, self.r_b, self.s_c, self.r_c, self.s_d, self.r_d = sems
        self.half = p1.shape[2]

    def copy_a(self, i):
        rows = rows_of(i)
        return remote(self.send_a.at[rows], self.recv_a.at[rows], self.s_a.at[i], self.r_a.at[i], self.at.sib)

    def copy_b(self, i):
        rows, c = rows_of(i), self.at.c
        return remote(self.p1.at[c, rows], self.p2.at[c, rows], self.s_b.at[i], self.r_b.at[i], self.at.par)

    def copy_c(self, i, side):
        rows = rows_of(i)
        return remote(self.p1.at[side, rows], self.p1.at[side, rows], self.s_c.at[i], self.r_c.at[i], self.at.sib)

    def copy_d(self, i, side):
        rows = rows_of(i)
        return remote(self.p2.at[side, rows], self.p2.at[side, rows], self.s_d.at[i], self.r_d.at[i], self.at.sib)

    def partial(self, i, terms):
        half = self.half

        def side(which):
            rows = pl.ds(pl.multiple_of(which * half, 128), half)
            return sum(nt(value, w[rows]) for value, w in terms)

        self.send_a[rows_of(i)] = side(self.at.o).astype(BF)
        self.copy_a(i).start()
        self.acc[lax.rem(i, 2)] = side(self.at.c)

    def swap(self, i):
        self.copy_a(i).wait_recv()
        self.p1[self.at.c, rows_of(i)] = (self.acc[lax.rem(i, 2)] + self.recv_a[rows_of(i)].astype(F32)).astype(BF)
        if self.prior is not None:
            pl.semaphore_wait(self.prior.free.at[i], 1)
        self.copy_b(i).start()
        self.copy_c(i, self.at.c).start()

    def share(self, i):
        self.copy_b(i).wait_recv()
        self.copy_d(i, self.at.c).start()

    def ready(self, i):
        self.copy_c(i, self.at.o).wait_recv()
        self.copy_d(i, self.at.o).wait_recv()

    def total(self, rs):
        p1, p2 = self.p1, self.p2
        return jnp.concatenate(
            [p1[0, rs].astype(F32) + p2[0, rs].astype(F32), p1[1, rs].astype(F32) + p2[1, rs].astype(F32)], axis=1
        )

    def drain(self, i):
        self.copy_a(i).wait_send()
        self.copy_b(i).wait_send()
        self.copy_c(i, self.at.c).wait_send()
        self.copy_d(i, self.at.c).wait_send()
        pl.semaphore_signal(self.free.at[i], inc=1, device_id=self.at.par, device_id_type=MESH)


def rows_of(i):
    return pl.ds(pl.multiple_of(i * CH, 16), CH)


def each(low, high, fn):
    def body(i, carry):
        fn(i)
        return carry

    lax.fori_loop(low, high, body, 0)


def sub_blocks(i, fn):
    each(0, CH // SUB, lambda k: fn(k, pl.ds(pl.multiple_of(i * CH + k * SUB, SUB), SUB), pl.ds(pl.multiple_of(k * SUB, SUB), SUB)))


NEG = -1e30


def nn(a, b):
    return jnp.dot(a, b, preferred_element_type=F32)


def lanes(shape):
    return lax.broadcasted_iota(jnp.int32, shape, len(shape) - 1)


def head_mask(value, which):
    lane = lanes(value.shape)
    keep = (lane < HEAD) if which == 0 else (lane >= HEAD)
    return jnp.where(keep, value, jnp.zeros_like(value))


def attend_step(i, q_ref, q_off, k_ref, k_off, v_ref, v_off, keys, valid, out_ref, lse_ref, heads, hook=None):
    rows = rows_of(i)
    lse = jnp.zeros((CH, 128), F32)
    for pair in range(heads // 2):
        qp = q_ref[rows, q_off + 128 * pair:q_off + 128 * (pair + 1)]
        kp = k_ref[:, k_off + 128 * pair:k_off + 128 * (pair + 1)]
        vp = v_ref[:, v_off + 128 * pair:v_off + 128 * (pair + 1)]
        mixed = []
        for which in range(2):
            s = nt(head_mask(qp, which), kp)
            s = jnp.where(lanes((1, keys)) < valid, s, NEG)
            top = jnp.max(s, axis=1, keepdims=True)
            e = jnp.exp(s - top)
            total = jnp.sum(e, axis=1, keepdims=True)
            mixed.append(nn(e.astype(BF), vp) / total)
            lse = jnp.where(lanes(lse.shape) == 2 * pair + which, top + jnp.log(total), lse)
        both = jnp.where(lanes(mixed[0].shape) < HEAD, mixed[0], mixed[1])
        out_ref[rows, 128 * pair:128 * (pair + 1)] = both.astype(BF)
        if hook is not None:
            hook(pair)
    lse_ref[rows] = lse


def attend_back(q_ref, q_off, k_ref, k_off, v_ref, v_off, keys, kblock, valid, do_ref, out_ref, lse_ref, lse_t, delta_t, dqt, emit_q, emit_kv, heads, hook=None):
    queries = q_ref.shape[0]
    lse_t[...] = lse_ref[...].T
    delta = jnp.zeros((queries, 128), F32)
    for pair in range(heads // 2):
        cols = slice(128 * pair, 128 * (pair + 1))
        prod = do_ref[:, cols].astype(F32) * out_ref[:, cols].astype(F32)
        for which in range(2):
            one = jnp.sum(head_mask(prod, which), axis=1, keepdims=True)
            delta = jnp.where(lanes(delta.shape) == 2 * pair + which, one, delta)
    delta_t[...] = delta.T
    for pair in range(heads // 2):
        qc = slice(q_off + 128 * pair, q_off + 128 * (pair + 1))
        kc = slice(k_off + 128 * pair, k_off + 128 * (pair + 1))
        vc = slice(v_off + 128 * pair, v_off + 128 * (pair + 1))
        oc = slice(128 * pair, 128 * (pair + 1))
        dqt[...] = jnp.zeros_like(dqt)

        def keys_step(j, carry):
            rows = pl.ds(pl.multiple_of(j * kblock, 16), kblock)
            kb, vb = k_ref[rows, kc], v_ref[rows, vc]
            dks, dvs = [], []
            for which in range(2):
                h = 2 * pair + which
                km = head_mask(kb, which)
                p = jnp.exp(nt(km, q_ref[:, qc]) - lse_t[h:h + 1])
                if keys != valid:
                    pos = j * kblock + lax.broadcasted_iota(jnp.int32, (kblock, 1), 0)
                    p = jnp.where(pos < valid, p, 0.0)
                dp = nt(head_mask(vb, which), do_ref[:, oc])
                ds = (p * (dp - delta_t[h:h + 1])).astype(BF)
                dvs.append(nn(p.astype(BF), do_ref[:, oc]))
                dks.append(nn(ds, q_ref[:, qc]))
                dqt[...] += nn(km.T, ds)
            low = lanes(dks[0].shape) < HEAD
            emit_kv(pair, rows, jnp.where(low, dks[0], dks[1]), jnp.where(low, dvs[0], dvs[1]))
            if hook is not None:
                hook(pair, j)
            return carry

        lax.fori_loop(0, keys // kblock, keys_step, 0)
        emit_q(pair, dqt[...].T)


def rotate_lanes(u, cos, sin_low, sin_high):
    width = u.shape[-1]
    return u * cos + pltpu.roll(u, width - ROT // 2, u.ndim - 1) * sin_low + pltpu.roll(u, ROT // 2, u.ndim - 1) * sin_high


def norm_back(tot, x, prior, gain, wide):
    xh, inv = row_stats(x, wide)
    e = tot * gain
    m1 = jnp.sum(e, axis=1, keepdims=True) * (1.0 / wide)
    m2 = jnp.sum(e * xh, axis=1, keepdims=True) * (1.0 / wide)
    return prior + inv * (e - m1 - xh * m2), tot * xh


def fold(ref, at, value):
    ref[at] += value[:8] + value[8:]


def local(src, dst, sem):
    return pltpu.make_async_copy(src, dst, sem)


def start_all(copies):
    for cp in copies:
        cp.start()


def wait_all(copies):
    for cp in copies:
        cp.wait()


def pad_into(dst, src, count):
    whole = count // 16 * 16
    dst[:whole] = src[:whole]
    left = count - whole
    rows = lax.broadcasted_iota(jnp.int32, (16, dst.shape[1]), 0)
    tile = jnp.zeros((16, dst.shape[1]), F32)
    for k in range(left):
        tile = jnp.where(rows == k, src[whole + k:whole + k + 1].astype(F32), tile)
    dst[whole:whole + 16] = tile.astype(dst.dtype)


def spread_tables(trig, cos, low, high):
    half = ROT // 2
    t = trig[...]
    lane = lanes(t.shape)
    place = lax.rem(lane, HEAD)
    first, second = place < half, jnp.logical_and(place >= half, place < ROT)
    both = lambda u: jnp.where(lane < HEAD, u, pltpu.roll(u, HEAD, 1))
    shift = lambda u: pltpu.roll(u, half, 1)
    back = lambda u: pltpu.roll(u, 128 - half, 1)
    c16, s16 = both(t), both(back(t))
    cos[...] = jnp.where(first, c16, jnp.where(second, shift(c16), 1.0))
    low[...] = jnp.where(first, -s16, 0.0)
    high[...] = jnp.where(second, shift(s16), 0.0)


def front_phase(k, gather):
    at, f, wide = k.at, k.f, k.wide
    dma = pltpu.SemaphoreType.DMA

    def run(latv, teachv, condv, latp, teachp, condp, smallv, trig, cos, low, high, x, h, qkv, a, lse, st, w, vec, ssem, lsem, sem):
        ins = [local(k.lat, latv, sem.at[0]), local(k.teach, teachv, sem.at[1]), local(k.cond, condv, sem.at[2]), local(k.trig, trig, sem.at[4])]
        start_all(ins)
        rowg = RowGather(at, [(latp, k.x0), (smallv, k.vecs), (condp, k.cond_full), (teachp, k.teach_full)], ssem, k.row_sem, lsem)
        ins[0].wait()
        pad_into(latp, latv, LEN)
        smallv[...] = jnp.zeros_like(smallv)
        for j in range(6):
            smallv[j, :] = k.small[j][...]
        at.enter(True, diagonal=True)
        rowg.start(0)
        rowg.start(1)
        gather.begin()
        wait_all(ins[1:3])
        pad_into(condp, condv, CLEN)
        pad_into(teachp, teachv, LEN)
        ins[3].wait()
        spread_tables(trig, cos, low, high)
        rowg.forward(0)
        rowg.forward(1)
        gather.advance(0)
        rowg.finish(0)
        rowg.finish(1)
        more = [local(k.x0, x, sem.at[0]), local(k.vecs, vec, sem.at[1])]
        start_all(more)
        rowg.start(2)
        rowg.start(3)
        wait_all(more)

        def norm(b):
            rows = pl.ds(pl.multiple_of(b * SUB, SUB), SUB)
            v = x[rows].astype(F32)
            mean = jnp.sum(v, axis=1, keepdims=True) * (1.0 / wide)
            xc = v - mean
            inv = lax.rsqrt(jnp.sum(xc * xc, axis=1, keepdims=True) * (1.0 / wide) + EPSILON)
            h[rows] = (xc * inv * vec[0:1] + vec[1:2]).astype(BF)
            st[rows] = jnp.where(lanes((SUB, 128)) == 2, mean, inv)

        each(0, TP // SUB, norm)
        outs = [local(h, k.h1, sem.at[2]), local(st, k.st1, sem.at[3])]
        start_all(outs)
        gather.advance(1)
        gather.advance(2)
        rowg.forward(2)
        fetch = lambda p: local(gather.pieces[p][1], w.at[p % 2], sem.at[4 + p % 2])
        gather.finish(0)
        fetch(0).start()
        for part in range(3):
            fetch(part).wait()
            if part < 2:
                if part == 1:
                    gather.pass_on(2, True)
                gather.finish(part + 1)
                fetch(part + 1).start()

            def project(i):
                rows = rows_of(i)
                c, lo, hi = cos[rows], low[rows], high[rows]
                res = nn(h[rows], w[part % 2])
                for pair in range(f // 128):
                    u = res[:, pair * 128:(pair + 1) * 128]
                    if part < 2:
                        u = rotate_lanes(u, c, lo, hi).astype(BF)
                    else:
                        u = u.astype(BF)
                    if part == 0:
                        u = u * HEAD ** (-0.5)
                    qkv[rows, part * f + pair * 128:part * f + (pair + 1) * 128] = u

            each(0, NCH, project)
        gather.advance(3, flush=False)

        def attend(i):
            def hook(pair):
                for p in range(4, k.front_pieces):
                    pl.when(i * 3 + pair == (p - 4) * 15 // (k.front_pieces - 4))(lambda: gather.advance(p))

            attend_step(i, qkv, 0, qkv, f, qkv, 2 * f, TP, LEN, a, lse, f // HEAD, hook)

        each(0, NCH, attend)
        last = [local(qkv, k.qkv, sem.at[0]), local(a, k.a, sem.at[1]), local(lse, k.lse1, sem.at[6])]
        start_all(last)
        rowg.forward(3)
        rowg.finish(2)
        rowg.finish(3)
        wait_all(outs + last)

    vm = pltpu.VMEM
    pl.run_scoped(
        run,
        latv=vm((LEN, f), BF), teachv=vm((LEN, f), BF), condv=vm((CLEN, f), BF), latp=vm((TP, f), BF), teachp=vm((TP, f), BF),
        condp=vm((CP, f), BF), smallv=vm((8, f), F32), trig=vm((TP, 128), F32), cos=vm((TP, 128), F32), low=vm((TP, 128), F32),
        high=vm((TP, 128), F32), x=vm((TP, wide), BF), h=vm((TP, wide), BF), qkv=vm((TP, 3 * f), BF), a=vm((TP, f), BF),
        lse=vm((TP, 128), F32), st=vm((TP, 128), F32), w=vm((2, wide, f), BF), vec=vm((8, wide), F32),
        ssem=dma((4, 3)), lsem=dma((4,)), sem=dma((7,)),
    )


def mid_phase(k, gather, first, second):
    at, f, wide = k.at, k.f, k.wide
    dma, vm = pltpu.SemaphoreType.DMA, pltpu.VMEM
    slots = list(range(k.front_pieces, k.mid_pieces))

    def run(a, x0, x, low, wo, wq, wk, wv, wc, cq, ckv, c, lse, cond, vec, acc, sem, osem, esem):
        first.acc, second.acc = acc, acc
        for p in range(3, 8):
            gather.finish(p)
        loads = [
            local(src, dst, sem.at[j])
            for j, (src, dst) in enumerate(
                ((k.a, a), (k.full[3], wo), (k.full[5], wk), (k.full[6], wv), (k.cond_full, cond), (k.x0, x0), (k.full[4], wq), (k.full[7], wc), (k.vecs, vec))
            )
        ]
        start_all(loads)
        wait_all(loads[:2])

        def project(i):
            first.partial(i, [(a[rows_of(i)], wo)])
            pl.when(i > 0)(lambda: first.swap(i - 1))

        each(0, NCH, project)
        first.swap(NCH - 1)
        wait_all(loads[2:])
        ckv[:, :f] = nn(cond[...], wk[...]).astype(BF)
        ckv[:, f:] = nn(cond[...], wv[...]).astype(BF)

        def outs(i, main, lowest, which):
            return [
                local(x.at[rows_of(i)], main.at[rows_of(i)], osem.at[which, 2 * i]),
                local(low.at[rows_of(i)], lowest.at[rows_of(i)], osem.at[which, 2 * i + 1]),
            ]

        def hook(slot):
            for j, p in enumerate(slots):
                pl.when(slot == j * 2 * NCH // len(slots))(lambda: gather.advance(p))

        def cross(i):
            first.ready(i)

            def block(b, rs, ls):
                v = x0[rs].astype(F32) + first.total(rs)
                x[rs] = v
                low[rs] = (row_stats(v, wide)[0] * vec[2:3] + vec[3:4]).astype(BF)

            sub_blocks(i, block)
            start_all(outs(i, k.x1, k.h2, 0))
            rows = rows_of(i)
            cq[rows] = nn(low[rows], wq[...]).astype(BF) * HEAD ** (-0.5)
            attend_step(i, cq, 0, ckv, 0, ckv, f, CP, CLEN, c, lse, f // HEAD)
            first.drain(i)
            second.partial(i, [(c[rows], wc)])
            pl.when(i > 0)(lambda: second.swap(i - 1))

        def step(i):
            first.share(i)
            pl.when(i > 0)(lambda: cross(i - 1))
            hook(i)

        each(0, NCH, step)
        cross(NCH - 1)
        second.swap(NCH - 1)
        ends = [local(cq, k.cq, esem.at[0]), local(ckv, k.ckv, esem.at[1]), local(c, k.c, esem.at[2]), local(lse, k.lse2, esem.at[3])]
        start_all(ends)

        def last(i):
            second.ready(i)
            wait_all(outs(i, k.x1, k.h2, 0))

            def block(b, rs, ls):
                v = x[rs] + second.total(rs)
                x[rs] = v
                low[rs] = (row_stats(v, wide)[0] * vec[4:5] + vec[5:6]).astype(BF)

            sub_blocks(i, block)
            start_all(outs(i, k.x2, k.h3, 1))

        def step_two(i):
            second.share(i)
            pl.when(i > 0)(lambda: last(i - 1))
            hook(NCH + i)

        each(0, NCH, step_two)
        last(NCH - 1)

        def end(i):
            second.drain(i)
            wait_all(outs(i, k.x2, k.h3, 1))

        each(0, NCH, end)
        wait_all(ends)

    weight = lambda: vm((wide, f), BF)
    pl.run_scoped(
        run,
        a=vm((TP, f), BF), x0=vm((TP, wide), BF), x=vm((TP, wide), F32), low=vm((TP, wide), BF), wo=weight(), wq=weight(), wk=weight(),
        wv=weight(), wc=weight(), cq=vm((TP, f), BF), ckv=vm((CP, 2 * f), BF), c=vm((TP, f), BF), lse=vm((TP, 128), F32),
        cond=vm((CP, wide), BF), vec=vm((8, wide), F32), acc=vm((2, CH, wide // 2), F32), sem=dma((9,)), osem=dma((2, 2 * NCH)), esem=dma((4,)),
    )


def mlp_phase(k, gather, red, nxt, h, hid, sg, tt, dm):
    at, f, wide = k.at, k.f, k.wide
    dma, vm = pltpu.SemaphoreType.DMA, pltpu.VMEM
    parts = k.parts
    col = lambda j: slice(j * f, (j + 1) * f)
    own = pl.ds(pl.multiple_of(at.r * f, 128), f)

    def run(wg, wu, wd, acc, xbuf, tbuf, sq, sem, wsem, xsem, tsem, rsem, ysem):
        red.acc, nxt.acc = acc, acc
        hcp = local(k.h3, h, sem.at[0])
        hcp.start()
        sq[...] = jnp.zeros_like(sq)

        def slot_in(i):
            s = lax.rem(i, 2)
            return [local(k.x2.at[rows_of(i)], xbuf.at[s], xsem.at[s]), local(k.teach_full.at[rows_of(i)], tbuf.at[s], tsem.at[s])]

        for i in range(2):
            start_all(slot_in(i))
        pending = list(range(k.mid_pieces, len(gather.pieces)))

        def fetch(p):
            q, j = (p - 8) % 2 if p < 16 else 2, (p - 8) // 2 if p < 16 else p - 16
            return local(gather.pieces[p][1], (wg, wu, wd)[q].at[:, col(j)], wsem.at[p - 8])

        done = [8]

        def bring(upto):
            while done[0] <= upto:
                while pending and pending[0] <= done[0] + 1:
                    gather.advance(pending.pop(0))
                gather.finish(done[0])
                fetch(done[0]).start()
                done[0] += 1

        bring(9)
        hcp.wait()
        for j in range(parts):
            if j < parts - 1:
                bring(11 + 2 * j)
            fetch(8 + 2 * j).wait()
            fetch(9 + 2 * j).wait()

            def hidden(i):
                rows = rows_of(i)
                gate = nn(h[rows], wg[:, col(j)])
                up = nn(h[rows], wu[:, col(j)])
                sig = jax.nn.sigmoid(gate)
                act = gate * sig
                hid[rows, col(j)] = (act * up).astype(BF)
                sg[rows, col(j)] = act.astype(BF)
                tt[rows, col(j)] = (up * sig * (1.0 + gate * (1.0 - sig))).astype(BF)

            each(0, NCH, hidden)
            if pending:
                gather.advance(pending.pop(0))
        bring(15 + parts)
        for j in range(parts):
            fetch(16 + j).wait()

        def project(i):
            red.partial(i, [(hid[rows_of(i)], wd)])
            pl.when(i > 0)(lambda: red.swap(i - 1))

        each(0, NCH, project)
        red.swap(NCH - 1)

        def outs_of(i):
            s = lax.rem(i, 2)
            return [local(xbuf.at[s], k.res.at[rows_of(i)], rsem.at[s]), local(tbuf.at[s, :, own], k.y.at[rows_of(i)], ysem.at[s])]

        def finish(i):
            s = lax.rem(i, 2)
            red.ready(i)

            @pl.when(i >= 1)
            def _():
                wait_all(outs_of(i - 1))
                pl.when(i < NCH - 1)(lambda: start_all(slot_in(i + 1)))

            wait_all(slot_in(i))

            def block(b, rs, ls):
                y = xbuf[s, ls] + red.total(rs)
                pos = i * CH + b * SUB + lax.broadcasted_iota(jnp.int32, (SUB, wide), 0)
                res = jnp.where(pos < LEN, y - tbuf[s, ls].astype(F32), 0.0)
                xbuf[s, ls] = res
                dm[rs] = res.astype(BF)
                tbuf[s, ls] = y.astype(BF)
                sq_ = res * res
                sq[...] += sq_[:8] + sq_[8:]

            sub_blocks(i, block)
            start_all(outs_of(i))
            rows = rows_of(i)
            for j in range(parts):
                dh = nn(dm[rows], wd[:, col(j)])
                tt[rows, col(j)] = (dh * tt[rows, col(j)].astype(F32)).astype(BF)
                sg[rows, col(j)] = (dh * sg[rows, col(j)].astype(F32)).astype(BF)
            red.drain(i)
            nxt.partial(i, [(tt[rows], wg), (sg[rows], wu)])
            pl.when(i > 0)(lambda: nxt.swap(i - 1))

        def step(i):
            red.share(i)
            pl.when(i > 0)(lambda: finish(i - 1))

        each(0, NCH, step)
        finish(NCH - 1)
        nxt.swap(NCH - 1)
        scp = local(sq, k.squares, sem.at[0])
        scp.start()
        wait_all(outs_of(NCH - 1))
        scp.wait()

    weight = lambda: vm((wide, parts * f), BF)
    pl.run_scoped(
        run,
        wg=weight(), wu=weight(), wd=weight(), acc=vm((2, CH, wide // 2), F32), xbuf=vm((2, CH, wide), F32), tbuf=vm((2, CH, wide), BF),
        sq=vm((8, wide), F32), sem=dma((1,)), wsem=dma((3 * parts,)), xsem=dma((2,)), tsem=dma((2,)),
        rsem=dma((2,)), ysem=dma((2,)),
    )


class Grads:
    def __init__(self, part, stage, sem, f):
        self.part, self.stage, self.sem, self.f = part, stage, sem, f

    def copy(self, p):
        return local(self.stage, self.part.at[:, p * self.f:(p + 1) * self.f], self.sem.at[p % 2])

    def make(self, p, left, right):
        wide = left.shape[1]

        def one(j):
            cols = pl.ds(pl.multiple_of(j * 512, 128), 512)
            self.stage[cols] = tn(left[:, cols], right()).astype(BF)

        each(0, wide // 512, one)
        self.copy(p).start()


def mid_back_phase(k, scatter, first, second, h, hid, sg, tt, dm):
    at, f, wide = k.at, k.f, k.wide
    dma, vm = pltpu.SemaphoreType.DMA, pltpu.VMEM

    def run(g, low, xs, wc, wq, dkv, dc, cq, ckv, c, lse, dcq, sums, vec, acc, stage, sem, xsem, osem, gsem):
        second.acc = acc
        grads = Grads(k.part, stage, gsem, f)
        rest = [
            local(src, dst, sem.at[j])
            for j, (src, dst) in enumerate(((k.res, g), (k.full[7], wc), (k.full[4], wq), (k.cq, cq), (k.ckv, ckv), (k.c, c), (k.lse2, lse), (k.vecs, vec)))
        ]
        start_all(rest)

        def stream(src, i, s):
            return local(src.at[rows_of(i)], xs.at[s], xsem.at[s])

        stream(k.x2, 0, 0).start()
        stream(k.x2, 1, 1).start()
        sums[...] = jnp.zeros_like(sums)
        dkv[...] = jnp.zeros_like(dkv)

        def make(p):
            q, j = p // 4, p % 4
            left, right = ((h, tt), (h, sg), (dm, hid))[q]
            grads.make(p, left, lambda: right[:, j * f:(j + 1) * f])

        for p in range(2):
            make(p)
            grads.copy(p).wait()
            scatter.start(p)
        wait_all(rest)

        def hook(slot):
            for p in range(2, 12):
                @pl.when(slot == p - 2)
                def _():
                    make(p)
                    grads.copy(p).wait()
                    if p < scatter.ahead:
                        scatter.start(p)

            for p in range(k.back_pieces):
                pl.when(slot == p * 2 * NCH // k.back_pieces + 1)(lambda: scatter.advance(p))

        def low_out(i, which):
            return local(low.at[lax.rem(i + which * NCH, 2)], (k.dco, k.do)[which].at[rows_of(i)], osem.at[which, i])

        def g_out(i):
            return local(g.at[rows_of(i)], k.g1.at[rows_of(i)], osem.at[2, i])

        valid = lambda: lax.broadcasted_iota(jnp.int32, (CP, 1), 0) < CLEN

        def cross(i):
            first.ready(i)
            s = lax.rem(i, 2)
            stream(k.x2, i, s).wait()
            pl.when(i >= 2)(lambda: low_out(i - 2, 0).wait())

            def block(b, rs, ls):
                tot = first.total(rs)
                new, dx = norm_back(tot, xs[s, ls], g[rs], vec[4:5], wide)
                g[rs] = new
                low[s, ls] = new.astype(BF)
                fold(sums, 0, dx)
                fold(sums, 1, tot)

            sub_blocks(i, block)
            pl.when(i < NCH - 2)(lambda: stream(k.x2, i + 2, s).start())
            pl.when(i >= NCH - 2)(lambda: stream(k.x1, i + 2 - NCH, s).start())
            low_out(i, 0).start()
            rows = rows_of(i)
            dc[...] = nn(low[s], wc[...]).astype(BF)
            lse_t = lse[rows].T
            delta = jnp.zeros((CH, 128), F32)
            for pair in range(f // 128):
                cols = slice(128 * pair, 128 * (pair + 1))
                prod = dc[:, cols].astype(F32) * c[rows, cols].astype(F32)
                for which in range(2):
                    one = jnp.sum(head_mask(prod, which), axis=1, keepdims=True)
                    delta = jnp.where(lanes(delta.shape) == 2 * pair + which, one, delta)
            delta_t = delta.T
            for pair in range(f // 128):
                cols = slice(128 * pair, 128 * (pair + 1))
                vcols = slice(f + 128 * pair, f + 128 * (pair + 1))
                kb, vb, qc, doc = ckv[:, cols], ckv[:, vcols], cq[rows, cols], dc[:, cols]
                dks, dvs, dqt = [], [], None
                for which in range(2):
                    hd = 2 * pair + which
                    km = head_mask(kb, which)
                    p = jnp.where(valid(), jnp.exp(nt(km, qc) - lse_t[hd:hd + 1]), 0.0)
                    dp = nt(head_mask(vb, which), doc)
                    ds = (p * (dp - delta_t[hd:hd + 1])).astype(BF)
                    dvs.append(nn(p.astype(BF), doc))
                    dks.append(nn(ds, qc))
                    part = nn(km.T, ds)
                    dqt = part if dqt is None else dqt + part
                left = lanes(dks[0].shape) < HEAD
                dkv[:, cols] += jnp.where(left, dks[0], dks[1])
                dkv[:, vcols] += jnp.where(left, dvs[0], dvs[1])
                dcq[rows, cols] = (dqt.T * HEAD ** (-0.5)).astype(BF)
            first.drain(i)
            second.partial(i, [(dcq[rows], wq)])
            pl.when(i > 0)(lambda: second.swap(i - 1))

        def step(i):
            first.share(i)
            pl.when(i > 0)(lambda: cross(i - 1))
            hook(i)

        each(0, NCH, step)
        cross(NCH - 1)
        second.swap(NCH - 1)
        ckv[...] = dkv[...].astype(BF)

        def last(i):
            second.ready(i)
            s = lax.rem(i + NCH, 2)
            stream(k.x1, i, s).wait()
            pl.when(i < 2)(lambda: low_out(NCH - 2 + i, 0).wait())
            pl.when(i >= 2)(lambda: low_out(i - 2, 1).wait())

            def block(b, rs, ls):
                tot = second.total(rs)
                new, dx = norm_back(tot, xs[s, ls], g[rs], vec[2:3], wide)
                g[rs] = new
                low[s, ls] = new.astype(BF)
                fold(sums, 2, dx)
                fold(sums, 3, tot)

            sub_blocks(i, block)
            pl.when(i < NCH - 2)(lambda: stream(k.x1, i + 2, s).start())
            low_out(i, 1).start()
            g_out(i).start()

        def step_two(i):
            second.share(i)
            pl.when(i > 0)(lambda: last(i - 1))
            hook(NCH + i)

        each(0, NCH, step_two)
        last(NCH - 1)
        ends = [local(dcq, k.dcq, sem.at[0]), local(ckv, k.dckv, sem.at[1]), local(sums, k.sums, sem.at[2])]
        start_all(ends)

        def end(i):
            second.drain(i)
            pl.when(i >= NCH - 2)(lambda: low_out(i, 1).wait())
            g_out(i).wait()

        each(0, NCH, end)
        wait_all(ends)

    pl.run_scoped(
        run,
        g=vm((TP, wide), F32), low=vm((2, CH, wide), BF), xs=vm((2, CH, wide), F32), wc=vm((wide, f), BF), wq=vm((wide, f), BF),
        dkv=vm((CP, 2 * f), F32), dc=vm((CH, f), BF), cq=vm((TP, f), BF), ckv=vm((CP, 2 * f), BF), c=vm((TP, f), BF),
        lse=vm((TP, 128), F32), dcq=vm((TP, f), BF), sums=vm((4, 8, wide), F32), vec=vm((8, wide), F32), acc=vm((2, CH, wide // 2), F32),
        stage=vm((wide, f), BF), sem=dma((8,)), xsem=dma((2,)), osem=dma((3, NCH)), gsem=dma((2,)),
    )


def end_phase(k, scatter):
    at, f, wide = k.at, k.f, k.wide
    dma, vm = pltpu.SemaphoreType.DMA, pltpu.VMEM
    r, c_, o = at.r, at.c, at.o
    own = pl.ds(pl.multiple_of(r * f, 128), f)
    send_a, recv_a = k.send_a, k.recv_a
    send_b, recv_b = k.p1.at[0, :, :f], k.p2.at[0, :, :f]

    def run(xa, xb, wt, w1, da, dqkv, lse_t, delta_t, dqt, stage, xo, go, g1, tot, acc, st, back, st_t, cpart, qkv, a, lse, trig,
            cos, low, high, c, dcq, dckv, cond, sums, sq, vr, vb, lat, gc, sem, gsem, s_c, s_x, s_v):
        grads = Grads(k.part, stage, gsem, f)
        names = {}

        def load(name, src, dst):
            names[name] = local(src, dst, sem.at[len(names)])
            names[name].start()

        load("do", k.do, xa)
        load("wo", k.full[3], wt)
        load("a", k.a, a)
        load("qkv", k.qkv, qkv)
        load("lse", k.lse1, lse)
        load("trig", k.trig, trig)
        load("h2", k.h2, xb)
        load("c", k.c, c)
        load("dcq", k.dcq, dcq)
        load("dckv", k.dckv, dckv)
        load("cond", k.cond_full, cond)
        rest = ["st", "xo", "go", "g1", "sums", "sq"]
        for name, src, dst in (
            ("st", k.st1, st), ("xo", k.x0.at[:, own], xo), ("go", k.vecs.at[:, own], go), ("g1", k.g1.at[:, own], g1),
            ("sums", k.sums.at[:, :, own], sums), ("sq", k.squares, sq),
        ):
            load(name, src, dst)
        for j in range(3):
            load(f"w{j}", k.full[j], w1.at[:, j * f:(j + 1) * f])
            rest.append(f"w{j}")

        def ready(*which):
            for name in which:
                names[name].wait()

        def make(p, left, right):
            grads.make(p, left, right)
            grads.copy(p).wait()

        ready("do", "wo", "a")

        def project_da(i):
            da[rows_of(i)] = nn(xa[rows_of(i)], wt[...]).astype(BF)

        each(0, NCH, project_da)
        make(12, xa, lambda: a[...])
        again = local(k.dco, xa, sem.at[0])
        again.start()
        wck_cp = local(k.full[5], wt, sem.at[1])
        wck_cp.start()
        ready("qkv", "lse", "trig")
        spread_tables(trig, cos, low, high)

        def emit_q(pair, dq):
            dqkv[:, 128 * pair:128 * (pair + 1)] = rotate_lanes(dq * HEAD ** (-0.5), cos[...], -low[...], -high[...]).astype(BF)

        def emit_kv(pair, rows, dk, dv):
            dqkv[rows, f + 128 * pair:f + 128 * (pair + 1)] = rotate_lanes(dk, cos[rows], -low[rows], -high[rows]).astype(BF)
            dqkv[rows, 2 * f + 128 * pair:2 * f + 128 * (pair + 1)] = dv.astype(BF)

        pairs = f // 128
        nxt = k.back_pieces

        def hook(pair, j):
            pl.when(j == 3)(lambda: scatter.advance(nxt + pair))

        attend_back(qkv, 0, qkv, f, qkv, 2 * f, TP, CH, LEN, da, a, lse, lse_t, delta_t, dqt, emit_q, emit_kv, f // HEAD, hook)
        nxt = nxt + pairs

        ready("h2", "c", "dcq", "dckv", "cond")
        again.wait()
        make(13, xa, lambda: c[...])
        make(14, xb, lambda: dcq[...])
        h1_cp = local(k.h1, xb, sem.at[0])
        h1_cp.start()
        make(15, cond, lambda: dckv[:, :f])
        make(16, cond, lambda: dckv[:, f:])
        scatter.advance(nxt)
        wck_cp.wait()
        for j in range(4):
            cpart[j] = nt(dckv[:, :f], wt[j * f:(j + 1) * f])
        wcv_cp = local(k.full[6], wt, sem.at[1])
        wcv_cp.start()
        h1_cp.wait()
        for j in range(3):
            make(17 + j, xb, lambda: dqkv[:, j * f:(j + 1) * f])
        scatter.advance(nxt + 1)
        wcv_cp.wait()
        crecv = k.crecv
        for j in range(4):
            crecv[j] = (cpart[j] + nt(dckv[:, f:], wt[j * f:(j + 1) * f])).astype(BF)
        peers = (at.sib, at.par, at.diag)
        cond_cps = [remote(crecv.at[peers[j][0]], crecv.at[4 + j], s_c.at[j], k.r_c.at[j], peers[j]) for j in range(3)]
        start_all(cond_cps)
        ready(*rest)

        wblock = lambda j: w1[pl.ds(pl.multiple_of(j * f, 128), f)]

        def copy_a(i):
            return remote(send_a.at[rows_of(i)], recv_a.at[rows_of(i)], k.e_sa.at[i], k.e_ra.at[i], at.sib)

        def copy_b(i):
            return remote(send_b.at[rows_of(i)], recv_b.at[rows_of(i)], k.e_sb.at[i], k.e_rb.at[i], at.par)

        def swap(i):
            copy_a(i).wait_recv()
            both = acc[lax.rem(i, 2)] + recv_a[rows_of(i)].astype(F32)
            left, right = both[:, :f], both[:, f:]
            tot[rows_of(i)] = jnp.where(at.xi == 0, left, right)
            send_b[rows_of(i)] = jnp.where(at.xi == 0, right, left).astype(BF)
            pl.semaphore_wait(k.last_sum.free.at[i], 1)
            copy_b(i).start()

        def project(i):
            y = dqkv[rows_of(i)]
            send_a[rows_of(i), :f] = nt(y, wblock(o)).astype(BF)
            send_a[rows_of(i), f:] = nt(y, wblock(2 + o)).astype(BF)
            copy_a(i).start()
            acc[lax.rem(i, 2), :, :f] = nt(y, wblock(c_))
            acc[lax.rem(i, 2), :, f:] = nt(y, wblock(2 + c_))
            pl.when(i > 0)(lambda: swap(i - 1))

        each(0, NCH, project)
        swap(NCH - 1)
        vr[...] = jnp.zeros_like(vr)
        scatter.advance(nxt + 2)

        def sums_of(i):
            copy_b(i).wait_recv()

            def block(b, rs, ls):
                t = tot[rs] + recv_b[rs].astype(F32)
                tot[rs] = t
                own_st = st[rs]
                mean, inv = own_st[:, 2:3], own_st[:, 3:4]
                xh = (xo[rs].astype(F32) - mean) * inv
                e = t * go[0:1]
                lane = lanes((SUB, 128))
                first = jnp.sum(e, axis=1, keepdims=True)
                cross = jnp.sum(e * xh, axis=1, keepdims=True)
                back[rs] = jnp.where(lane == 0, first, cross)
                fold(vr, 0, t * xh)
                fold(vr, 1, t)

            sub_blocks(i, block)

        each(0, NCH, sums_of)
        sx = k.sx
        st_t[...] = back[...].T
        sx[0] = st_t[:8]
        stat_cps = [remote(sx.at[0], sx.at[1 + j], s_x.at[j], k.r_x.at[j], peers[j]) for j in range(3)]
        start_all(stat_cps)
        total = lambda x: jnp.sum(x, axis=0, keepdims=True)
        error = jnp.sum(total(sq[...]), axis=1, keepdims=True)
        vb[0:1] = total(vr[0])
        vb[1:2] = total(vr[1])
        vb[2:3] = total(sums[2])
        vb[3:4] = total(sums[3])
        vb[4:5] = total(sums[0])
        vb[5:6] = total(sums[1])
        vb[6:8] = jnp.broadcast_to(error, (2, f))
        vz = k.vz
        pair_cp = remote(vb, vz.at[at.outer], s_v.at[at.outer], k.r_v.at[at.outer], at.ypar)
        pair_cp.start()
        scatter.advance(nxt + 3)
        for cp in cond_cps:
            cp.wait_recv()
        gc[...] = (crecv[r].astype(F32) + crecv[4].astype(F32) + crecv[5].astype(F32) + crecv[6].astype(F32)).astype(BF)
        for cp in stat_cps:
            cp.wait_recv()
        st_t[:8] = sx[0] + sx[1] + sx[2] + sx[3]
        back[...] = st_t[...].T
        pair_cp.wait()
        vz[at.zo] = vb[...] + vz[at.outer]

        def vec_out(step):
            return remote(vz.at[at.zo], vz.at[at.zo], s_v.at[step], k.r_v.at[at.zo], (r, 2 * at.zpeer(step) + at.yi))

        each(1, at.outer, lambda step: vec_out(step).start())

        def last(i):
            def block(b, rs, ls):
                e = tot[rs] * go[0:1]
                row_sums, own_st = back[rs], st[rs]
                first, cross = row_sums[:, 0:1] * (1.0 / wide), row_sums[:, 1:2] * (1.0 / wide)
                mean, inv = own_st[:, 2:3], own_st[:, 3:4]
                xh = (xo[rs].astype(F32) - mean) * inv
                lat[rs] = (g1[rs] + inv * (e - first - xh * cross)).astype(BF)

            sub_blocks(i, block)

        each(0, NCH, last)
        outs = [local(lat, k.glat, sem.at[0]), local(gc, k.gcond, sem.at[1])]
        start_all(outs)
        for p in range(nxt + 4, len(scatter.pieces)):
            scatter.advance(p)
        vb[...] = vz[at.zo]

        def vec_in(step):
            zs = at.zpeer(at.outer - step)
            remote(vz.at[zs], vz.at[zs], s_v.at[step], k.r_v.at[zs], at.ypar).wait_recv()
            vb[...] += vz[zs]

        each(1, at.outer, vec_in)
        vec_cp = local(vb, k.vec, sem.at[2])
        vec_cp.start()
        each(1, at.outer, lambda step: vec_out(step).wait_send())
        scatter.complete()
        for cp in stat_cps + cond_cps:
            cp.wait_send()

        def drain(i):
            copy_a(i).wait_send()
            copy_b(i).wait_send()

        each(0, NCH, drain)
        wait_all(outs + [vec_cp])

    tab = lambda: vm((TP, 128), F32)
    flip = lambda: vm((128, TP), F32)
    pl.run_scoped(
        run,
        xa=vm((TP, wide), BF), xb=vm((TP, wide), BF), wt=vm((wide, f), BF), w1=vm((wide, 3 * f), BF), da=vm((TP, f), BF),
        dqkv=vm((TP, 3 * f), BF), lse_t=flip(), delta_t=flip(), dqt=flip(), stage=vm((wide, f), BF), xo=vm((TP, f), BF),
        go=vm((8, f), F32), g1=vm((TP, f), F32), tot=vm((TP, f), F32), acc=vm((2, CH, 2 * f), F32), st=tab(), back=tab(), st_t=flip(),
        cpart=vm((4, CP, f), F32), qkv=vm((TP, 3 * f), BF), a=vm((TP, f), BF), lse=tab(), trig=tab(), cos=tab(), low=tab(), high=tab(),
        c=vm((TP, f), BF), dcq=vm((TP, f), BF), dckv=vm((CP, 2 * f), BF), cond=vm((CP, wide), BF), sums=vm((4, 8, f), F32),
        sq=vm((8, wide), F32), vr=vm((2, 8, f), F32), vb=vm((8, f), F32), lat=vm((TP, f), BF), gc=vm((CP, f), BF),
        sem=dma((24,)), gsem=dma((2,)), s_c=dma((3,)), s_x=dma((3,)), s_v=dma((k.outer + 1,)),
    )


class Names:
    pass


def layer_kernel(n, f, pieces, front_pieces, mid_pieces, back_pieces, ahead, s_ahead, slots, *refs):
    refs = list(refs)
    take = lambda count: [refs.pop(0) for _ in range(count)]
    k = Names()
    k.at, k.f, k.wide, k.outer = Place(n), f, 4 * f, n // 2
    k.front_pieces, k.mid_pieces, k.back_pieces = front_pieces, mid_pieces, back_pieces
    k.lat, k.teach, k.cond, k.trig = take(4)
    k.small = take(6)
    shards = take(11)
    k.y, k.glat, k.gcond, k.vec = take(4)
    gate_out, up_out, down_out = take(3)
    square_out = take(8)
    k.full = take(8)
    mlp_full = take(3)
    k.x0, k.vecs, k.cond_full, k.teach_full, k.h1, k.st1, k.qkv, k.a, k.lse1 = take(9)
    k.x1, k.h2, k.cq, k.ckv, k.c, k.lse2, k.x2, k.h3 = take(8)
    k.res, k.squares, k.g1, k.dco, k.do, k.dcq, k.dckv, k.sums, k.part = take(9)
    k.send_a, k.recv_a, k.p1, k.p2, k.sx, k.crecv, k.vz = take(7)
    sems = [take(8) for _ in range(5)]
    free = take(5)
    k.e_sa, k.e_ra, k.e_sb, k.e_rb, k.row_sem, k.r_c, k.r_x, k.r_v = take(8)
    gather_sem = take(3)
    bufs, scatter_sem = take(5), take(8)
    k.parts = shards[8].shape[1] // f
    col = lambda j: slice(j * f, (j + 1) * f)
    made = [(shards[j], k.full[j]) for j in range(8)]
    for j in range(k.parts):
        for q in range(2):
            made.append((shards[8 + q].at[:, col(j)], mlp_full[q].at[:, col(j)]))
    made += [(shards[10].at[:, col(j)], mlp_full[2].at[:, col(j)]) for j in range(k.parts)]
    gather = ColGather(k.at, made, ahead, *gather_sem)
    sums = []
    for q, out in enumerate((gate_out, up_out, down_out)):
        sums += [(k.part.at[:, col(q * k.parts + j)], out.at[:, col(j)]) for j in range(k.parts)]
    sums += [(k.part.at[:, col(3 * k.parts + j)], square_out[j]) for j in range(8)]
    scatter = ColScatter(k.at, sums, s_ahead, slots, bufs, scatter_sem)
    red = [None]
    for j in range(5):
        red.append(RowReduce(k.at, k.send_a, k.recv_a, None, k.p1, k.p2, sems[j], free[j], red[j]))
    red = red[1:]
    k.last_sum = red[4]
    front_phase(k, gather)
    mid_phase(k, gather, red[0], red[1])
    full = pltpu.VMEM((TP, k.wide), BF)

    def back(h, hid, sg, tt, dm):
        mlp_phase(k, gather, red[2], red[3], h, hid, sg, tt, dm)
        mid_back_phase(k, scatter, red[3], red[4], h, hid, sg, tt, dm)

    pl.run_scoped(back, h=full, hid=full, sg=full, tt=full, dm=full)
    end_phase(k, scatter)


def layer_call(n, lat, teach, cond, trig, small, shards, front_pieces=9, mid_pieces=15, back_pieces=5, ahead=4, s_ahead=2, slots=4):
    f = lat.shape[1]
    wide, size, outer = 4 * f, shards[0].shape[0], n // 2
    ffl = shards[8].shape[1]
    sd = jax.ShapeDtypeStruct
    dma = pltpu.SemaphoreType.DMA
    vm = pltpu.VMEM
    half = wide // 2
    results = [sd((TP, f), BF), sd((TP, f), BF), sd((CP, f), BF), sd((8, f), F32)]
    results += [sd((size, ffl), F32)] * 3 + [sd((size, f), F32)] * 8
    between = [sd((wide, f), BF)] * 8 + [sd((wide, ffl), BF)] * 3
    rows, rows32 = sd((TP, wide), BF), sd((TP, wide), F32)
    between += [rows, sd((8, wide), F32), sd((CP, wide), BF), rows, rows, sd((TP, 128), F32), sd((TP, 3 * f), BF), sd((TP, f), BF), sd((TP, 128), F32)]
    between += [rows32, rows, sd((TP, f), BF), sd((CP, 2 * f), BF), sd((TP, f), BF), sd((TP, 128), F32), rows32, rows]
    between += [rows32, sd((8, wide), F32), rows32, rows, rows, sd((TP, f), BF), sd((CP, 2 * f), BF), sd((4, 8, wide), F32), sd((wide, 3 * ffl + 8 * f), BF)]
    pieces = 8 + 3 * ffl // f
    scratch = [
        vm((TP, half), BF), vm((TP, half), BF), vm((2, TP, half), BF), vm((2, TP, half), BF),
        vm((4, 8, TP), F32), vm((7, CP, f), BF), vm((outer + 1, 8, f), F32),
    ] + [dma((NCH,))] * 40 + [pltpu.SemaphoreType.REGULAR((NCH,))] * 5 + [dma((NCH,))] * 4 + [dma((4, 3)), dma((3,)), dma((3,)), dma((outer + 1,))]
    bufs, sems = scatter_scratch(pieces, slots, n, f, wide)
    scratch += gather_sems(pieces, n) + bufs + sems
    out = pl.pallas_call(
        functools.partial(layer_kernel, n, f, pieces, front_pieces, mid_pieces, back_pieces, ahead, s_ahead, slots),
        out_shape=results + between,
        in_specs=[hspec()] * 4 + [vspec()] * 6 + [hspec()] * 11,
        out_specs=[hspec()] * (len(results) + len(between)),
        scratch_shapes=scratch,
        compiler_params=pltpu.CompilerParams(collective_id=0, has_side_effects=True, vmem_limit_bytes=66_900_000),
        name="layer",
    )(lat, teach, cond, trig, *small, *shards)
    return out[:len(results)]


def emit_kernel(n, scale, *refs):
    refs = list(refs)
    take = lambda count: [refs.pop(0) for _ in range(count)]
    moved, grads = take(4), take(11)
    y_out, lat_out, cond_out, vec_out = take(4)
    grad_outs = take(11)
    y, lat, cond, vec, sem, vsem = take(6)
    held = take(11)
    cps = [local(src, dst, sem.at[j]) for j, (src, dst) in enumerate(zip(grads, held))]
    out_cps = [local(src, dst, sem.at[j]) for j, (src, dst) in enumerate(zip(held, grad_outs))]
    ins = [local(src, dst, vsem.at[j]) for j, (src, dst) in enumerate(zip(moved, (y, lat, cond, vec)))]
    start_all(cps + ins)
    for cp, out in zip(cps, out_cps):
        cp.wait()
        out.start()
    wait_all(ins)
    y_out[...] = y[:y_out.shape[0]]
    lat_out[...] = lat[:lat_out.shape[0]]
    cond_out[...] = cond[:cond_out.shape[0]]
    width = vec_out.shape[1]
    v = vec[...]
    rows = lax.broadcasted_iota(jnp.int32, v.shape, 0)
    turned = pltpu.roll(v, lax.rem((n - lax.axis_index("col")) * width, v.shape[1]), 1)
    vec_out[...] = jnp.where(rows == 6, v * scale, turned)[:, :width]
    wait_all(out_cps)


def emit_call(n, scale, y, lat, cond, vec, grads):
    f = y.shape[1]
    sd = jax.ShapeDtypeStruct
    return pl.pallas_call(
        functools.partial(emit_kernel, n, scale),
        out_shape=[sd((LEN, f), BF), sd((LEN, f), BF), sd((CLEN, f), BF), sd((8, f // n), F32)] + [sd(g.shape, F32) for g in grads],
        in_specs=[hspec()] * 15,
        out_specs=[vspec()] * 4 + [hspec()] * 11,
        scratch_shapes=[
            pltpu.VMEM((TP, f), BF), pltpu.VMEM((TP, f), BF), pltpu.VMEM((CP, f), BF), pltpu.VMEM((8, f), F32),
            pltpu.SemaphoreType.DMA((11,)), pltpu.SemaphoreType.DMA((4,)),
        ] + [pltpu.VMEM(g.shape, F32) for g in grads],
        compiler_params=pltpu.CompilerParams(vmem_limit_bytes=62 << 20),
        name="emit",
    )(y, lat, cond, vec, *grads)


def trig_table():
    half_size = ROT // 2
    rates = np.exp(np.arange(half_size) * (-2.0 * math.log(10000.0) / ROT))
    angles = np.arange(TP)[:, None] * rates[None, :]
    table = np.zeros((TP, 128), np.float32)
    table[:, :half_size], table[:, half_size:ROT] = np.cos(angles), np.sin(angles)
    return jnp.asarray(table)


def body(
    latents,
    conditioning,
    teacher,
    gain_attn,
    bias_attn,
    gain_cross,
    bias_cross,
    gain_mlp,
    bias_mlp,
    w_query,
    w_key,
    w_value,
    w_out,
    w_cross_query,
    w_cross_key,
    w_cross_value,
    w_cross_out,
    w_gate,
    w_up,
    w_down,
):

    F = latents.shape[1]
    wide = F * lax.axis_size("row")
    n = lax.axis_size("col")
    y, glat, gcond, vec, *grads = layer_call(
        n, latents, teacher, conditioning, trig_table(), [gain_attn, bias_attn, gain_cross, bias_cross, gain_mlp, bias_mlp],
        [w_query, w_key, w_value, w_out.T, w_cross_query, w_cross_key, w_cross_value, w_cross_out.T, w_gate, w_up, w_down.T],
    )
    outputs, glat, gcond, vec, ggate, gup, gdown, go, gco, gcq, gck, gcv, gq, gk, gv = emit_call(
        n, 1.0 / (LEN * wide * n), y, glat, gcond, vec, grads
    )
    return (
        outputs, vec[6, 0], glat, gcond, gq, gk, gv, go.T, gcq, gck, gcv, gco.T, ggate, gup, gdown.T,
        vec[0], vec[1], vec[2], vec[3], vec[4], vec[5],
    )


def solution(mesh):
    in_specs = (
        P("col", "row"),
        P("col", "row"),
        P("col", "row"),
        P("row"),
        P("row"),
        P("row"),
        P("row"),
        P("row"),
        P("row"),
        P("col", "row"),
        P("col", "row"),
        P("col", "row"),
        P("row", "col"),
        P("col", "row"),
        P("col", "row"),
        P("col", "row"),
        P("row", "col"),
        P("col", "row"),
        P("col", "row"),
        P("row", "col"),
    )
    out_specs = (
        P("col", "row"),
        P(),
        P("col", "row"),
        P("col", "row"),
        P("col", "row"),
        P("col", "row"),
        P("col", "row"),
        P("row", "col"),
        P("col", "row"),
        P("col", "row"),
        P("col", "row"),
        P("row", "col"),
        P("col", "row"),
        P("col", "row"),
        P("row", "col"),
        P(("row", "col")),
        P(("row", "col")),
        P(("row", "col")),
        P(("row", "col")),
        P(("row", "col")),
        P(("row", "col")),
    )
    return jax.shard_map(body, mesh=mesh, in_specs=in_specs, out_specs=out_specs, check_vma=False)
```

```python
import functools
import math

import jax
import jax.numpy as jnp
import numpy as np
from jax import lax
from jax.sharding import PartitionSpec as P
from jax.experimental import pallas as pl
from jax.experimental.pallas import tpu as pltpu

BF, F32 = jnp.bfloat16, jnp.float32
MESH = pl.DeviceIdType.MESH
TP = 1040
LEN = 1025
CLEN = 130
CP = 144
HEAD = 64
ROT = 32
EPSILON = 1e-06
CH = 208
NCH = TP // CH
SUB = 16


def nt(a, b):
    return lax.dot_general(a, b, (((1,), (1,)), ((), ())), preferred_element_type=F32)


def remote(src, dst, ssem, rsem, dev):
    return pltpu.make_async_remote_copy(src_ref=src, dst_ref=dst, send_sem=ssem, recv_sem=rsem, device_id=dev, device_id_type=MESH)


def tn(left, right):
    return lax.dot_general(left, right, (((0,), (0,)), ((), ())), preferred_element_type=F32)


def row_stats(x, wide):
    xc = x - jnp.sum(x, axis=1, keepdims=True) * (1.0 / wide)
    inv = lax.rsqrt(jnp.sum(xc * xc, axis=1, keepdims=True) * (1.0 / wide) + EPSILON)
    return xc * inv, inv


def rotate_lanes(u, cos, sin_low, sin_high):
    width = u.shape[-1]
    return u * cos + pltpu.roll(u, width - ROT // 2, u.ndim - 1) * sin_low + pltpu.roll(u, ROT // 2, u.ndim - 1) * sin_high


def vspec():
    return pl.BlockSpec(memory_space=pltpu.VMEM)


def hspec():
    return pl.BlockSpec(memory_space=pl.ANY)


class Place:
    def __init__(self, n):
        self.n, self.outer = n, n // 2
        self.r, self.col = lax.axis_index("row"), lax.axis_index("col")
        self.c = lax.rem(self.r, 2)
        self.o = 1 - self.c
        self.xi = lax.div(self.r, 2)
        self.sib = (self.r + 1 - 2 * self.c, self.col)
        self.par = (self.r + 2 - 4 * self.xi, self.col)
        self.diag = (self.par[0] + 1 - 2 * self.c, self.col)
        self.zo, self.yi = lax.div(self.col, 2), lax.rem(self.col, 2)
        self.ypar = (self.r, self.col + 1 - 2 * self.yi)

    def zpeer(self, step):
        return lax.rem(self.zo + step, self.outer)

    def near(self, z):
        gap = z - self.zo
        return jnp.logical_and(gap < 3, gap > -3)

    def enter(self, with_cols, diagonal=False):
        barrier = pltpu.get_barrier_semaphore()
        pl.semaphore_signal(barrier, inc=1, device_id=self.sib, device_id_type=MESH)
        pl.semaphore_signal(barrier, inc=1, device_id=self.par, device_id_type=MESH)
        count = 2
        if diagonal:
            pl.semaphore_signal(barrier, inc=1, device_id=self.diag, device_id_type=MESH)
            count += 1
        if with_cols:
            pl.semaphore_signal(barrier, inc=1, device_id=self.ypar, device_id_type=MESH)

            def greet(step, carry):
                pl.semaphore_signal(barrier, inc=1, device_id=(self.r, 2 * self.zpeer(step) + self.yi), device_id_type=MESH)
                return carry

            lax.fori_loop(1, self.outer, greet, 0)
            count += self.outer
        pl.semaphore_wait(barrier, count)


class ColGather:
    more = 8

    def __init__(self, place, pieces, ahead, ssem, rsem, lsem):
        self.at, self.pieces, self.ahead, self.ssem, self.rsem, self.lsem = place, pieces, ahead, ssem, rsem, lsem
        self.line = place.outer == 4

    def rows(self, p, j):
        size = self.pieces[p][0].shape[0]
        return self.pieces[p][1].at[pl.ds(pl.multiple_of(j * size, 16), size)]

    def local(self, p):
        return pltpu.make_async_copy(self.pieces[p][0], self.rows(p, self.at.col), self.lsem.at[p])

    def send(self, p, slot, j, to, own=False):
        src = self.pieces[p][0] if own else self.rows(p, j)
        return remote(src, self.rows(p, j), self.ssem.at[p, slot], self.rsem.at[p, j], to)

    def across(self, p):
        return self.send(p, 0, self.at.col, self.at.ypar, own=True)

    def outward(self, p, step):
        at = self.at
        return self.send(p, step, at.col, (at.r, 2 * at.zpeer(step) + at.yi), own=True)

    def onward(self, p, step):
        at = self.at
        return self.send(p, at.outer - 1 + step, 2 * at.zpeer(at.outer - step) + at.yi, at.ypar)

    def steps(self, fn, source, far=False):
        at = self.at
        if far and not self.line:
            return

        def one(step):
            if not self.line:
                fn(step)
                return
            near = at.near(at.zpeer(at.outer - step) if source else at.zpeer(step))
            pl.when(jnp.logical_not(near) if far else near)(lambda: fn(step))

        each(1, at.outer, one)

    def relay(self, p, act):
        if not self.line:
            return
        at = self.at
        for mine, source, end in ((2, 0, 3), (1, 3, 0)):
            pl.when(at.zo == mine)(lambda: act(self.send(p, at.n - 1, 2 * source + at.yi, (at.r, 2 * end + at.yi))))

    def start(self, p):
        if p < len(self.pieces):
            self.local(p).start()
            self.across(p).start()
            self.steps(lambda step: self.outward(p, step).start(), False)

    def pass_on(self, p, far):
        def one(step):
            cp = self.onward(p, step)
            cp.wait_recv()
            cp.start()

        self.steps(one, True, far)

    def started(self, p):
        return self.ahead + p + 1 + max(0, min(p - 2, self.more))

    def begin(self):
        for p in range(self.ahead):
            self.start(p)

    def advance(self, p, flush=True):
        self.pass_on(p, False)
        self.relay(p, lambda cp: cp.start())
        for later in range(self.started(p - 1), self.started(p)):
            self.start(later)
        if flush and p > 0:
            self.pass_on(p - 1, True)
        if p == len(self.pieces) - 1:
            self.pass_on(p, True)

    def finish(self, p):
        at = self.at
        self.local(p).wait()
        self.across(p).wait_send()
        self.steps(lambda step: self.outward(p, step).wait_send(), False)
        each(0, at.outer, lambda z: self.send(p, 0, 2 * z + 1 - at.yi, at.ypar).wait_recv())
        self.steps(lambda step: self.onward(p, step).wait_send(), True)
        self.steps(lambda step: self.onward(p, step).wait_send(), True, far=True)
        self.relay(p, lambda cp: cp.wait_send())


def gather_sems(pieces, n):
    return [pltpu.SemaphoreType.DMA((pieces, n)), pltpu.SemaphoreType.DMA((pieces, n)), pltpu.SemaphoreType.DMA((pieces,))]


class ColScatter:
    def __init__(self, place, pieces, ahead, slots, bufs, sems):
        self.at, self.pieces, self.ahead, self.slots = place, pieces, ahead, slots
        self.ry, self.hb, self.rz, self.rl, self.ob = bufs
        self.ls, self.sy, self.ryr, self.sz, self.rzr, self.rlr, self.os, self.credit = sems
        self.line = place.outer == 4
        self.size = self.hb.shape[2]

    def rows(self, p, j):
        return self.pieces[p][0].at[pl.ds(pl.multiple_of(j * self.size, 16), self.size)]

    def across(self, p, z):
        at = self.at
        return remote(
            self.rows(p, 2 * z + 1 - at.yi), self.ry.at[p % self.slots, z], self.sy.at[p, z], self.ryr.at[p, z], at.ypar
        )

    def own(self, p, z):
        return pltpu.make_async_copy(self.rows(p, 2 * z + self.at.yi), self.hb.at[p % 2, z], self.ls.at[p, z])

    def outward(self, p, z):
        at, s = self.at, p % self.slots
        return remote(self.ry.at[s, z], self.rz.at[s, at.zo], self.sz.at[p, z], self.rzr.at[p, at.zo], (at.r, 2 * z + at.yi))

    def detour(self, p, z):
        at, s = self.at, p % self.slots
        via = lax.div(at.zo, 3) + 1
        return remote(self.ry.at[s, z], self.rl.at[s], self.sz.at[p, z], self.rlr.at[p], (at.r, 2 * via + at.yi))

    def merging(self, z):
        zo = self.at.zo
        return jnp.logical_or(jnp.logical_and(zo == 1, z == 3), jnp.logical_and(zo == 2, z == 0))

    def arrives(self, zs):
        return self.at.near(zs)

    def blocks(self, fn):
        each(0, self.size // 48, lambda k: fn(pl.ds(pl.multiple_of(k * 48, 16), 48)))

    def begin(self):
        for p in range(self.ahead):
            self.start(p)

    def start(self, p):
        if p >= len(self.pieces):
            return
        if p >= self.slots:
            pl.semaphore_wait(self.credit.at[p - self.slots], self.at.outer)

        def one(z):
            self.across(p, z).start()
            if p < 2:
                self.own(p, z).start()

        each(0, self.at.outer, one)

    def reduce(self, p):
        at, s = self.at, p % self.slots

        def one(step):
            z = at.zpeer(step)
            self.own(p, z).wait()
            self.across(p, z).wait_recv()

            def add(rs):
                self.ry[s, z, rs] = (self.hb[p % 2, z, rs].astype(F32) + self.ry[s, z, rs].astype(F32)).astype(BF)

            self.blocks(add)

            @pl.when(z != at.zo)
            def _():
                if not self.line:
                    self.outward(p, z).start()
                    return
                near = at.near(z)
                pl.when(jnp.logical_not(near))(lambda: self.detour(p, z).start())
                pl.when(jnp.logical_and(near, jnp.logical_not(self.merging(z))))(lambda: self.outward(p, z).start())

        each(1, at.outer + 1, one)
        if p + 2 < len(self.pieces):
            each(0, at.outer, lambda z: self.own(p + 2, z).start())

    def merge(self, p):
        if not self.line:
            return
        at, s = self.at, p % self.slots
        for mine, z, origin in ((1, 3, 0), (2, 0, 3)):
            @pl.when(at.zo == mine)
            def _():
                remote(self.rl.at[s], self.rl.at[s], self.sz.at[p, z], self.rlr.at[p], at.ypar).wait_recv()

                def add(rs):
                    self.ry[s, z, rs] = (self.ry[s, z, rs].astype(F32) + self.rl[s, rs].astype(F32)).astype(BF)

                self.blocks(add)
                self.outward(p, z).start()

    def result(self, p):
        return pltpu.make_async_copy(self.ob.at[p % 2], self.pieces[p][1], self.os.at[p])

    def finish(self, p):
        at, s = self.at, p % self.slots
        if p >= 2:
            self.result(p - 2).wait()

        def first(rs):
            self.ob[p % 2, rs] = self.ry[s, at.zo, rs].astype(F32)

        self.blocks(first)

        def one(step):
            zs = at.zpeer(at.outer - step)

            def take():
                remote(self.rz.at[s, zs], self.rz.at[s, zs], self.sz.at[p, zs], self.rzr.at[p, zs], at.ypar).wait_recv()

                def add(rs):
                    self.ob[p % 2, rs] += self.rz[s, zs, rs].astype(F32)

                self.blocks(add)

            if self.line:
                pl.when(at.near(zs))(take)
            else:
                take()

        each(1, at.outer, one)
        self.result(p).start()

        def sent(z):
            self.across(p, z).wait_send()

            @pl.when(z != at.zo)
            def _():
                self.outward(p, z).wait_send()

        each(0, at.outer, sent)
        if p + self.slots < len(self.pieces):
            pl.semaphore_signal(self.credit.at[p], inc=1, device_id=at.ypar, device_id_type=MESH)
            each(
                1,
                at.outer,
                lambda step: pl.semaphore_signal(
                    self.credit.at[p], inc=1, device_id=(at.r, 2 * at.zpeer(step) + at.yi), device_id_type=MESH
                ),
            )

    def advance(self, p):
        if p < len(self.pieces):
            self.reduce(p)
        if 0 <= p - 1 < len(self.pieces):
            self.merge(p - 1)
        if 0 <= p - 2 < len(self.pieces):
            self.finish(p - 2)
        self.start(p + self.ahead)

    def complete(self):
        count = len(self.pieces)
        self.advance(count)
        self.advance(count + 1)
        for p in range(max(0, count - 2), count):
            self.result(p).wait()


def scatter_scratch(pieces, slots, n, f, rows):
    size, outer = rows // n, n // 2
    dma = pltpu.SemaphoreType.DMA
    block = lambda *lead: pltpu.VMEM(lead + (size, f), BF)
    return [
        block(slots, outer), block(2, outer), block(slots, outer), block(slots),
        pltpu.VMEM((2, size, f), F32),
    ], [
        dma((pieces, outer)), dma((pieces, outer)), dma((pieces, outer)), dma((pieces, outer)), dma((pieces, outer)),
        dma((pieces,)), dma((pieces,)), pltpu.SemaphoreType.REGULAR((pieces,)),
    ]


class RowGather:
    def __init__(self, place, pieces, ssem, rsem, lsem):
        self.at, self.pieces, self.ssem, self.rsem, self.lsem = place, pieces, ssem, rsem, lsem

    def cols(self, p, j):
        size = self.pieces[p][0].shape[1]
        return self.pieces[p][1].at[:, pl.ds(pl.multiple_of(j * size, 128), size)]

    def copies(self, p):
        at = self.at
        src, mine = self.pieces[p][0], self.cols(p, at.r)
        theirs = self.cols(p, at.par[0])
        return (
            pltpu.make_async_copy(src, mine, self.lsem.at[p]),
            remote(src, mine, self.ssem.at[p, 0], self.rsem.at[p, 0], at.sib),
            remote(src, mine, self.ssem.at[p, 1], self.rsem.at[p, 1], at.par),
            remote(theirs, theirs, self.ssem.at[p, 2], self.rsem.at[p, 2], at.sib),
        )

    def start(self, p):
        for cp in self.copies(p)[:3]:
            cp.start()

    def forward(self, p):
        local, near, far, on = self.copies(p)
        far.wait_recv()
        on.start()

    def finish(self, p):
        local, near, far, on = self.copies(p)
        local.wait()
        near.wait_recv()
        on.wait_recv()
        near.wait_send()
        far.wait_send()
        on.wait_send()


class RowReduce:
    def __init__(self, at, send_a, recv_a, acc, p1, p2, sems, free, prior):
        self.free, self.prior = free, prior
        self.at, self.send_a, self.recv_a, self.acc, self.p1, self.p2 = at, send_a, recv_a, acc, p1, p2
        self.s_a, self.r_a, self.s_b, self.r_b, self.s_c, self.r_c, self.s_d, self.r_d = sems
        self.half = p1.shape[2]

    def copy_a(self, i):
        rows = rows_of(i)
        return remote(self.send_a.at[rows], self.recv_a.at[rows], self.s_a.at[i], self.r_a.at[i], self.at.sib)

    def copy_b(self, i):
        rows, c = rows_of(i), self.at.c
        return remote(self.p1.at[c, rows], self.p2.at[c, rows], self.s_b.at[i], self.r_b.at[i], self.at.par)

    def copy_c(self, i, side):
        rows = rows_of(i)
        return remote(self.p1.at[side, rows], self.p1.at[side, rows], self.s_c.at[i], self.r_c.at[i], self.at.sib)

    def copy_d(self, i, side):
        rows = rows_of(i)
        return remote(self.p2.at[side, rows], self.p2.at[side, rows], self.s_d.at[i], self.r_d.at[i], self.at.sib)

    def partial(self, i, terms):
        half = self.half

        def side(which):
            rows = pl.ds(pl.multiple_of(which * half, 128), half)
            return sum(nt(value, w[rows]) for value, w in terms)

        self.send_a[rows_of(i)] = side(self.at.o).astype(BF)
        self.copy_a(i).start()
        self.acc[lax.rem(i, 2)] = side(self.at.c)

    def swap(self, i):
        self.copy_a(i).wait_recv()
        self.p1[self.at.c, rows_of(i)] = (self.acc[lax.rem(i, 2)] + self.recv_a[rows_of(i)].astype(F32)).astype(BF)
        if self.prior is not None:
            pl.semaphore_wait(self.prior.free.at[i], 1)
        self.copy_b(i).start()
        self.copy_c(i, self.at.c).start()

    def share(self, i):
        self.copy_b(i).wait_recv()
        self.copy_d(i, self.at.c).start()

    def ready(self, i):
        self.copy_c(i, self.at.o).wait_recv()
        self.copy_d(i, self.at.o).wait_recv()

    def total(self, rs):
        p1, p2 = self.p1, self.p2
        return jnp.concatenate(
            [p1[0, rs].astype(F32) + p2[0, rs].astype(F32), p1[1, rs].astype(F32) + p2[1, rs].astype(F32)], axis=1
        )

    def drain(self, i):
        self.copy_a(i).wait_send()
        self.copy_b(i).wait_send()
        self.copy_c(i, self.at.c).wait_send()
        self.copy_d(i, self.at.c).wait_send()
        pl.semaphore_signal(self.free.at[i], inc=1, device_id=self.at.par, device_id_type=MESH)


def rows_of(i):
    return pl.ds(pl.multiple_of(i * CH, 16), CH)


def each(low, high, fn):
    def body(i, carry):
        fn(i)
        return carry

    lax.fori_loop(low, high, body, 0)


def sub_blocks(i, fn):
    each(0, CH // SUB, lambda k: fn(k, pl.ds(pl.multiple_of(i * CH + k * SUB, SUB), SUB), pl.ds(pl.multiple_of(k * SUB, SUB), SUB)))


NEG = -1e30


def nn(a, b):
    return jnp.dot(a, b, preferred_element_type=F32)


def lanes(shape):
    return lax.broadcasted_iota(jnp.int32, shape, len(shape) - 1)


def head_mask(value, which):
    lane = lanes(value.shape)
    keep = (lane < HEAD) if which == 0 else (lane >= HEAD)
    return jnp.where(keep, value, jnp.zeros_like(value))


def attend_step(i, q_ref, q_off, k_ref, k_off, v_ref, v_off, keys, valid, out_ref, lse_ref, heads, hook=None):
    rows = rows_of(i)
    lse = jnp.zeros((CH, 128), F32)
    for pair in range(heads // 2):
        qp = q_ref[rows, q_off + 128 * pair:q_off + 128 * (pair + 1)]
        kp = k_ref[:, k_off + 128 * pair:k_off + 128 * (pair + 1)]
        vp = v_ref[:, v_off + 128 * pair:v_off + 128 * (pair + 1)]
        mixed = []
        for which in range(2):
            s = nt(head_mask(qp, which), kp)
            s = jnp.where(lanes((1, keys)) < valid, s, NEG)
            top = jnp.max(s, axis=1, keepdims=True)
            e = jnp.exp(s - top)
            total = jnp.sum(e, axis=1, keepdims=True)
            mixed.append(nn(e.astype(BF), vp) / total)
            lse = jnp.where(lanes(lse.shape) == 2 * pair + which, top + jnp.log(total), lse)
        both = jnp.where(lanes(mixed[0].shape) < HEAD, mixed[0], mixed[1])
        out_ref[rows, 128 * pair:128 * (pair + 1)] = both.astype(BF)
        if hook is not None:
            hook(pair)
    lse_ref[rows] = lse


def attend_back(q_ref, q_off, k_ref, k_off, v_ref, v_off, keys, kblock, valid, do_ref, out_ref, lse_ref, lse_t, delta_t, dqt, emit_q, emit_kv, heads, hook=None):
    queries = q_ref.shape[0]
    lse_t[...] = lse_ref[...].T
    delta = jnp.zeros((queries, 128), F32)
    for pair in range(heads // 2):
        cols = slice(128 * pair, 128 * (pair + 1))
        prod = do_ref[:, cols].astype(F32) * out_ref[:, cols].astype(F32)
        for which in range(2):
            one = jnp.sum(head_mask(prod, which), axis=1, keepdims=True)
            delta = jnp.where(lanes(delta.shape) == 2 * pair + which, one, delta)
    delta_t[...] = delta.T
    for pair in range(heads // 2):
        qc = slice(q_off + 128 * pair, q_off + 128 * (pair + 1))
        kc = slice(k_off + 128 * pair, k_off + 128 * (pair + 1))
        vc = slice(v_off + 128 * pair, v_off + 128 * (pair + 1))
        oc = slice(128 * pair, 128 * (pair + 1))
        dqt[...] = jnp.zeros_like(dqt)

        def keys_step(j, carry):
            rows = pl.ds(pl.multiple_of(j * kblock, 16), kblock)
            kb, vb = k_ref[rows, kc], v_ref[rows, vc]
            dks, dvs = [], []
            for which in range(2):
                h = 2 * pair + which
                km = head_mask(kb, which)
                p = jnp.exp(nt(km, q_ref[:, qc]) - lse_t[h:h + 1])
                if keys != valid:
                    pos = j * kblock + lax.broadcasted_iota(jnp.int32, (kblock, 1), 0)
                    p = jnp.where(pos < valid, p, 0.0)
                dp = nt(head_mask(vb, which), do_ref[:, oc])
                ds = (p * (dp - delta_t[h:h + 1])).astype(BF)
                dvs.append(nn(p.astype(BF), do_ref[:, oc]))
                dks.append(nn(ds, q_ref[:, qc]))
                dqt[...] += nn(km.T, ds)
            low = lanes(dks[0].shape) < HEAD
            emit_kv(pair, rows, jnp.where(low, dks[0], dks[1]), jnp.where(low, dvs[0], dvs[1]))
            if hook is not None:
                hook(pair, j)
            return carry

        lax.fori_loop(0, keys // kblock, keys_step, 0)
        emit_q(pair, dqt[...].T)


def rotate_lanes(u, cos, sin_low, sin_high):
    width = u.shape[-1]
    return u * cos + pltpu.roll(u, width - ROT // 2, u.ndim - 1) * sin_low + pltpu.roll(u, ROT // 2, u.ndim - 1) * sin_high


def norm_back(tot, x, prior, gain, wide):
    xh, inv = row_stats(x, wide)
    e = tot * gain
    m1 = jnp.sum(e, axis=1, keepdims=True) * (1.0 / wide)
    m2 = jnp.sum(e * xh, axis=1, keepdims=True) * (1.0 / wide)
    return prior + inv * (e - m1 - xh * m2), tot * xh


def fold(ref, at, value):
    ref[at] += value[:8] + value[8:]


def local(src, dst, sem):
    return pltpu.make_async_copy(src, dst, sem)


def start_all(copies):
    for cp in copies:
        cp.start()


def wait_all(copies):
    for cp in copies:
        cp.wait()


def pad_into(dst, src, count):
    whole = count // 16 * 16
    dst[:whole] = src[:whole]
    left = count - whole
    rows = lax.broadcasted_iota(jnp.int32, (16, dst.shape[1]), 0)
    tile = jnp.zeros((16, dst.shape[1]), F32)
    for k in range(left):
        tile = jnp.where(rows == k, src[whole + k:whole + k + 1].astype(F32), tile)
    dst[whole:whole + 16] = tile.astype(dst.dtype)


def spread_tables(trig, cos, low, high):
    half = ROT // 2
    t = trig[...]
    lane = lanes(t.shape)
    place = lax.rem(lane, HEAD)
    first, second = place < half, jnp.logical_and(place >= half, place < ROT)
    both = lambda u: jnp.where(lane < HEAD, u, pltpu.roll(u, HEAD, 1))
    shift = lambda u: pltpu.roll(u, half, 1)
    back = lambda u: pltpu.roll(u, 128 - half, 1)
    c16, s16 = both(t), both(back(t))
    cos[...] = jnp.where(first, c16, jnp.where(second, shift(c16), 1.0))
    low[...] = jnp.where(first, -s16, 0.0)
    high[...] = jnp.where(second, shift(s16), 0.0)


def front_phase(k, gather):
    at, f, wide = k.at, k.f, k.wide
    dma = pltpu.SemaphoreType.DMA

    def run(latv, teachv, condv, latp, teachp, condp, smallv, trig, cos, low, high, x, h, qkv, a, lse, st, w, vec, ssem, lsem, sem):
        ins = [local(k.lat, latv, sem.at[0]), local(k.teach, teachv, sem.at[1]), local(k.cond, condv, sem.at[2]), local(k.trig, trig, sem.at[4])]
        start_all(ins)
        rowg = RowGather(at, [(latp, k.x0), (smallv, k.vecs), (condp, k.cond_full), (teachp, k.teach_full)], ssem, k.row_sem, lsem)
        ins[0].wait()
        pad_into(latp, latv, LEN)
        smallv[...] = jnp.zeros_like(smallv)
        for j in range(6):
            smallv[j, :] = k.small[j][...]
        at.enter(True, diagonal=True)
        rowg.start(0)
        rowg.start(1)
        gather.begin()
        wait_all(ins[1:3])
        pad_into(condp, condv, CLEN)
        pad_into(teachp, teachv, LEN)
        ins[3].wait()
        spread_tables(trig, cos, low, high)
        rowg.forward(0)
        rowg.forward(1)
        gather.advance(0)
        rowg.finish(0)
        rowg.finish(1)
        more = [local(k.x0, x, sem.at[0]), local(k.vecs, vec, sem.at[1])]
        start_all(more)
        rowg.start(2)
        rowg.start(3)
        wait_all(more)

        def norm(b):
            rows = pl.ds(pl.multiple_of(b * SUB, SUB), SUB)
            v = x[rows].astype(F32)
            mean = jnp.sum(v, axis=1, keepdims=True) * (1.0 / wide)
            xc = v - mean
            inv = lax.rsqrt(jnp.sum(xc * xc, axis=1, keepdims=True) * (1.0 / wide) + EPSILON)
            h[rows] = (xc * inv * vec[0:1] + vec[1:2]).astype(BF)
            st[rows] = jnp.where(lanes((SUB, 128)) == 2, mean, inv)

        each(0, TP // SUB, norm)
        outs = [local(h, k.h1, sem.at[2]), local(st, k.st1, sem.at[3])]
        start_all(outs)
        gather.advance(1)
        gather.advance(2)
        rowg.forward(2)
        fetch = lambda p: local(gather.pieces[p][1], w.at[p % 2], sem.at[4 + p % 2])
        gather.finish(0)
        fetch(0).start()
        for part in range(3):
            fetch(part).wait()
            if part < 2:
                if part == 1:
                    gather.pass_on(2, True)
                gather.finish(part + 1)
                fetch(part + 1).start()

            def project(i):
                rows = rows_of(i)
                c, lo, hi = cos[rows], low[rows], high[rows]
                res = nn(h[rows], w[part % 2])
                for pair in range(f // 128):
                    u = res[:, pair * 128:(pair + 1) * 128]
                    if part < 2:
                        u = rotate_lanes(u, c, lo, hi).astype(BF)
                    else:
                        u = u.astype(BF)
                    if part == 0:
                        u = u * HEAD ** (-0.5)
                    qkv[rows, part * f + pair * 128:part * f + (pair + 1) * 128] = u

            each(0, NCH, project)
        gather.advance(3, flush=False)

        def attend(i):
            def hook(pair):
                for p in range(4, k.front_pieces):
                    pl.when(i * 3 + pair == (p - 4) * 15 // (k.front_pieces - 4))(lambda: gather.advance(p))

            attend_step(i, qkv, 0, qkv, f, qkv, 2 * f, TP, LEN, a, lse, f // HEAD, hook)

        each(0, NCH, attend)
        last = [local(qkv, k.qkv, sem.at[0]), local(a, k.a, sem.at[1]), local(lse, k.lse1, sem.at[6])]
        start_all(last)
        rowg.forward(3)
        rowg.finish(2)
        rowg.finish(3)
        wait_all(outs + last)

    vm = pltpu.VMEM
    pl.run_scoped(
        run,
        latv=vm((LEN, f), BF), teachv=vm((LEN, f), BF), condv=vm((CLEN, f), BF), latp=vm((TP, f), BF), teachp=vm((TP, f), BF),
        condp=vm((CP, f), BF), smallv=vm((8, f), F32), trig=vm((TP, 128), F32), cos=vm((TP, 128), F32), low=vm((TP, 128), F32),
        high=vm((TP, 128), F32), x=vm((TP, wide), BF), h=vm((TP, wide), BF), qkv=vm((TP, 3 * f), BF), a=vm((TP, f), BF),
        lse=vm((TP, 128), F32), st=vm((TP, 128), F32), w=vm((2, wide, f), BF), vec=vm((8, wide), F32),
        ssem=dma((4, 3)), lsem=dma((4,)), sem=dma((7,)),
    )


def mid_phase(k, gather, first, second):
    at, f, wide = k.at, k.f, k.wide
    dma, vm = pltpu.SemaphoreType.DMA, pltpu.VMEM
    slots = list(range(k.front_pieces, k.mid_pieces))

    def run(a, x0, x, low, wo, wq, wk, wv, wc, cq, ckv, c, lse, cond, vec, acc, sem, osem, esem):
        first.acc, second.acc = acc, acc
        for p in range(3, 8):
            gather.finish(p)
        loads = [
            local(src, dst, sem.at[j])
            for j, (src, dst) in enumerate(
                ((k.a, a), (k.full[3], wo), (k.full[5], wk), (k.full[6], wv), (k.cond_full, cond), (k.x0, x0), (k.full[4], wq), (k.full[7], wc), (k.vecs, vec))
            )
        ]
        start_all(loads)
        wait_all(loads[:2])

        def project(i):
            first.partial(i, [(a[rows_of(i)], wo)])
            pl.when(i > 0)(lambda: first.swap(i - 1))

        each(0, NCH, project)
        first.swap(NCH - 1)
        wait_all(loads[2:])
        ckv[:, :f] = nn(cond[...], wk[...]).astype(BF)
        ckv[:, f:] = nn(cond[...], wv[...]).astype(BF)

        def outs(i, main, lowest, which):
            return [
                local(x.at[rows_of(i)], main.at[rows_of(i)], osem.at[which, 2 * i]),
                local(low.at[rows_of(i)], lowest.at[rows_of(i)], osem.at[which, 2 * i + 1]),
            ]

        def hook(slot):
            for j, p in enumerate(slots):
                pl.when(slot == j * 2 * NCH // len(slots))(lambda: gather.advance(p))

        def cross(i):
            first.ready(i)

            def block(b, rs, ls):
                v = x0[rs].astype(F32) + first.total(rs)
                x[rs] = v
                low[rs] = (row_stats(v, wide)[0] * vec[2:3] + vec[3:4]).astype(BF)

            sub_blocks(i, block)
            start_all(outs(i, k.x1, k.h2, 0))
            rows = rows_of(i)
            cq[rows] = nn(low[rows], wq[...]).astype(BF) * HEAD ** (-0.5)
            attend_step(i, cq, 0, ckv, 0, ckv, f, CP, CLEN, c, lse, f // HEAD)
            first.drain(i)
            second.partial(i, [(c[rows], wc)])
            pl.when(i > 0)(lambda: second.swap(i - 1))

        def step(i):
            first.share(i)
            pl.when(i > 0)(lambda: cross(i - 1))
            hook(i)

        each(0, NCH, step)
        cross(NCH - 1)
        second.swap(NCH - 1)
        ends = [local(cq, k.cq, esem.at[0]), local(ckv, k.ckv, esem.at[1]), local(c, k.c, esem.at[2]), local(lse, k.lse2, esem.at[3])]
        start_all(ends)

        def last(i):
            second.ready(i)
            wait_all(outs(i, k.x1, k.h2, 0))

            def block(b, rs, ls):
                v = x[rs] + second.total(rs)
                x[rs] = v
                low[rs] = (row_stats(v, wide)[0] * vec[4:5] + vec[5:6]).astype(BF)

            sub_blocks(i, block)
            start_all(outs(i, k.x2, k.h3, 1))

        def step_two(i):
            second.share(i)
            pl.when(i > 0)(lambda: last(i - 1))
            hook(NCH + i)

        each(0, NCH, step_two)
        last(NCH - 1)

        def end(i):
            second.drain(i)
            wait_all(outs(i, k.x2, k.h3, 1))

        each(0, NCH, end)
        wait_all(ends)

    weight = lambda: vm((wide, f), BF)
    pl.run_scoped(
        run,
        a=vm((TP, f), BF), x0=vm((TP, wide), BF), x=vm((TP, wide), F32), low=vm((TP, wide), BF), wo=weight(), wq=weight(), wk=weight(),
        wv=weight(), wc=weight(), cq=vm((TP, f), BF), ckv=vm((CP, 2 * f), BF), c=vm((TP, f), BF), lse=vm((TP, 128), F32),
        cond=vm((CP, wide), BF), vec=vm((8, wide), F32), acc=vm((2, CH, wide // 2), F32), sem=dma((9,)), osem=dma((2, 2 * NCH)), esem=dma((4,)),
    )


def mlp_phase(k, gather, red, nxt, h, hid, sg, tt, dm):
    at, f, wide = k.at, k.f, k.wide
    dma, vm = pltpu.SemaphoreType.DMA, pltpu.VMEM
    parts = k.parts
    col = lambda j: slice(j * f, (j + 1) * f)
    own = pl.ds(pl.multiple_of(at.r * f, 128), f)

    def run(wg, wu, wd, acc, xbuf, tbuf, sq, sem, wsem, xsem, tsem, rsem, ysem):
        red.acc, nxt.acc = acc, acc
        hcp = local(k.h3, h, sem.at[0])
        hcp.start()
        sq[...] = jnp.zeros_like(sq)

        def slot_in(i):
            s = lax.rem(i, 2)
            return [local(k.x2.at[rows_of(i)], xbuf.at[s], xsem.at[s]), local(k.teach_full.at[rows_of(i)], tbuf.at[s], tsem.at[s])]

        for i in range(2):
            start_all(slot_in(i))
        pending = list(range(k.mid_pieces, len(gather.pieces)))

        def fetch(p):
            q, j = (p - 8) % 2 if p < 16 else 2, (p - 8) // 2 if p < 16 else p - 16
            return local(gather.pieces[p][1], (wg, wu, wd)[q].at[:, col(j)], wsem.at[p - 8])

        done = [8]

        def bring(upto):
            while done[0] <= upto:
                while pending and pending[0] <= done[0] + 1:
                    gather.advance(pending.pop(0))
                gather.finish(done[0])
                fetch(done[0]).start()
                done[0] += 1

        bring(9)
        hcp.wait()
        for j in range(parts):
            if j < parts - 1:
                bring(11 + 2 * j)
            fetch(8 + 2 * j).wait()
            fetch(9 + 2 * j).wait()

            def hidden(i):
                rows = rows_of(i)
                gate = nn(h[rows], wg[:, col(j)])
                up = nn(h[rows], wu[:, col(j)])
                sig = jax.nn.sigmoid(gate)
                act = gate * sig
                hid[rows, col(j)] = (act * up).astype(BF)
                sg[rows, col(j)] = act.astype(BF)
                tt[rows, col(j)] = (up * sig * (1.0 + gate * (1.0 - sig))).astype(BF)

            each(0, NCH, hidden)
            if pending:
                gather.advance(pending.pop(0))
        bring(15 + parts)
        for j in range(parts):
            fetch(16 + j).wait()

        def project(i):
            red.partial(i, [(hid[rows_of(i)], wd)])
            pl.when(i > 0)(lambda: red.swap(i - 1))

        each(0, NCH, project)
        red.swap(NCH - 1)

        def outs_of(i):
            s = lax.rem(i, 2)
            return [local(xbuf.at[s], k.res.at[rows_of(i)], rsem.at[s]), local(tbuf.at[s, :, own], k.y.at[rows_of(i)], ysem.at[s])]

        def finish(i):
            s = lax.rem(i, 2)
            red.ready(i)

            @pl.when(i >= 1)
            def _():
                wait_all(outs_of(i - 1))
                pl.when(i < NCH - 1)(lambda: start_all(slot_in(i + 1)))

            wait_all(slot_in(i))

            def block(b, rs, ls):
                y = xbuf[s, ls] + red.total(rs)
                pos = i * CH + b * SUB + lax.broadcasted_iota(jnp.int32, (SUB, wide), 0)
                res = jnp.where(pos < LEN, y - tbuf[s, ls].astype(F32), 0.0)
                xbuf[s, ls] = res
                dm[rs] = res.astype(BF)
                tbuf[s, ls] = y.astype(BF)
                sq_ = res * res
                sq[...] += sq_[:8] + sq_[8:]

            sub_blocks(i, block)
            start_all(outs_of(i))
            rows = rows_of(i)
            for j in range(parts):
                dh = nn(dm[rows], wd[:, col(j)])
                tt[rows, col(j)] = (dh * tt[rows, col(j)].astype(F32)).astype(BF)
                sg[rows, col(j)] = (dh * sg[rows, col(j)].astype(F32)).astype(BF)
            red.drain(i)
            nxt.partial(i, [(tt[rows], wg), (sg[rows], wu)])
            pl.when(i > 0)(lambda: nxt.swap(i - 1))

        def step(i):
            red.share(i)
            pl.when(i > 0)(lambda: finish(i - 1))

        each(0, NCH, step)
        finish(NCH - 1)
        nxt.swap(NCH - 1)
        scp = local(sq, k.squares, sem.at[0])
        scp.start()
        wait_all(outs_of(NCH - 1))
        scp.wait()

    weight = lambda: vm((wide, parts * f), BF)
    pl.run_scoped(
        run,
        wg=weight(), wu=weight(), wd=weight(), acc=vm((2, CH, wide // 2), F32), xbuf=vm((2, CH, wide), F32), tbuf=vm((2, CH, wide), BF),
        sq=vm((8, wide), F32), sem=dma((1,)), wsem=dma((3 * parts,)), xsem=dma((2,)), tsem=dma((2,)),
        rsem=dma((2,)), ysem=dma((2,)),
    )


class Grads:
    def __init__(self, part, stage, sem, f):
        self.part, self.stage, self.sem, self.f = part, stage, sem, f

    def copy(self, p):
        return local(self.stage, self.part.at[:, p * self.f:(p + 1) * self.f], self.sem.at[p % 2])

    def make(self, p, left, right):
        wide = left.shape[1]

        def one(j):
            cols = pl.ds(pl.multiple_of(j * 512, 128), 512)
            self.stage[cols] = tn(left[:, cols], right()).astype(BF)

        each(0, wide // 512, one)
        self.copy(p).start()


def mid_back_phase(k, scatter, first, second, h, hid, sg, tt, dm):
    at, f, wide = k.at, k.f, k.wide
    dma, vm = pltpu.SemaphoreType.DMA, pltpu.VMEM

    def run(g, low, xs, wc, wq, dkv, dc, cq, ckv, c, lse, dcq, sums, vec, acc, stage, sem, xsem, osem, gsem):
        second.acc = acc
        grads = Grads(k.part, stage, gsem, f)
        rest = [
            local(src, dst, sem.at[j])
            for j, (src, dst) in enumerate(((k.res, g), (k.full[7], wc), (k.full[4], wq), (k.cq, cq), (k.ckv, ckv), (k.c, c), (k.lse2, lse), (k.vecs, vec)))
        ]
        start_all(rest)

        def stream(src, i, s):
            return local(src.at[rows_of(i)], xs.at[s], xsem.at[s])

        stream(k.x2, 0, 0).start()
        stream(k.x2, 1, 1).start()
        sums[...] = jnp.zeros_like(sums)
        dkv[...] = jnp.zeros_like(dkv)

        def make(p):
            q, j = p // 4, p % 4
            left, right = ((h, tt), (h, sg), (dm, hid))[q]
            grads.make(p, left, lambda: right[:, j * f:(j + 1) * f])

        for p in range(2):
            make(p)
            grads.copy(p).wait()
            scatter.start(p)
        wait_all(rest)

        def hook(slot):
            for p in range(2, 12):
                @pl.when(slot == p - 2)
                def _():
                    make(p)
                    grads.copy(p).wait()
                    if p < scatter.ahead:
                        scatter.start(p)

            for p in range(k.back_pieces):
                pl.when(slot == p * 2 * NCH // k.back_pieces + 1)(lambda: scatter.advance(p))

        def low_out(i, which):
            return local(low.at[lax.rem(i + which * NCH, 2)], (k.dco, k.do)[which].at[rows_of(i)], osem.at[which, i])

        def g_out(i):
            return local(g.at[rows_of(i)], k.g1.at[rows_of(i)], osem.at[2, i])

        valid = lambda: lax.broadcasted_iota(jnp.int32, (CP, 1), 0) < CLEN

        def cross(i):
            first.ready(i)
            s = lax.rem(i, 2)
            stream(k.x2, i, s).wait()
            pl.when(i >= 2)(lambda: low_out(i - 2, 0).wait())

            def block(b, rs, ls):
                tot = first.total(rs)
                new, dx = norm_back(tot, xs[s, ls], g[rs], vec[4:5], wide)
                g[rs] = new
                low[s, ls] = new.astype(BF)
                fold(sums, 0, dx)
                fold(sums, 1, tot)

            sub_blocks(i, block)
            pl.when(i < NCH - 2)(lambda: stream(k.x2, i + 2, s).start())
            pl.when(i >= NCH - 2)(lambda: stream(k.x1, i + 2 - NCH, s).start())
            low_out(i, 0).start()
            rows = rows_of(i)
            dc[...] = nn(low[s], wc[...]).astype(BF)
            lse_t = lse[rows].T
            delta = jnp.zeros((CH, 128), F32)
            for pair in range(f // 128):
                cols = slice(128 * pair, 128 * (pair + 1))
                prod = dc[:, cols].astype(F32) * c[rows, cols].astype(F32)
                for which in range(2):
                    one = jnp.sum(head_mask(prod, which), axis=1, keepdims=True)
                    delta = jnp.where(lanes(delta.shape) == 2 * pair + which, one, delta)
            delta_t = delta.T
            for pair in range(f // 128):
                cols = slice(128 * pair, 128 * (pair + 1))
                vcols = slice(f + 128 * pair, f + 128 * (pair + 1))
                kb, vb, qc, doc = ckv[:, cols], ckv[:, vcols], cq[rows, cols], dc[:, cols]
                dks, dvs, dqt = [], [], None
                for which in range(2):
                    hd = 2 * pair + which
                    km = head_mask(kb, which)
                    p = jnp.where(valid(), jnp.exp(nt(km, qc) - lse_t[hd:hd + 1]), 0.0)
                    dp = nt(head_mask(vb, which), doc)
                    ds = (p * (dp - delta_t[hd:hd + 1])).astype(BF)
                    dvs.append(nn(p.astype(BF), doc))
                    dks.append(nn(ds, qc))
                    part = nn(km.T, ds)
                    dqt = part if dqt is None else dqt + part
                left = lanes(dks[0].shape) < HEAD
                dkv[:, cols] += jnp.where(left, dks[0], dks[1])
                dkv[:, vcols] += jnp.where(left, dvs[0], dvs[1])
                dcq[rows, cols] = (dqt.T * HEAD ** (-0.5)).astype(BF)
            first.drain(i)
            second.partial(i, [(dcq[rows], wq)])
            pl.when(i > 0)(lambda: second.swap(i - 1))

        def step(i):
            first.share(i)
            pl.when(i > 0)(lambda: cross(i - 1))
            hook(i)

        each(0, NCH, step)
        cross(NCH - 1)
        second.swap(NCH - 1)
        ckv[...] = dkv[...].astype(BF)

        def last(i):
            second.ready(i)
            s = lax.rem(i + NCH, 2)
            stream(k.x1, i, s).wait()
            pl.when(i < 2)(lambda: low_out(NCH - 2 + i, 0).wait())
            pl.when(i >= 2)(lambda: low_out(i - 2, 1).wait())

            def block(b, rs, ls):
                tot = second.total(rs)
                new, dx = norm_back(tot, xs[s, ls], g[rs], vec[2:3], wide)
                g[rs] = new
                low[s, ls] = new.astype(BF)
                fold(sums, 2, dx)
                fold(sums, 3, tot)

            sub_blocks(i, block)
            pl.when(i < NCH - 2)(lambda: stream(k.x1, i + 2, s).start())
            low_out(i, 1).start()
            g_out(i).start()

        def step_two(i):
            second.share(i)
            pl.when(i > 0)(lambda: last(i - 1))
            hook(NCH + i)

        each(0, NCH, step_two)
        last(NCH - 1)
        ends = [local(dcq, k.dcq, sem.at[0]), local(ckv, k.dckv, sem.at[1]), local(sums, k.sums, sem.at[2])]
        start_all(ends)

        def end(i):
            second.drain(i)
            pl.when(i >= NCH - 2)(lambda: low_out(i, 1).wait())
            g_out(i).wait()

        each(0, NCH, end)
        wait_all(ends)

    pl.run_scoped(
        run,
        g=vm((TP, wide), F32), low=vm((2, CH, wide), BF), xs=vm((2, CH, wide), F32), wc=vm((wide, f), BF), wq=vm((wide, f), BF),
        dkv=vm((CP, 2 * f), F32), dc=vm((CH, f), BF), cq=vm((TP, f), BF), ckv=vm((CP, 2 * f), BF), c=vm((TP, f), BF),
        lse=vm((TP, 128), F32), dcq=vm((TP, f), BF), sums=vm((4, 8, wide), F32), vec=vm((8, wide), F32), acc=vm((2, CH, wide // 2), F32),
        stage=vm((wide, f), BF), sem=dma((8,)), xsem=dma((2,)), osem=dma((3, NCH)), gsem=dma((2,)),
    )


def end_phase(k, scatter):
    at, f, wide = k.at, k.f, k.wide
    dma, vm = pltpu.SemaphoreType.DMA, pltpu.VMEM
    r, c_, o = at.r, at.c, at.o
    own = pl.ds(pl.multiple_of(r * f, 128), f)
    send_a, recv_a = k.send_a, k.recv_a
    send_b, recv_b = k.p1.at[0, :, :f], k.p2.at[0, :, :f]

    def run(xa, xb, wt, w1, da, dqkv, lse_t, delta_t, dqt, stage, xo, go, g1, tot, acc, st, back, st_t, cpart, qkv, a, lse, trig,
            cos, low, high, c, dcq, dckv, cond, sums, sq, vr, vb, lat, gc, sem, gsem, s_c, s_x, s_v):
        grads = Grads(k.part, stage, gsem, f)
        names = {}

        def load(name, src, dst):
            names[name] = local(src, dst, sem.at[len(names)])
            names[name].start()

        load("do", k.do, xa)
        load("wo", k.full[3], wt)
        load("a", k.a, a)
        load("qkv", k.qkv, qkv)
        load("lse", k.lse1, lse)
        load("trig", k.trig, trig)
        load("h2", k.h2, xb)
        load("c", k.c, c)
        load("dcq", k.dcq, dcq)
        load("dckv", k.dckv, dckv)
        load("cond", k.cond_full, cond)
        rest = ["st", "xo", "go", "g1", "sums", "sq"]
        for name, src, dst in (
            ("st", k.st1, st), ("xo", k.x0.at[:, own], xo), ("go", k.vecs.at[:, own], go), ("g1", k.g1.at[:, own], g1),
            ("sums", k.sums.at[:, :, own], sums), ("sq", k.squares, sq),
        ):
            load(name, src, dst)
        for j in range(3):
            load(f"w{j}", k.full[j], w1.at[:, j * f:(j + 1) * f])
            rest.append(f"w{j}")

        def ready(*which):
            for name in which:
                names[name].wait()

        def make(p, left, right):
            grads.make(p, left, right)
            grads.copy(p).wait()

        ready("do", "wo", "a")

        def project_da(i):
            da[rows_of(i)] = nn(xa[rows_of(i)], wt[...]).astype(BF)

        each(0, NCH, project_da)
        make(12, xa, lambda: a[...])
        again = local(k.dco, xa, sem.at[0])
        again.start()
        wck_cp = local(k.full[5], wt, sem.at[1])
        wck_cp.start()
        nxt = k.back_pieces
        scatter.advance(nxt)
        nxt = nxt + 1
        ready("h2", "c", "dcq", "dckv", "cond")
        again.wait()
        make(13, xa, lambda: c[...])
        make(14, xb, lambda: dcq[...])
        h1_cp = local(k.h1, xb, sem.at[0])
        h1_cp.start()
        make(15, cond, lambda: dckv[:, :f])
        make(16, cond, lambda: dckv[:, f:])
        ready("qkv", "lse", "trig")
        spread_tables(trig, cos, low, high)

        def emit_q(pair, dq):
            dqkv[:, 128 * pair:128 * (pair + 1)] = rotate_lanes(dq * HEAD ** (-0.5), cos[...], -low[...], -high[...]).astype(BF)

        def emit_kv(pair, rows, dk, dv):
            dqkv[rows, f + 128 * pair:f + 128 * (pair + 1)] = rotate_lanes(dk, cos[rows], -low[rows], -high[rows]).astype(BF)
            dqkv[rows, 2 * f + 128 * pair:2 * f + 128 * (pair + 1)] = dv.astype(BF)


        def hook(pair, j):
            for step, spot in enumerate(k.end_spots):
                if spot[0] == pair:
                    pl.when(j == spot[1])(lambda: scatter.advance(nxt + step))

        attend_back(qkv, 0, qkv, f, qkv, 2 * f, TP, CH, LEN, da, a, lse, lse_t, delta_t, dqt, emit_q, emit_kv, f // HEAD, hook)
        nxt = nxt + len(k.end_spots)

        h1_cp.wait()
        for j in range(3):
            make(17 + j, xb, lambda: dqkv[:, j * f:(j + 1) * f])
        scatter.advance(nxt)

        wck_cp.wait()
        for j in range(4):
            cpart[j] = nt(dckv[:, :f], wt[j * f:(j + 1) * f])
        wcv_cp = local(k.full[6], wt, sem.at[1])
        wcv_cp.start()
        scatter.advance(nxt + 1)
        wcv_cp.wait()
        crecv = k.crecv
        for j in range(4):
            crecv[j] = (cpart[j] + nt(dckv[:, f:], wt[j * f:(j + 1) * f])).astype(BF)
        peers = (at.sib, at.par, at.diag)
        cond_cps = [remote(crecv.at[peers[j][0]], crecv.at[4 + j], s_c.at[j], k.r_c.at[j], peers[j]) for j in range(3)]
        start_all(cond_cps)
        ready(*rest)

        wblock = lambda j: w1[pl.ds(pl.multiple_of(j * f, 128), f)]

        def copy_a(i):
            return remote(send_a.at[rows_of(i)], recv_a.at[rows_of(i)], k.e_sa.at[i], k.e_ra.at[i], at.sib)

        def copy_b(i):
            return remote(send_b.at[rows_of(i)], recv_b.at[rows_of(i)], k.e_sb.at[i], k.e_rb.at[i], at.par)

        def swap(i):
            copy_a(i).wait_recv()
            both = acc[lax.rem(i, 2)] + recv_a[rows_of(i)].astype(F32)
            left, right = both[:, :f], both[:, f:]
            tot[rows_of(i)] = jnp.where(at.xi == 0, left, right)
            send_b[rows_of(i)] = jnp.where(at.xi == 0, right, left).astype(BF)
            pl.semaphore_wait(k.last_sum.free.at[i], 1)
            copy_b(i).start()

        def project(i):
            y = dqkv[rows_of(i)]
            send_a[rows_of(i), :f] = nt(y, wblock(o)).astype(BF)
            send_a[rows_of(i), f:] = nt(y, wblock(2 + o)).astype(BF)
            copy_a(i).start()
            acc[lax.rem(i, 2), :, :f] = nt(y, wblock(c_))
            acc[lax.rem(i, 2), :, f:] = nt(y, wblock(2 + c_))
            pl.when(i > 0)(lambda: swap(i - 1))

        each(0, NCH, project)
        swap(NCH - 1)
        vr[...] = jnp.zeros_like(vr)
        scatter.advance(nxt + 2)

        def sums_of(i):
            copy_b(i).wait_recv()

            def block(b, rs, ls):
                t = tot[rs] + recv_b[rs].astype(F32)
                tot[rs] = t
                own_st = st[rs]
                mean, inv = own_st[:, 2:3], own_st[:, 3:4]
                xh = (xo[rs].astype(F32) - mean) * inv
                e = t * go[0:1]
                lane = lanes((SUB, 128))
                first = jnp.sum(e, axis=1, keepdims=True)
                cross = jnp.sum(e * xh, axis=1, keepdims=True)
                back[rs] = jnp.where(lane == 0, first, cross)
                fold(vr, 0, t * xh)
                fold(vr, 1, t)

            sub_blocks(i, block)

        each(0, NCH, sums_of)
        sx = k.sx
        st_t[...] = back[...].T
        sx[0] = st_t[:8]
        stat_cps = [remote(sx.at[0], sx.at[1 + j], s_x.at[j], k.r_x.at[j], peers[j]) for j in range(3)]
        start_all(stat_cps)
        total = lambda x: jnp.sum(x, axis=0, keepdims=True)
        error = jnp.sum(total(sq[...]), axis=1, keepdims=True)
        vb[0:1] = total(vr[0])
        vb[1:2] = total(vr[1])
        vb[2:3] = total(sums[2])
        vb[3:4] = total(sums[3])
        vb[4:5] = total(sums[0])
        vb[5:6] = total(sums[1])
        vb[6:8] = jnp.broadcast_to(error, (2, f))
        vz = k.vz
        pair_cp = remote(vb, vz.at[at.outer], s_v.at[at.outer], k.r_v.at[at.outer], at.ypar)
        pair_cp.start()
        scatter.advance(nxt + 3)
        for cp in cond_cps:
            cp.wait_recv()
        gc[...] = (crecv[r].astype(F32) + crecv[4].astype(F32) + crecv[5].astype(F32) + crecv[6].astype(F32)).astype(BF)
        for cp in stat_cps:
            cp.wait_recv()
        st_t[:8] = sx[0] + sx[1] + sx[2] + sx[3]
        back[...] = st_t[...].T
        pair_cp.wait()
        vz[at.zo] = vb[...] + vz[at.outer]

        def vec_out(step):
            return remote(vz.at[at.zo], vz.at[at.zo], s_v.at[step], k.r_v.at[at.zo], (r, 2 * at.zpeer(step) + at.yi))

        each(1, at.outer, lambda step: vec_out(step).start())

        def last(i):
            def block(b, rs, ls):
                e = tot[rs] * go[0:1]
                row_sums, own_st = back[rs], st[rs]
                first, cross = row_sums[:, 0:1] * (1.0 / wide), row_sums[:, 1:2] * (1.0 / wide)
                mean, inv = own_st[:, 2:3], own_st[:, 3:4]
                xh = (xo[rs].astype(F32) - mean) * inv
                lat[rs] = (g1[rs] + inv * (e - first - xh * cross)).astype(BF)

            sub_blocks(i, block)

        each(0, NCH, last)
        outs = [local(lat, k.glat, sem.at[0]), local(gc, k.gcond, sem.at[1])]
        start_all(outs)
        for p in range(nxt + 4, len(scatter.pieces)):
            scatter.advance(p)
        vb[...] = vz[at.zo]

        def vec_in(step):
            zs = at.zpeer(at.outer - step)
            remote(vz.at[zs], vz.at[zs], s_v.at[step], k.r_v.at[zs], at.ypar).wait_recv()
            vb[...] += vz[zs]

        each(1, at.outer, vec_in)
        vec_cp = local(vb, k.vec, sem.at[2])
        vec_cp.start()
        each(1, at.outer, lambda step: vec_out(step).wait_send())
        scatter.complete()
        for cp in stat_cps + cond_cps:
            cp.wait_send()

        def drain(i):
            copy_a(i).wait_send()
            copy_b(i).wait_send()

        each(0, NCH, drain)
        wait_all(outs + [vec_cp])

    tab = lambda: vm((TP, 128), F32)
    flip = lambda: vm((128, TP), F32)
    pl.run_scoped(
        run,
        xa=vm((TP, wide), BF), xb=vm((TP, wide), BF), wt=vm((wide, f), BF), w1=vm((wide, 3 * f), BF), da=vm((TP, f), BF),
        dqkv=vm((TP, 3 * f), BF), lse_t=flip(), delta_t=flip(), dqt=flip(), stage=vm((wide, f), BF), xo=vm((TP, f), BF),
        go=vm((8, f), F32), g1=vm((TP, f), F32), tot=vm((TP, f), F32), acc=vm((2, CH, 2 * f), F32), st=tab(), back=tab(), st_t=flip(),
        cpart=vm((4, CP, f), F32), qkv=vm((TP, 3 * f), BF), a=vm((TP, f), BF), lse=tab(), trig=tab(), cos=tab(), low=tab(), high=tab(),
        c=vm((TP, f), BF), dcq=vm((TP, f), BF), dckv=vm((CP, 2 * f), BF), cond=vm((CP, wide), BF), sums=vm((4, 8, f), F32),
        sq=vm((8, wide), F32), vr=vm((2, 8, f), F32), vb=vm((8, f), F32), lat=vm((TP, f), BF), gc=vm((CP, f), BF),
        sem=dma((24,)), gsem=dma((2,)), s_c=dma((3,)), s_x=dma((3,)), s_v=dma((k.outer + 1,)),
    )


class Names:
    pass


def layer_kernel(n, f, pieces, front_pieces, mid_pieces, back_pieces, ahead, s_ahead, slots, *refs):
    refs = list(refs)
    take = lambda count: [refs.pop(0) for _ in range(count)]
    k = Names()
    k.at, k.f, k.wide, k.outer = Place(n), f, 4 * f, n // 2
    k.front_pieces, k.mid_pieces, k.back_pieces = front_pieces, mid_pieces, back_pieces
    k.end_spots = ((0, 2), (1, 0), (1, 3), (2, 2))
    k.lat, k.teach, k.cond, k.trig = take(4)
    k.small = take(6)
    shards = take(11)
    k.y, k.glat, k.gcond, k.vec = take(4)
    gate_out, up_out, down_out = take(3)
    square_out = take(8)
    k.full = take(8)
    mlp_full = take(3)
    k.x0, k.vecs, k.cond_full, k.teach_full, k.h1, k.st1, k.qkv, k.a, k.lse1 = take(9)
    k.x1, k.h2, k.cq, k.ckv, k.c, k.lse2, k.x2, k.h3 = take(8)
    k.res, k.squares, k.g1, k.dco, k.do, k.dcq, k.dckv, k.sums, k.part = take(9)
    k.send_a, k.recv_a, k.p1, k.p2, k.sx, k.crecv, k.vz = take(7)
    sems = [take(8) for _ in range(5)]
    free = take(5)
    k.e_sa, k.e_ra, k.e_sb, k.e_rb, k.row_sem, k.r_c, k.r_x, k.r_v = take(8)
    gather_sem = take(3)
    bufs, scatter_sem = take(5), take(8)
    k.parts = shards[8].shape[1] // f
    col = lambda j: slice(j * f, (j + 1) * f)
    made = [(shards[j], k.full[j]) for j in range(8)]
    for j in range(k.parts):
        for q in range(2):
            made.append((shards[8 + q].at[:, col(j)], mlp_full[q].at[:, col(j)]))
    made += [(shards[10].at[:, col(j)], mlp_full[2].at[:, col(j)]) for j in range(k.parts)]
    gather = ColGather(k.at, made, ahead, *gather_sem)
    sums = []
    for q, out in enumerate((gate_out, up_out, down_out)):
        sums += [(k.part.at[:, col(q * k.parts + j)], out.at[:, col(j)]) for j in range(k.parts)]
    sums += [(k.part.at[:, col(3 * k.parts + j)], square_out[j]) for j in range(8)]
    scatter = ColScatter(k.at, sums, s_ahead, slots, bufs, scatter_sem)
    red = [None]
    for j in range(5):
        red.append(RowReduce(k.at, k.send_a, k.recv_a, None, k.p1, k.p2, sems[j], free[j], red[j]))
    red = red[1:]
    k.last_sum = red[4]
    front_phase(k, gather)
    mid_phase(k, gather, red[0], red[1])
    full = pltpu.VMEM((TP, k.wide), BF)

    def back(h, hid, sg, tt, dm):
        mlp_phase(k, gather, red[2], red[3], h, hid, sg, tt, dm)
        mid_back_phase(k, scatter, red[3], red[4], h, hid, sg, tt, dm)

    pl.run_scoped(back, h=full, hid=full, sg=full, tt=full, dm=full)
    end_phase(k, scatter)


def layer_call(n, lat, teach, cond, trig, small, shards, front_pieces=12, mid_pieces=19, back_pieces=9, ahead=4, s_ahead=3, slots=5):
    f = lat.shape[1]
    wide, size, outer = 4 * f, shards[0].shape[0], n // 2
    ffl = shards[8].shape[1]
    sd = jax.ShapeDtypeStruct
    dma = pltpu.SemaphoreType.DMA
    vm = pltpu.VMEM
    half = wide // 2
    results = [sd((TP, f), BF), sd((TP, f), BF), sd((CP, f), BF), sd((8, f), F32)]
    results += [sd((size, ffl), F32)] * 3 + [sd((size, f), F32)] * 8
    between = [sd((wide, f), BF)] * 8 + [sd((wide, ffl), BF)] * 3
    rows, rows32 = sd((TP, wide), BF), sd((TP, wide), F32)
    between += [rows, sd((8, wide), F32), sd((CP, wide), BF), rows, rows, sd((TP, 128), F32), sd((TP, 3 * f), BF), sd((TP, f), BF), sd((TP, 128), F32)]
    between += [rows32, rows, sd((TP, f), BF), sd((CP, 2 * f), BF), sd((TP, f), BF), sd((TP, 128), F32), rows32, rows]
    between += [rows32, sd((8, wide), F32), rows32, rows, rows, sd((TP, f), BF), sd((CP, 2 * f), BF), sd((4, 8, wide), F32), sd((wide, 3 * ffl + 8 * f), BF)]
    pieces = 8 + 3 * ffl // f
    scratch = [
        vm((TP, half), BF), vm((TP, half), BF), vm((2, TP, half), BF), vm((2, TP, half), BF),
        vm((4, 8, TP), F32), vm((7, CP, f), BF), vm((outer + 1, 8, f), F32),
    ] + [dma((NCH,))] * 40 + [pltpu.SemaphoreType.REGULAR((NCH,))] * 5 + [dma((NCH,))] * 4 + [dma((4, 3)), dma((3,)), dma((3,)), dma((outer + 1,))]
    bufs, sems = scatter_scratch(pieces, slots, n, f, wide)
    scratch += gather_sems(pieces, n) + bufs + sems
    out = pl.pallas_call(
        functools.partial(layer_kernel, n, f, pieces, front_pieces, mid_pieces, back_pieces, ahead, s_ahead, slots),
        out_shape=results + between,
        in_specs=[hspec()] * 4 + [vspec()] * 6 + [hspec()] * 11,
        out_specs=[hspec()] * (len(results) + len(between)),
        scratch_shapes=scratch,
        compiler_params=pltpu.CompilerParams(collective_id=0, has_side_effects=True, vmem_limit_bytes=66_900_000),
        name="layer",
    )(lat, teach, cond, trig, *small, *shards)
    return out[:len(results)]


def emit_kernel(n, scale, *refs):
    refs = list(refs)
    take = lambda count: [refs.pop(0) for _ in range(count)]
    moved, grads = take(4), take(11)
    y_out, lat_out, cond_out, vec_out = take(4)
    grad_outs = take(11)
    y, lat, cond, vec, sem, vsem = take(6)
    held = take(11)
    cps = [local(src, dst, sem.at[j]) for j, (src, dst) in enumerate(zip(grads, held))]
    out_cps = [local(src, dst, sem.at[j]) for j, (src, dst) in enumerate(zip(held, grad_outs))]
    ins = [local(src, dst, vsem.at[j]) for j, (src, dst) in enumerate(zip(moved, (y, lat, cond, vec)))]
    start_all(cps + ins)
    for cp, out in zip(cps, out_cps):
        cp.wait()
        out.start()
    wait_all(ins)
    y_out[...] = y[:y_out.shape[0]]
    lat_out[...] = lat[:lat_out.shape[0]]
    cond_out[...] = cond[:cond_out.shape[0]]
    width = vec_out.shape[1]
    v = vec[...]
    rows = lax.broadcasted_iota(jnp.int32, v.shape, 0)
    turned = pltpu.roll(v, lax.rem((n - lax.axis_index("col")) * width, v.shape[1]), 1)
    vec_out[...] = jnp.where(rows == 6, v * scale, turned)[:, :width]
    wait_all(out_cps)


def emit_call(n, scale, y, lat, cond, vec, grads):
    f = y.shape[1]
    sd = jax.ShapeDtypeStruct
    return pl.pallas_call(
        functools.partial(emit_kernel, n, scale),
        out_shape=[sd((LEN, f), BF), sd((LEN, f), BF), sd((CLEN, f), BF), sd((8, f // n), F32)] + [sd(g.shape, F32) for g in grads],
        in_specs=[hspec()] * 15,
        out_specs=[vspec()] * 4 + [hspec()] * 11,
        scratch_shapes=[
            pltpu.VMEM((TP, f), BF), pltpu.VMEM((TP, f), BF), pltpu.VMEM((CP, f), BF), pltpu.VMEM((8, f), F32),
            pltpu.SemaphoreType.DMA((11,)), pltpu.SemaphoreType.DMA((4,)),
        ] + [pltpu.VMEM(g.shape, F32) for g in grads],
        compiler_params=pltpu.CompilerParams(vmem_limit_bytes=62 << 20),
        name="emit",
    )(y, lat, cond, vec, *grads)


def trig_table():
    half_size = ROT // 2
    rates = np.exp(np.arange(half_size) * (-2.0 * math.log(10000.0) / ROT))
    angles = np.arange(TP)[:, None] * rates[None, :]
    table = np.zeros((TP, 128), np.float32)
    table[:, :half_size], table[:, half_size:ROT] = np.cos(angles), np.sin(angles)
    return jnp.asarray(table)


def body(
    latents,
    conditioning,
    teacher,
    gain_attn,
    bias_attn,
    gain_cross,
    bias_cross,
    gain_mlp,
    bias_mlp,
    w_query,
    w_key,
    w_value,
    w_out,
    w_cross_query,
    w_cross_key,
    w_cross_value,
    w_cross_out,
    w_gate,
    w_up,
    w_down,
):

    F = latents.shape[1]
    wide = F * lax.axis_size("row")
    n = lax.axis_size("col")
    y, glat, gcond, vec, *grads = layer_call(
        n, latents, teacher, conditioning, trig_table(), [gain_attn, bias_attn, gain_cross, bias_cross, gain_mlp, bias_mlp],
        [w_query, w_key, w_value, w_out.T, w_cross_query, w_cross_key, w_cross_value, w_cross_out.T, w_gate, w_up, w_down.T],
    )
    outputs, glat, gcond, vec, ggate, gup, gdown, go, gco, gcq, gck, gcv, gq, gk, gv = emit_call(
        n, 1.0 / (LEN * wide * n), y, glat, gcond, vec, grads
    )
    return (
        outputs, vec[6, 0], glat, gcond, gq, gk, gv, go.T, gcq, gck, gcv, gco.T, ggate, gup, gdown.T,
        vec[0], vec[1], vec[2], vec[3], vec[4], vec[5],
    )


def solution(mesh):
    in_specs = (
        P("col", "row"),
        P("col", "row"),
        P("col", "row"),
        P("row"),
        P("row"),
        P("row"),
        P("row"),
        P("row"),
        P("row"),
        P("col", "row"),
        P("col", "row"),
        P("col", "row"),
        P("row", "col"),
        P("col", "row"),
        P("col", "row"),
        P("col", "row"),
        P("row", "col"),
        P("col", "row"),
        P("col", "row"),
        P("row", "col"),
    )
    out_specs = (
        P("col", "row"),
        P(),
        P("col", "row"),
        P("col", "row"),
        P("col", "row"),
        P("col", "row"),
        P("col", "row"),
        P("row", "col"),
        P("col", "row"),
        P("col", "row"),
        P("col", "row"),
        P("row", "col"),
        P("col", "row"),
        P("col", "row"),
        P("row", "col"),
        P(("row", "col")),
        P(("row", "col")),
        P(("row", "col")),
        P(("row", "col")),
        P(("row", "col")),
        P(("row", "col")),
    )
    return jax.shard_map(body, mesh=mesh, in_specs=in_specs, out_specs=out_specs, check_vma=False)
```

```python
import functools
import math

import jax
import jax.numpy as jnp
import numpy as np
from jax import lax
from jax.sharding import PartitionSpec as P
from jax.experimental import pallas as pl
from jax.experimental.pallas import tpu as pltpu

BF, F32 = jnp.bfloat16, jnp.float32
MESH = pl.DeviceIdType.MESH
TP = 1040
LEN = 1025
CLEN = 130
CP = 144
HEAD = 64
ROT = 32
EPSILON = 1e-06
CH = 208
NCH = TP // CH
SUB = 16


def nt(a, b):
    return lax.dot_general(a, b, (((1,), (1,)), ((), ())), preferred_element_type=F32)


def remote(src, dst, ssem, rsem, dev):
    return pltpu.make_async_remote_copy(src_ref=src, dst_ref=dst, send_sem=ssem, recv_sem=rsem, device_id=dev, device_id_type=MESH)


def tn(left, right):
    return lax.dot_general(left, right, (((0,), (0,)), ((), ())), preferred_element_type=F32)


def row_stats(x, wide):
    xc = x - jnp.sum(x, axis=1, keepdims=True) * (1.0 / wide)
    inv = lax.rsqrt(jnp.sum(xc * xc, axis=1, keepdims=True) * (1.0 / wide) + EPSILON)
    return xc * inv, inv


def rotate_lanes(u, cos, sin_low, sin_high):
    width = u.shape[-1]
    return u * cos + pltpu.roll(u, width - ROT // 2, u.ndim - 1) * sin_low + pltpu.roll(u, ROT // 2, u.ndim - 1) * sin_high


def vspec():
    return pl.BlockSpec(memory_space=pltpu.VMEM)


def hspec():
    return pl.BlockSpec(memory_space=pl.ANY)


class Place:
    def __init__(self, n):
        self.n, self.outer = n, n // 2
        self.r, self.col = lax.axis_index("row"), lax.axis_index("col")
        self.c = lax.rem(self.r, 2)
        self.o = 1 - self.c
        self.xi = lax.div(self.r, 2)
        self.sib = (self.r + 1 - 2 * self.c, self.col)
        self.par = (self.r + 2 - 4 * self.xi, self.col)
        self.diag = (self.par[0] + 1 - 2 * self.c, self.col)
        self.zo, self.yi = lax.div(self.col, 2), lax.rem(self.col, 2)
        self.ypar = (self.r, self.col + 1 - 2 * self.yi)

    def zpeer(self, step):
        return lax.rem(self.zo + step, self.outer)

    def near(self, z):
        gap = z - self.zo
        return jnp.logical_and(gap < 3, gap > -3)

    def enter(self, with_cols, diagonal=False):
        barrier = pltpu.get_barrier_semaphore()
        pl.semaphore_signal(barrier, inc=1, device_id=self.sib, device_id_type=MESH)
        pl.semaphore_signal(barrier, inc=1, device_id=self.par, device_id_type=MESH)
        count = 2
        if diagonal:
            pl.semaphore_signal(barrier, inc=1, device_id=self.diag, device_id_type=MESH)
            count += 1
        if with_cols:
            pl.semaphore_signal(barrier, inc=1, device_id=self.ypar, device_id_type=MESH)

            def greet(step, carry):
                pl.semaphore_signal(barrier, inc=1, device_id=(self.r, 2 * self.zpeer(step) + self.yi), device_id_type=MESH)
                return carry

            lax.fori_loop(1, self.outer, greet, 0)
            count += self.outer
        pl.semaphore_wait(barrier, count)


class ColGather:
    more = 8

    def __init__(self, place, pieces, ahead, ssem, rsem, lsem):
        self.at, self.pieces, self.ahead, self.ssem, self.rsem, self.lsem = place, pieces, ahead, ssem, rsem, lsem
        self.line = place.outer == 4

    def rows(self, p, j):
        size = self.pieces[p][0].shape[0]
        return self.pieces[p][1].at[pl.ds(pl.multiple_of(j * size, 16), size)]

    def local(self, p):
        return pltpu.make_async_copy(self.pieces[p][0], self.rows(p, self.at.col), self.lsem.at[p])

    def send(self, p, slot, j, to, own=False):
        src = self.pieces[p][0] if own else self.rows(p, j)
        return remote(src, self.rows(p, j), self.ssem.at[p, slot], self.rsem.at[p, j], to)

    def across(self, p):
        return self.send(p, 0, self.at.col, self.at.ypar, own=True)

    def outward(self, p, step):
        at = self.at
        return self.send(p, step, at.col, (at.r, 2 * at.zpeer(step) + at.yi), own=True)

    def onward(self, p, step):
        at = self.at
        return self.send(p, at.outer - 1 + step, 2 * at.zpeer(at.outer - step) + at.yi, at.ypar)

    def steps(self, fn, source, far=False):
        at = self.at
        if far and not self.line:
            return

        def one(step):
            if not self.line:
                fn(step)
                return
            near = at.near(at.zpeer(at.outer - step) if source else at.zpeer(step))
            pl.when(jnp.logical_not(near) if far else near)(lambda: fn(step))

        each(1, at.outer, one)

    def relay(self, p, act):
        if not self.line:
            return
        at = self.at
        for mine, source, end in ((2, 0, 3), (1, 3, 0)):
            pl.when(at.zo == mine)(lambda: act(self.send(p, at.n - 1, 2 * source + at.yi, (at.r, 2 * end + at.yi))))

    def start(self, p):
        if p < len(self.pieces):
            self.local(p).start()
            self.across(p).start()
            self.steps(lambda step: self.outward(p, step).start(), False)

    def pass_on(self, p, far):
        def one(step):
            cp = self.onward(p, step)
            cp.wait_recv()
            cp.start()

        self.steps(one, True, far)

    def started(self, p):
        return self.ahead + p + 1 + max(0, min(p - 2, self.more))

    def begin(self):
        for p in range(self.ahead):
            self.start(p)

    def advance(self, p, flush=True):
        self.pass_on(p, False)
        self.relay(p, lambda cp: cp.start())
        for later in range(self.started(p - 1), self.started(p)):
            self.start(later)
        if flush and p > 0:
            self.pass_on(p - 1, True)
        if p == len(self.pieces) - 1:
            self.pass_on(p, True)

    def finish(self, p):
        at = self.at
        self.local(p).wait()
        self.across(p).wait_send()
        self.steps(lambda step: self.outward(p, step).wait_send(), False)
        each(0, at.outer, lambda z: self.send(p, 0, 2 * z + 1 - at.yi, at.ypar).wait_recv())
        self.steps(lambda step: self.onward(p, step).wait_send(), True)
        self.steps(lambda step: self.onward(p, step).wait_send(), True, far=True)
        self.relay(p, lambda cp: cp.wait_send())


def gather_sems(pieces, n):
    return [pltpu.SemaphoreType.DMA((pieces, n)), pltpu.SemaphoreType.DMA((pieces, n)), pltpu.SemaphoreType.DMA((pieces,))]


class ColScatter:
    def __init__(self, place, pieces, ahead, slots, bufs, sems):
        self.at, self.pieces, self.ahead, self.slots = place, pieces, ahead, slots
        self.ry, self.hb, self.rz, self.rl, self.ob = bufs
        self.ls, self.sy, self.ryr, self.sz, self.rzr, self.rlr, self.os, self.credit = sems
        self.line = place.outer == 4
        self.size = self.hb.shape[2]

    def rows(self, p, j):
        return self.pieces[p][0].at[pl.ds(pl.multiple_of(j * self.size, 16), self.size)]

    def across(self, p, z):
        at = self.at
        return remote(
            self.rows(p, 2 * z + 1 - at.yi), self.ry.at[p % self.slots, z], self.sy.at[p, z], self.ryr.at[p, z], at.ypar
        )

    def own(self, p, z):
        return pltpu.make_async_copy(self.rows(p, 2 * z + self.at.yi), self.hb.at[p % 2, z], self.ls.at[p, z])

    def outward(self, p, z):
        at, s = self.at, p % self.slots
        return remote(self.ry.at[s, z], self.rz.at[s, at.zo], self.sz.at[p, z], self.rzr.at[p, at.zo], (at.r, 2 * z + at.yi))

    def detour(self, p, z):
        at, s = self.at, p % self.slots
        via = lax.div(at.zo, 3) + 1
        return remote(self.ry.at[s, z], self.rl.at[s], self.sz.at[p, z], self.rlr.at[p], (at.r, 2 * via + at.yi))

    def merging(self, z):
        zo = self.at.zo
        return jnp.logical_or(jnp.logical_and(zo == 1, z == 3), jnp.logical_and(zo == 2, z == 0))

    def arrives(self, zs):
        return self.at.near(zs)

    def blocks(self, fn):
        each(0, self.size // 48, lambda k: fn(pl.ds(pl.multiple_of(k * 48, 16), 48)))

    def begin(self):
        for p in range(self.ahead):
            self.start(p)

    def start(self, p):
        if p >= len(self.pieces):
            return
        if p >= self.slots:
            pl.semaphore_wait(self.credit.at[p - self.slots], self.at.outer)

        def one(z):
            self.across(p, z).start()
            if p < 2:
                self.own(p, z).start()

        each(0, self.at.outer, one)

    def reduce(self, p):
        at, s = self.at, p % self.slots

        def one(step):
            z = at.zpeer(step)
            self.own(p, z).wait()
            self.across(p, z).wait_recv()

            def add(rs):
                self.ry[s, z, rs] = (self.hb[p % 2, z, rs].astype(F32) + self.ry[s, z, rs].astype(F32)).astype(BF)

            self.blocks(add)

            @pl.when(z != at.zo)
            def _():
                if not self.line:
                    self.outward(p, z).start()
                    return
                near = at.near(z)
                pl.when(jnp.logical_not(near))(lambda: self.detour(p, z).start())
                pl.when(jnp.logical_and(near, jnp.logical_not(self.merging(z))))(lambda: self.outward(p, z).start())

        each(1, at.outer + 1, one)
        if p + 2 < len(self.pieces):
            each(0, at.outer, lambda z: self.own(p + 2, z).start())

    def merge(self, p):
        if not self.line:
            return
        at, s = self.at, p % self.slots
        for mine, z, origin in ((1, 3, 0), (2, 0, 3)):
            @pl.when(at.zo == mine)
            def _():
                remote(self.rl.at[s], self.rl.at[s], self.sz.at[p, z], self.rlr.at[p], at.ypar).wait_recv()

                def add(rs):
                    self.ry[s, z, rs] = (self.ry[s, z, rs].astype(F32) + self.rl[s, rs].astype(F32)).astype(BF)

                self.blocks(add)
                self.outward(p, z).start()

    def result(self, p):
        return pltpu.make_async_copy(self.ob.at[p % 2], self.pieces[p][1], self.os.at[p])

    def finish(self, p):
        at, s = self.at, p % self.slots
        if p >= 2:
            self.result(p - 2).wait()

        def first(rs):
            self.ob[p % 2, rs] = self.ry[s, at.zo, rs].astype(F32)

        self.blocks(first)

        def one(step):
            zs = at.zpeer(at.outer - step)

            def take():
                remote(self.rz.at[s, zs], self.rz.at[s, zs], self.sz.at[p, zs], self.rzr.at[p, zs], at.ypar).wait_recv()

                def add(rs):
                    self.ob[p % 2, rs] += self.rz[s, zs, rs].astype(F32)

                self.blocks(add)

            if self.line:
                pl.when(at.near(zs))(take)
            else:
                take()

        each(1, at.outer, one)
        self.result(p).start()

        def sent(z):
            self.across(p, z).wait_send()

            @pl.when(z != at.zo)
            def _():
                self.outward(p, z).wait_send()

        each(0, at.outer, sent)
        if p + self.slots < len(self.pieces):
            pl.semaphore_signal(self.credit.at[p], inc=1, device_id=at.ypar, device_id_type=MESH)
            each(
                1,
                at.outer,
                lambda step: pl.semaphore_signal(
                    self.credit.at[p], inc=1, device_id=(at.r, 2 * at.zpeer(step) + at.yi), device_id_type=MESH
                ),
            )

    def advance(self, p):
        if p < len(self.pieces):
            self.reduce(p)
        if 0 <= p - 1 < len(self.pieces):
            self.merge(p - 1)
        if 0 <= p - 2 < len(self.pieces):
            self.finish(p - 2)
        self.start(p + self.ahead)

    def complete(self):
        count = len(self.pieces)
        self.advance(count)
        self.advance(count + 1)
        for p in range(max(0, count - 2), count):
            self.result(p).wait()


def scatter_scratch(pieces, slots, n, f, rows):
    size, outer = rows // n, n // 2
    dma = pltpu.SemaphoreType.DMA
    block = lambda *lead: pltpu.VMEM(lead + (size, f), BF)
    return [
        block(slots, outer), block(2, outer), block(slots, outer), block(slots),
        pltpu.VMEM((2, size, f), F32),
    ], [
        dma((pieces, outer)), dma((pieces, outer)), dma((pieces, outer)), dma((pieces, outer)), dma((pieces, outer)),
        dma((pieces,)), dma((pieces,)), pltpu.SemaphoreType.REGULAR((pieces,)),
    ]


class RowGather:
    def __init__(self, place, pieces, ssem, rsem, lsem):
        self.at, self.pieces, self.ssem, self.rsem, self.lsem = place, pieces, ssem, rsem, lsem

    def cols(self, p, j):
        size = self.pieces[p][0].shape[1]
        return self.pieces[p][1].at[:, pl.ds(pl.multiple_of(j * size, 128), size)]

    def copies(self, p):
        at = self.at
        src, mine = self.pieces[p][0], self.cols(p, at.r)
        theirs = self.cols(p, at.par[0])
        return (
            pltpu.make_async_copy(src, mine, self.lsem.at[p]),
            remote(src, mine, self.ssem.at[p, 0], self.rsem.at[p, 0], at.sib),
            remote(src, mine, self.ssem.at[p, 1], self.rsem.at[p, 1], at.par),
            remote(theirs, theirs, self.ssem.at[p, 2], self.rsem.at[p, 2], at.sib),
        )

    def start(self, p):
        for cp in self.copies(p)[:3]:
            cp.start()

    def forward(self, p):
        local, near, far, on = self.copies(p)
        far.wait_recv()
        on.start()

    def finish(self, p):
        local, near, far, on = self.copies(p)
        local.wait()
        near.wait_recv()
        on.wait_recv()
        near.wait_send()
        far.wait_send()
        on.wait_send()


class RowReduce:
    def __init__(self, at, send_a, recv_a, acc, p1, p2, sems, free, prior):
        self.free, self.prior = free, prior
        self.at, self.send_a, self.recv_a, self.acc, self.p1, self.p2 = at, send_a, recv_a, acc, p1, p2
        self.s_a, self.r_a, self.s_b, self.r_b, self.s_c, self.r_c, self.s_d, self.r_d = sems
        self.half = p1.shape[2]

    def copy_a(self, i):
        rows = rows_of(i)
        return remote(self.send_a.at[rows], self.recv_a.at[rows], self.s_a.at[i], self.r_a.at[i], self.at.sib)

    def copy_b(self, i):
        rows, c = rows_of(i), self.at.c
        return remote(self.p1.at[c, rows], self.p2.at[c, rows], self.s_b.at[i], self.r_b.at[i], self.at.par)

    def copy_c(self, i, side):
        rows = rows_of(i)
        return remote(self.p1.at[side, rows], self.p1.at[side, rows], self.s_c.at[i], self.r_c.at[i], self.at.sib)

    def copy_d(self, i, side):
        rows = rows_of(i)
        return remote(self.p2.at[side, rows], self.p2.at[side, rows], self.s_d.at[i], self.r_d.at[i], self.at.sib)

    def partial(self, i, terms):
        half = self.half

        def side(which):
            rows = pl.ds(pl.multiple_of(which * half, 128), half)
            return sum(nt(value, w[rows]) for value, w in terms)

        self.send_a[rows_of(i)] = side(self.at.o).astype(BF)
        self.copy_a(i).start()
        self.acc[lax.rem(i, 2)] = side(self.at.c)

    def swap(self, i):
        self.copy_a(i).wait_recv()
        self.p1[self.at.c, rows_of(i)] = (self.acc[lax.rem(i, 2)] + self.recv_a[rows_of(i)].astype(F32)).astype(BF)
        if self.prior is not None:
            pl.semaphore_wait(self.prior.free.at[i], 1)
        self.copy_b(i).start()
        self.copy_c(i, self.at.c).start()

    def share(self, i):
        self.copy_b(i).wait_recv()
        self.copy_d(i, self.at.c).start()

    def ready(self, i):
        self.copy_c(i, self.at.o).wait_recv()
        self.copy_d(i, self.at.o).wait_recv()

    def total(self, rs):
        p1, p2 = self.p1, self.p2
        return jnp.concatenate(
            [p1[0, rs].astype(F32) + p2[0, rs].astype(F32), p1[1, rs].astype(F32) + p2[1, rs].astype(F32)], axis=1
        )

    def drain(self, i):
        self.copy_a(i).wait_send()
        self.copy_b(i).wait_send()
        self.copy_c(i, self.at.c).wait_send()
        self.copy_d(i, self.at.c).wait_send()
        pl.semaphore_signal(self.free.at[i], inc=1, device_id=self.at.par, device_id_type=MESH)


def rows_of(i):
    return pl.ds(pl.multiple_of(i * CH, 16), CH)


def each(low, high, fn):
    def body(i, carry):
        fn(i)
        return carry

    lax.fori_loop(low, high, body, 0)


def sub_blocks(i, fn):
    each(0, CH // SUB, lambda k: fn(k, pl.ds(pl.multiple_of(i * CH + k * SUB, SUB), SUB), pl.ds(pl.multiple_of(k * SUB, SUB), SUB)))


NEG = -1e30


def nn(a, b):
    return jnp.dot(a, b, preferred_element_type=F32)


def lanes(shape):
    return lax.broadcasted_iota(jnp.int32, shape, len(shape) - 1)


def head_mask(value, which):
    lane = lanes(value.shape)
    keep = (lane < HEAD) if which == 0 else (lane >= HEAD)
    return jnp.where(keep, value, jnp.zeros_like(value))


def attend_step(i, q_ref, q_off, k_ref, k_off, v_ref, v_off, keys, valid, out_ref, lse_ref, heads, hook=None):
    rows = rows_of(i)
    lse = jnp.zeros((CH, 128), F32)
    for pair in range(heads // 2):
        qp = q_ref[rows, q_off + 128 * pair:q_off + 128 * (pair + 1)]
        kp = k_ref[:, k_off + 128 * pair:k_off + 128 * (pair + 1)]
        vp = v_ref[:, v_off + 128 * pair:v_off + 128 * (pair + 1)]
        mixed = []
        for which in range(2):
            s = nt(head_mask(qp, which), kp)
            s = jnp.where(lanes((1, keys)) < valid, s, NEG)
            top = jnp.max(s, axis=1, keepdims=True)
            e = jnp.exp(s - top)
            total = jnp.sum(e, axis=1, keepdims=True)
            mixed.append(nn(e.astype(BF), vp) / total)
            lse = jnp.where(lanes(lse.shape) == 2 * pair + which, top + jnp.log(total), lse)
        both = jnp.where(lanes(mixed[0].shape) < HEAD, mixed[0], mixed[1])
        out_ref[rows, 128 * pair:128 * (pair + 1)] = both.astype(BF)
        if hook is not None:
            hook(pair)
    lse_ref[rows] = lse


def attend_back(q_ref, q_off, k_ref, k_off, v_ref, v_off, keys, kblock, valid, do_ref, out_ref, lse_ref, lse_t, delta_t, dqt, emit_q, emit_kv, heads, hook=None):
    queries = q_ref.shape[0]
    lse_t[...] = lse_ref[...].T
    delta = jnp.zeros((queries, 128), F32)
    for pair in range(heads // 2):
        cols = slice(128 * pair, 128 * (pair + 1))
        prod = do_ref[:, cols].astype(F32) * out_ref[:, cols].astype(F32)
        for which in range(2):
            one = jnp.sum(head_mask(prod, which), axis=1, keepdims=True)
            delta = jnp.where(lanes(delta.shape) == 2 * pair + which, one, delta)
    delta_t[...] = delta.T
    for pair in range(heads // 2):
        qc = slice(q_off + 128 * pair, q_off + 128 * (pair + 1))
        kc = slice(k_off + 128 * pair, k_off + 128 * (pair + 1))
        vc = slice(v_off + 128 * pair, v_off + 128 * (pair + 1))
        oc = slice(128 * pair, 128 * (pair + 1))
        dqt[...] = jnp.zeros_like(dqt)

        def keys_step(j, carry):
            rows = pl.ds(pl.multiple_of(j * kblock, 16), kblock)
            kb, vb = k_ref[rows, kc], v_ref[rows, vc]
            dks, dvs = [], []
            for which in range(2):
                h = 2 * pair + which
                km = head_mask(kb, which)
                p = jnp.exp(nt(km, q_ref[:, qc]) - lse_t[h:h + 1])
                if keys != valid:
                    pos = j * kblock + lax.broadcasted_iota(jnp.int32, (kblock, 1), 0)
                    p = jnp.where(pos < valid, p, 0.0)
                dp = nt(head_mask(vb, which), do_ref[:, oc])
                ds = (p * (dp - delta_t[h:h + 1])).astype(BF)
                dvs.append(nn(p.astype(BF), do_ref[:, oc]))
                dks.append(nn(ds, q_ref[:, qc]))
                dqt[...] += nn(km.T, ds)
            low = lanes(dks[0].shape) < HEAD
            emit_kv(pair, rows, jnp.where(low, dks[0], dks[1]), jnp.where(low, dvs[0], dvs[1]))
            if hook is not None:
                hook(pair, j)
            return carry

        lax.fori_loop(0, keys // kblock, keys_step, 0)
        emit_q(pair, dqt[...].T)


def rotate_lanes(u, cos, sin_low, sin_high):
    width = u.shape[-1]
    return u * cos + pltpu.roll(u, width - ROT // 2, u.ndim - 1) * sin_low + pltpu.roll(u, ROT // 2, u.ndim - 1) * sin_high


def norm_back(tot, x, prior, gain, wide):
    xh, inv = row_stats(x, wide)
    e = tot * gain
    m1 = jnp.sum(e, axis=1, keepdims=True) * (1.0 / wide)
    m2 = jnp.sum(e * xh, axis=1, keepdims=True) * (1.0 / wide)
    return prior + inv * (e - m1 - xh * m2), tot * xh


def fold(ref, at, value):
    ref[at] += value[:8] + value[8:]


def local(src, dst, sem):
    return pltpu.make_async_copy(src, dst, sem)


def start_all(copies):
    for cp in copies:
        cp.start()


def wait_all(copies):
    for cp in copies:
        cp.wait()


def pad_into(dst, src, count):
    whole = count // 16 * 16
    dst[:whole] = src[:whole]
    left = count - whole
    rows = lax.broadcasted_iota(jnp.int32, (16, dst.shape[1]), 0)
    tile = jnp.zeros((16, dst.shape[1]), F32)
    for k in range(left):
        tile = jnp.where(rows == k, src[whole + k:whole + k + 1].astype(F32), tile)
    dst[whole:whole + 16] = tile.astype(dst.dtype)


def spread_tables(trig, cos, low, high):
    half = ROT // 2
    t = trig[...]
    lane = lanes(t.shape)
    place = lax.rem(lane, HEAD)
    first, second = place < half, jnp.logical_and(place >= half, place < ROT)
    both = lambda u: jnp.where(lane < HEAD, u, pltpu.roll(u, HEAD, 1))
    shift = lambda u: pltpu.roll(u, half, 1)
    back = lambda u: pltpu.roll(u, 128 - half, 1)
    c16, s16 = both(t), both(back(t))
    cos[...] = jnp.where(first, c16, jnp.where(second, shift(c16), 1.0))
    low[...] = jnp.where(first, -s16, 0.0)
    high[...] = jnp.where(second, shift(s16), 0.0)


def front_phase(k, gather):
    at, f, wide = k.at, k.f, k.wide
    dma = pltpu.SemaphoreType.DMA

    def run(latv, teachv, condv, latp, teachp, condp, smallv, trig, cos, low, high, x, h, qkv, a, lse, st, w, vec, ssem, lsem, sem):
        ins = [local(k.lat, latv, sem.at[0]), local(k.teach, teachv, sem.at[1]), local(k.cond, condv, sem.at[2]), local(k.trig, trig, sem.at[4])]
        start_all(ins)
        rowg = RowGather(at, [(latp, k.x0), (smallv, k.vecs), (condp, k.cond_full), (teachp, k.teach_full)], ssem, k.row_sem, lsem)
        ins[0].wait()
        pad_into(latp, latv, LEN)
        smallv[...] = jnp.zeros_like(smallv)
        for j in range(6):
            smallv[j, :] = k.small[j][...]
        at.enter(True, diagonal=True)
        rowg.start(0)
        rowg.start(1)
        gather.begin()
        wait_all(ins[1:3])
        pad_into(condp, condv, CLEN)
        pad_into(teachp, teachv, LEN)
        ins[3].wait()
        spread_tables(trig, cos, low, high)
        gather.advance(0)
        rowg.forward(0)
        rowg.forward(1)
        gather.advance(1)
        rowg.finish(0)
        rowg.finish(1)
        more = [local(k.x0, x, sem.at[0]), local(k.vecs, vec, sem.at[1])]
        start_all(more)
        rowg.start(2)
        rowg.start(3)
        wait_all(more)

        def norm(b):
            rows = pl.ds(pl.multiple_of(b * SUB, SUB), SUB)
            v = x[rows].astype(F32)
            mean = jnp.sum(v, axis=1, keepdims=True) * (1.0 / wide)
            xc = v - mean
            inv = lax.rsqrt(jnp.sum(xc * xc, axis=1, keepdims=True) * (1.0 / wide) + EPSILON)
            h[rows] = (xc * inv * vec[0:1] + vec[1:2]).astype(BF)
            st[rows] = jnp.where(lanes((SUB, 128)) == 2, mean, inv)

        each(0, TP // SUB, norm)
        outs = [local(h, k.h1, sem.at[2]), local(st, k.st1, sem.at[3])]
        start_all(outs)
        gather.advance(2)
        rowg.forward(2)
        fetch = lambda p: local(gather.pieces[p][1], w.at[p % 2], sem.at[4 + p % 2])
        gather.finish(0)
        fetch(0).start()
        for part in range(3):
            fetch(part).wait()
            gather.advance(3 + part)
            if part < 2:
                gather.finish(part + 1)
                fetch(part + 1).start()

            def project(i):
                rows = rows_of(i)
                c, lo, hi = cos[rows], low[rows], high[rows]
                res = nn(h[rows], w[part % 2])
                for pair in range(f // 128):
                    u = res[:, pair * 128:(pair + 1) * 128]
                    if part < 2:
                        u = rotate_lanes(u, c, lo, hi).astype(BF)
                    else:
                        u = u.astype(BF)
                    if part == 0:
                        u = u * HEAD ** (-0.5)
                    qkv[rows, part * f + pair * 128:part * f + (pair + 1) * 128] = u

            each(0, NCH, project)

        def attend(i):
            def hook(pair):
                for p in range(6, k.front_pieces):
                    pl.when(i * 3 + pair == (p - 6) * 15 // (k.front_pieces - 6))(lambda: gather.advance(p))

            attend_step(i, qkv, 0, qkv, f, qkv, 2 * f, TP, LEN, a, lse, f // HEAD, hook)

        each(0, NCH, attend)
        last = [local(qkv, k.qkv, sem.at[0]), local(a, k.a, sem.at[1]), local(lse, k.lse1, sem.at[6])]
        start_all(last)
        rowg.forward(3)
        rowg.finish(2)
        rowg.finish(3)
        wait_all(outs + last)

    vm = pltpu.VMEM
    pl.run_scoped(
        run,
        latv=vm((LEN, f), BF), teachv=vm((LEN, f), BF), condv=vm((CLEN, f), BF), latp=vm((TP, f), BF), teachp=vm((TP, f), BF),
        condp=vm((CP, f), BF), smallv=vm((8, f), F32), trig=vm((TP, 128), F32), cos=vm((TP, 128), F32), low=vm((TP, 128), F32),
        high=vm((TP, 128), F32), x=vm((TP, wide), BF), h=vm((TP, wide), BF), qkv=vm((TP, 3 * f), BF), a=vm((TP, f), BF),
        lse=vm((TP, 128), F32), st=vm((TP, 128), F32), w=vm((2, wide, f), BF), vec=vm((8, wide), F32),
        ssem=dma((4, 3)), lsem=dma((4,)), sem=dma((7,)),
    )


def mid_phase(k, gather, first, second):
    at, f, wide = k.at, k.f, k.wide
    dma, vm = pltpu.SemaphoreType.DMA, pltpu.VMEM
    slots = list(range(k.front_pieces, k.mid_pieces))

    def run(a, x0, x, low, wo, wq, wk, wv, wc, cq, ckv, c, lse, cond, vec, acc, sem, osem, esem):
        first.acc, second.acc = acc, acc
        for p in range(3, 8):
            gather.finish(p)
        loads = [
            local(src, dst, sem.at[j])
            for j, (src, dst) in enumerate(
                ((k.a, a), (k.full[3], wo), (k.full[5], wk), (k.full[6], wv), (k.cond_full, cond), (k.x0, x0), (k.full[4], wq), (k.full[7], wc), (k.vecs, vec))
            )
        ]
        start_all(loads)
        wait_all(loads[:2])

        def project(i):
            first.partial(i, [(a[rows_of(i)], wo)])
            pl.when(i > 0)(lambda: first.swap(i - 1))

        each(0, NCH, project)
        first.swap(NCH - 1)
        wait_all(loads[2:])
        ckv[:, :f] = nn(cond[...], wk[...]).astype(BF)
        ckv[:, f:] = nn(cond[...], wv[...]).astype(BF)

        def outs(i, main, lowest, which):
            return [
                local(x.at[rows_of(i)], main.at[rows_of(i)], osem.at[which, 2 * i]),
                local(low.at[rows_of(i)], lowest.at[rows_of(i)], osem.at[which, 2 * i + 1]),
            ]

        def hook(slot, base):
            for j, p in enumerate(slots):
                spot = j * 2 * NCH // len(slots)
                if base <= spot < base + NCH:
                    pl.when(slot == spot - base)(lambda: gather.advance(p))

        def cross(i):
            first.ready(i)

            def block(b, rs, ls):
                v = x0[rs].astype(F32) + first.total(rs)
                x[rs] = v
                low[rs] = (row_stats(v, wide)[0] * vec[2:3] + vec[3:4]).astype(BF)

            sub_blocks(i, block)
            start_all(outs(i, k.x1, k.h2, 0))
            rows = rows_of(i)
            cq[rows] = nn(low[rows], wq[...]).astype(BF) * HEAD ** (-0.5)
            attend_step(i, cq, 0, ckv, 0, ckv, f, CP, CLEN, c, lse, f // HEAD)
            first.drain(i)
            second.partial(i, [(c[rows], wc)])
            pl.when(i > 0)(lambda: second.swap(i - 1))

        def step(i):
            first.share(i)
            pl.when(i > 0)(lambda: cross(i - 1))
            hook(i, 0)

        each(0, NCH, step)
        cross(NCH - 1)
        second.swap(NCH - 1)
        ends = [local(cq, k.cq, esem.at[0]), local(ckv, k.ckv, esem.at[1]), local(c, k.c, esem.at[2]), local(lse, k.lse2, esem.at[3])]
        start_all(ends)

        def last(i):
            second.ready(i)
            wait_all(outs(i, k.x1, k.h2, 0))

            def block(b, rs, ls):
                v = x[rs] + second.total(rs)
                x[rs] = v
                low[rs] = (row_stats(v, wide)[0] * vec[4:5] + vec[5:6]).astype(BF)

            sub_blocks(i, block)
            start_all(outs(i, k.x2, k.h3, 1))

        def step_two(i):
            second.share(i)
            pl.when(i > 0)(lambda: last(i - 1))
            hook(i, NCH)

        each(0, NCH, step_two)
        last(NCH - 1)

        def end(i):
            second.drain(i)
            wait_all(outs(i, k.x2, k.h3, 1))

        each(0, NCH, end)
        wait_all(ends)

    weight = lambda: vm((wide, f), BF)
    pl.run_scoped(
        run,
        a=vm((TP, f), BF), x0=vm((TP, wide), BF), x=vm((TP, wide), F32), low=vm((TP, wide), BF), wo=weight(), wq=weight(), wk=weight(),
        wv=weight(), wc=weight(), cq=vm((TP, f), BF), ckv=vm((CP, 2 * f), BF), c=vm((TP, f), BF), lse=vm((TP, 128), F32),
        cond=vm((CP, wide), BF), vec=vm((8, wide), F32), acc=vm((2, CH, wide // 2), F32), sem=dma((9,)), osem=dma((2, 2 * NCH)), esem=dma((4,)),
    )


def mlp_phase(k, gather, red, nxt, h, hid, sg, tt, dm):
    at, f, wide = k.at, k.f, k.wide
    dma, vm = pltpu.SemaphoreType.DMA, pltpu.VMEM
    parts = k.parts
    col = lambda j: slice(j * f, (j + 1) * f)
    own = pl.ds(pl.multiple_of(at.r * f, 128), f)

    def run(wg, wu, wd, acc, xbuf, tbuf, sq, sem, wsem, xsem, tsem, rsem, ysem):
        red.acc, nxt.acc = acc, acc
        hcp = local(k.h3, h, sem.at[0])
        hcp.start()
        sq[...] = jnp.zeros_like(sq)

        def slot_in(i):
            s = lax.rem(i, 2)
            return [local(k.x2.at[rows_of(i)], xbuf.at[s], xsem.at[s]), local(k.teach_full.at[rows_of(i)], tbuf.at[s], tsem.at[s])]

        for i in range(2):
            start_all(slot_in(i))
        pending = list(range(k.mid_pieces, len(gather.pieces)))

        def fetch(p):
            q, j = (p - 8) % 2 if p < 16 else 2, (p - 8) // 2 if p < 16 else p - 16
            return local(gather.pieces[p][1], (wg, wu, wd)[q].at[:, col(j)], wsem.at[p - 8])

        done = [8]

        def bring(upto):
            while done[0] <= upto:
                while pending and pending[0] <= done[0] + 1:
                    gather.advance(pending.pop(0))
                gather.finish(done[0])
                fetch(done[0]).start()
                done[0] += 1

        bring(9)
        hcp.wait()
        for j in range(parts):
            if j < parts - 1:
                bring(11 + 2 * j)
            fetch(8 + 2 * j).wait()
            fetch(9 + 2 * j).wait()

            def hidden(i):
                rows = rows_of(i)
                gate = nn(h[rows], wg[:, col(j)])
                up = nn(h[rows], wu[:, col(j)])
                sig = jax.nn.sigmoid(gate)
                act = gate * sig
                hid[rows, col(j)] = (act * up).astype(BF)
                sg[rows, col(j)] = act.astype(BF)
                tt[rows, col(j)] = (up * sig * (1.0 + gate * (1.0 - sig))).astype(BF)

            each(0, NCH, hidden)
            if pending:
                gather.advance(pending.pop(0))
        bring(15 + parts)
        for j in range(parts):
            fetch(16 + j).wait()

        def project(i):
            red.partial(i, [(hid[rows_of(i)], wd)])
            pl.when(i > 0)(lambda: red.swap(i - 1))

        each(0, NCH, project)
        red.swap(NCH - 1)

        def outs_of(i):
            s = lax.rem(i, 2)
            return [local(xbuf.at[s], k.res.at[rows_of(i)], rsem.at[s]), local(tbuf.at[s, :, own], k.y.at[rows_of(i)], ysem.at[s])]

        def finish(i):
            s = lax.rem(i, 2)
            red.ready(i)

            @pl.when(i >= 1)
            def _():
                wait_all(outs_of(i - 1))
                pl.when(i < NCH - 1)(lambda: start_all(slot_in(i + 1)))

            wait_all(slot_in(i))

            def block(b, rs, ls):
                y = xbuf[s, ls] + red.total(rs)
                pos = i * CH + b * SUB + lax.broadcasted_iota(jnp.int32, (SUB, wide), 0)
                res = jnp.where(pos < LEN, y - tbuf[s, ls].astype(F32), 0.0)
                xbuf[s, ls] = res
                dm[rs] = res.astype(BF)
                tbuf[s, ls] = y.astype(BF)
                sq_ = res * res
                sq[...] += sq_[:8] + sq_[8:]

            sub_blocks(i, block)
            start_all(outs_of(i))
            rows = rows_of(i)
            for j in range(parts):
                dh = nn(dm[rows], wd[:, col(j)])
                tt[rows, col(j)] = (dh * tt[rows, col(j)].astype(F32)).astype(BF)
                sg[rows, col(j)] = (dh * sg[rows, col(j)].astype(F32)).astype(BF)
            red.drain(i)
            nxt.partial(i, [(tt[rows], wg), (sg[rows], wu)])
            pl.when(i > 0)(lambda: nxt.swap(i - 1))

        def step(i):
            red.share(i)
            pl.when(i > 0)(lambda: finish(i - 1))

        each(0, NCH, step)
        finish(NCH - 1)
        nxt.swap(NCH - 1)
        scp = local(sq, k.squares, sem.at[0])
        scp.start()
        wait_all(outs_of(NCH - 1))
        scp.wait()

    weight = lambda: vm((wide, parts * f), BF)
    pl.run_scoped(
        run,
        wg=weight(), wu=weight(), wd=weight(), acc=vm((2, CH, wide // 2), F32), xbuf=vm((2, CH, wide), F32), tbuf=vm((2, CH, wide), BF),
        sq=vm((8, wide), F32), sem=dma((1,)), wsem=dma((3 * parts,)), xsem=dma((2,)), tsem=dma((2,)),
        rsem=dma((2,)), ysem=dma((2,)),
    )


class Grads:
    def __init__(self, part, stage, sem, f):
        self.part, self.stage, self.sem, self.f = part, stage, sem, f

    def copy(self, p):
        return local(self.stage, self.part.at[:, p * self.f:(p + 1) * self.f], self.sem.at[p % 2])

    def make(self, p, left, right):
        wide = left.shape[1]

        def one(j):
            cols = pl.ds(pl.multiple_of(j * 512, 128), 512)
            self.stage[cols] = tn(left[:, cols], right()).astype(BF)

        each(0, wide // 512, one)
        self.copy(p).start()


def mid_back_phase(k, scatter, first, second, h, hid, sg, tt, dm):
    at, f, wide = k.at, k.f, k.wide
    dma, vm = pltpu.SemaphoreType.DMA, pltpu.VMEM

    def run(g, low, xs, wc, wq, dkv, dc, cq, ckv, c, lse, dcq, sums, vec, acc, stage, sem, xsem, osem, gsem):
        second.acc = acc
        grads = Grads(k.part, stage, gsem, f)
        rest = [
            local(src, dst, sem.at[j])
            for j, (src, dst) in enumerate(((k.res, g), (k.full[7], wc), (k.full[4], wq), (k.cq, cq), (k.ckv, ckv), (k.c, c), (k.lse2, lse), (k.vecs, vec)))
        ]
        start_all(rest)

        def stream(src, i, s):
            return local(src.at[rows_of(i)], xs.at[s], xsem.at[s])

        stream(k.x2, 0, 0).start()
        stream(k.x2, 1, 1).start()
        sums[...] = jnp.zeros_like(sums)
        dkv[...] = jnp.zeros_like(dkv)

        def make(p):
            q, j = p // 4, p % 4
            left, right = ((h, tt), (h, sg), (dm, hid))[q]
            grads.make(p, left, lambda: right[:, j * f:(j + 1) * f])

        for p in range(2):
            make(p)
            grads.copy(p).wait()
            scatter.start(p)
        wait_all(rest)

        def hook(slot, base):
            for p in range(base + 2, base + 2 + NCH):
                @pl.when(slot == p - 2 - base)
                def _():
                    make(p)
                    grads.copy(p).wait()
                    if p < scatter.ahead:
                        scatter.start(p)

            for p in range(k.back_pieces):
                spot = p * 2 * NCH // k.back_pieces + 1
                if base <= spot < base + NCH:
                    pl.when(slot == spot - base)(lambda: scatter.advance(p))

        def low_out(i, which):
            return local(low.at[lax.rem(i + which * NCH, 2)], (k.dco, k.do)[which].at[rows_of(i)], osem.at[which, i])

        def g_out(i):
            return local(g.at[rows_of(i)], k.g1.at[rows_of(i)], osem.at[2, i])

        valid = lambda: lax.broadcasted_iota(jnp.int32, (CP, 1), 0) < CLEN

        def cross(i):
            first.ready(i)
            s = lax.rem(i, 2)
            stream(k.x2, i, s).wait()
            pl.when(i >= 2)(lambda: low_out(i - 2, 0).wait())

            def block(b, rs, ls):
                tot = first.total(rs)
                new, dx = norm_back(tot, xs[s, ls], g[rs], vec[4:5], wide)
                g[rs] = new
                low[s, ls] = new.astype(BF)
                fold(sums, 0, dx)
                fold(sums, 1, tot)

            sub_blocks(i, block)
            pl.when(i < NCH - 2)(lambda: stream(k.x2, i + 2, s).start())
            pl.when(i >= NCH - 2)(lambda: stream(k.x1, i + 2 - NCH, s).start())
            low_out(i, 0).start()
            rows = rows_of(i)
            dc[...] = nn(low[s], wc[...]).astype(BF)
            lse_t = lse[rows].T
            delta = jnp.zeros((CH, 128), F32)
            for pair in range(f // 128):
                cols = slice(128 * pair, 128 * (pair + 1))
                prod = dc[:, cols].astype(F32) * c[rows, cols].astype(F32)
                for which in range(2):
                    one = jnp.sum(head_mask(prod, which), axis=1, keepdims=True)
                    delta = jnp.where(lanes(delta.shape) == 2 * pair + which, one, delta)
            delta_t = delta.T
            for pair in range(f // 128):
                cols = slice(128 * pair, 128 * (pair + 1))
                vcols = slice(f + 128 * pair, f + 128 * (pair + 1))
                kb, vb, qc, doc = ckv[:, cols], ckv[:, vcols], cq[rows, cols], dc[:, cols]
                dks, dvs, dqt = [], [], None
                for which in range(2):
                    hd = 2 * pair + which
                    km = head_mask(kb, which)
                    p = jnp.where(valid(), jnp.exp(nt(km, qc) - lse_t[hd:hd + 1]), 0.0)
                    dp = nt(head_mask(vb, which), doc)
                    ds = (p * (dp - delta_t[hd:hd + 1])).astype(BF)
                    dvs.append(nn(p.astype(BF), doc))
                    dks.append(nn(ds, qc))
                    part = nn(km.T, ds)
                    dqt = part if dqt is None else dqt + part
                left = lanes(dks[0].shape) < HEAD
                dkv[:, cols] += jnp.where(left, dks[0], dks[1])
                dkv[:, vcols] += jnp.where(left, dvs[0], dvs[1])
                dcq[rows, cols] = (dqt.T * HEAD ** (-0.5)).astype(BF)
            first.drain(i)
            second.partial(i, [(dcq[rows], wq)])
            pl.when(i > 0)(lambda: second.swap(i - 1))

        def step(i):
            first.share(i)
            pl.when(i > 0)(lambda: cross(i - 1))
            hook(i, 0)

        each(0, NCH, step)
        cross(NCH - 1)
        second.swap(NCH - 1)
        ckv[...] = dkv[...].astype(BF)

        def last(i):
            second.ready(i)
            s = lax.rem(i + NCH, 2)
            stream(k.x1, i, s).wait()
            pl.when(i < 2)(lambda: low_out(NCH - 2 + i, 0).wait())
            pl.when(i >= 2)(lambda: low_out(i - 2, 1).wait())

            def block(b, rs, ls):
                tot = second.total(rs)
                new, dx = norm_back(tot, xs[s, ls], g[rs], vec[2:3], wide)
                g[rs] = new
                low[s, ls] = new.astype(BF)
                fold(sums, 2, dx)
                fold(sums, 3, tot)

            sub_blocks(i, block)
            pl.when(i < NCH - 2)(lambda: stream(k.x1, i + 2, s).start())
            low_out(i, 1).start()
            g_out(i).start()

        def step_two(i):
            second.share(i)
            pl.when(i > 0)(lambda: last(i - 1))
            hook(i, NCH)

        each(0, NCH, step_two)
        last(NCH - 1)
        ends = [local(dcq, k.dcq, sem.at[0]), local(ckv, k.dckv, sem.at[1]), local(sums, k.sums, sem.at[2])]
        start_all(ends)

        def end(i):
            second.drain(i)
            pl.when(i >= NCH - 2)(lambda: low_out(i, 1).wait())
            g_out(i).wait()

        each(0, NCH, end)
        wait_all(ends)

    pl.run_scoped(
        run,
        g=vm((TP, wide), F32), low=vm((2, CH, wide), BF), xs=vm((2, CH, wide), F32), wc=vm((wide, f), BF), wq=vm((wide, f), BF),
        dkv=vm((CP, 2 * f), F32), dc=vm((CH, f), BF), cq=vm((TP, f), BF), ckv=vm((CP, 2 * f), BF), c=vm((TP, f), BF),
        lse=vm((TP, 128), F32), dcq=vm((TP, f), BF), sums=vm((4, 8, wide), F32), vec=vm((8, wide), F32), acc=vm((2, CH, wide // 2), F32),
        stage=vm((wide, f), BF), sem=dma((8,)), xsem=dma((2,)), osem=dma((3, NCH)), gsem=dma((2,)),
    )


def end_phase(k, scatter):
    at, f, wide = k.at, k.f, k.wide
    dma, vm = pltpu.SemaphoreType.DMA, pltpu.VMEM
    r, c_, o = at.r, at.c, at.o
    own = pl.ds(pl.multiple_of(r * f, 128), f)
    send_a, recv_a = k.send_a, k.recv_a
    send_b, recv_b = k.p1.at[0, :, :f], k.p2.at[0, :, :f]

    def run(xa, xb, wt, w1, da, dqkv, lse_t, delta_t, dqt, stage, xo, go, g1, tot, acc, st, back, st_t, cpart, qkv, a, lse, trig,
            cos, low, high, c, dcq, dckv, cond, sums, sq, vr, vb, lat, gc, sem, gsem, s_c, s_x, s_v):
        grads = Grads(k.part, stage, gsem, f)
        names = {}

        def load(name, src, dst):
            names[name] = local(src, dst, sem.at[len(names)])
            names[name].start()

        load("do", k.do, xa)
        load("wo", k.full[3], wt)
        load("a", k.a, a)
        load("qkv", k.qkv, qkv)
        load("lse", k.lse1, lse)
        load("trig", k.trig, trig)
        load("h2", k.h2, xb)
        load("c", k.c, c)
        load("dcq", k.dcq, dcq)
        load("dckv", k.dckv, dckv)
        load("cond", k.cond_full, cond)
        rest = ["st", "xo", "go", "g1", "sums", "sq"]
        for name, src, dst in (
            ("st", k.st1, st), ("xo", k.x0.at[:, own], xo), ("go", k.vecs.at[:, own], go), ("g1", k.g1.at[:, own], g1),
            ("sums", k.sums.at[:, :, own], sums), ("sq", k.squares, sq),
        ):
            load(name, src, dst)
        for j in range(3):
            load(f"w{j}", k.full[j], w1.at[:, j * f:(j + 1) * f])
            rest.append(f"w{j}")

        def ready(*which):
            for name in which:
                names[name].wait()

        def make(p, left, right):
            grads.make(p, left, right)
            grads.copy(p).wait()

        ready("do", "wo", "a")

        def project_da(i):
            da[rows_of(i)] = nn(xa[rows_of(i)], wt[...]).astype(BF)

        each(0, NCH, project_da)
        make(12, xa, lambda: a[...])
        again = local(k.dco, xa, sem.at[0])
        again.start()
        wck_cp = local(k.full[5], wt, sem.at[1])
        wck_cp.start()
        nxt = k.back_pieces
        scatter.advance(nxt)
        nxt = nxt + 1
        ready("h2", "c", "dcq", "dckv", "cond")
        again.wait()
        make(13, xa, lambda: c[...])
        make(14, xb, lambda: dcq[...])
        h1_cp = local(k.h1, xb, sem.at[0])
        h1_cp.start()
        make(15, cond, lambda: dckv[:, :f])
        make(16, cond, lambda: dckv[:, f:])
        ready("qkv", "lse", "trig")
        spread_tables(trig, cos, low, high)

        def emit_q(pair, dq):
            dqkv[:, 128 * pair:128 * (pair + 1)] = rotate_lanes(dq * HEAD ** (-0.5), cos[...], -low[...], -high[...]).astype(BF)

        def emit_kv(pair, rows, dk, dv):
            dqkv[rows, f + 128 * pair:f + 128 * (pair + 1)] = rotate_lanes(dk, cos[rows], -low[rows], -high[rows]).astype(BF)
            dqkv[rows, 2 * f + 128 * pair:2 * f + 128 * (pair + 1)] = dv.astype(BF)


        def hook(pair, j):
            for step, spot in enumerate(k.end_spots):
                if spot[0] == pair:
                    pl.when(j == spot[1])(lambda: scatter.advance(nxt + step))

        attend_back(qkv, 0, qkv, f, qkv, 2 * f, TP, CH, LEN, da, a, lse, lse_t, delta_t, dqt, emit_q, emit_kv, f // HEAD, hook)
        nxt = nxt + len(k.end_spots)

        h1_cp.wait()
        for j in range(3):
            make(17 + j, xb, lambda: dqkv[:, j * f:(j + 1) * f])
        scatter.advance(nxt)

        wck_cp.wait()
        for j in range(4):
            cpart[j] = nt(dckv[:, :f], wt[j * f:(j + 1) * f])
        wcv_cp = local(k.full[6], wt, sem.at[1])
        wcv_cp.start()
        scatter.advance(nxt + 1)
        wcv_cp.wait()
        crecv = k.crecv
        for j in range(4):
            crecv[j] = (cpart[j] + nt(dckv[:, f:], wt[j * f:(j + 1) * f])).astype(BF)
        peers = (at.sib, at.par, at.diag)
        cond_cps = [remote(crecv.at[peers[j][0]], crecv.at[4 + j], s_c.at[j], k.r_c.at[j], peers[j]) for j in range(3)]
        start_all(cond_cps)
        ready(*rest)

        wblock = lambda j: w1[pl.ds(pl.multiple_of(j * f, 128), f)]

        def copy_a(i):
            return remote(send_a.at[rows_of(i)], recv_a.at[rows_of(i)], k.e_sa.at[i], k.e_ra.at[i], at.sib)

        def copy_b(i):
            return remote(send_b.at[rows_of(i)], recv_b.at[rows_of(i)], k.e_sb.at[i], k.e_rb.at[i], at.par)

        def swap(i):
            copy_a(i).wait_recv()
            both = acc[lax.rem(i, 2)] + recv_a[rows_of(i)].astype(F32)
            left, right = both[:, :f], both[:, f:]
            tot[rows_of(i)] = jnp.where(at.xi == 0, left, right)
            send_b[rows_of(i)] = jnp.where(at.xi == 0, right, left).astype(BF)
            pl.semaphore_wait(k.last_sum.free.at[i], 1)
            copy_b(i).start()

        def project(i):
            y = dqkv[rows_of(i)]
            send_a[rows_of(i), :f] = nt(y, wblock(o)).astype(BF)
            send_a[rows_of(i), f:] = nt(y, wblock(2 + o)).astype(BF)
            copy_a(i).start()
            acc[lax.rem(i, 2), :, :f] = nt(y, wblock(c_))
            acc[lax.rem(i, 2), :, f:] = nt(y, wblock(2 + c_))
            pl.when(i > 0)(lambda: swap(i - 1))

        each(0, NCH, project)
        swap(NCH - 1)
        vr[...] = jnp.zeros_like(vr)
        scatter.advance(nxt + 2)

        def sums_of(i):
            copy_b(i).wait_recv()

            def block(b, rs, ls):
                t = tot[rs] + recv_b[rs].astype(F32)
                tot[rs] = t
                own_st = st[rs]
                mean, inv = own_st[:, 2:3], own_st[:, 3:4]
                xh = (xo[rs].astype(F32) - mean) * inv
                e = t * go[0:1]
                lane = lanes((SUB, 128))
                first = jnp.sum(e, axis=1, keepdims=True)
                cross = jnp.sum(e * xh, axis=1, keepdims=True)
                back[rs] = jnp.where(lane == 0, first, cross)
                fold(vr, 0, t * xh)
                fold(vr, 1, t)

            sub_blocks(i, block)

        each(0, NCH, sums_of)
        sx = k.sx
        st_t[...] = back[...].T
        sx[0] = st_t[:8]
        stat_cps = [remote(sx.at[0], sx.at[1 + j], s_x.at[j], k.r_x.at[j], peers[j]) for j in range(3)]
        start_all(stat_cps)
        total = lambda x: jnp.sum(x, axis=0, keepdims=True)
        error = jnp.sum(total(sq[...]), axis=1, keepdims=True)
        vb[0:1] = total(vr[0])
        vb[1:2] = total(vr[1])
        vb[2:3] = total(sums[2])
        vb[3:4] = total(sums[3])
        vb[4:5] = total(sums[0])
        vb[5:6] = total(sums[1])
        vb[6:8] = jnp.broadcast_to(error, (2, f))
        vz = k.vz
        pair_cp = remote(vb, vz.at[at.outer], s_v.at[at.outer], k.r_v.at[at.outer], at.ypar)
        pair_cp.start()
        scatter.advance(nxt + 3)
        for cp in cond_cps:
            cp.wait_recv()
        gc[...] = (crecv[r].astype(F32) + crecv[4].astype(F32) + crecv[5].astype(F32) + crecv[6].astype(F32)).astype(BF)
        for cp in stat_cps:
            cp.wait_recv()
        st_t[:8] = sx[0] + sx[1] + sx[2] + sx[3]
        back[...] = st_t[...].T
        pair_cp.wait()
        vz[at.zo] = vb[...] + vz[at.outer]

        def vec_out(step):
            return remote(vz.at[at.zo], vz.at[at.zo], s_v.at[step], k.r_v.at[at.zo], (r, 2 * at.zpeer(step) + at.yi))

        each(1, at.outer, lambda step: vec_out(step).start())

        def last(i):
            def block(b, rs, ls):
                e = tot[rs] * go[0:1]
                row_sums, own_st = back[rs], st[rs]
                first, cross = row_sums[:, 0:1] * (1.0 / wide), row_sums[:, 1:2] * (1.0 / wide)
                mean, inv = own_st[:, 2:3], own_st[:, 3:4]
                xh = (xo[rs].astype(F32) - mean) * inv
                lat[rs] = (g1[rs] + inv * (e - first - xh * cross)).astype(BF)

            sub_blocks(i, block)

        each(0, NCH, last)
        outs = [local(lat, k.glat, sem.at[0]), local(gc, k.gcond, sem.at[1])]
        start_all(outs)
        for p in range(nxt + 4, len(scatter.pieces)):
            scatter.advance(p)
        vb[...] = vz[at.zo]

        def vec_in(step):
            zs = at.zpeer(at.outer - step)
            remote(vz.at[zs], vz.at[zs], s_v.at[step], k.r_v.at[zs], at.ypar).wait_recv()
            vb[...] += vz[zs]

        each(1, at.outer, vec_in)
        vec_cp = local(vb, k.vec, sem.at[2])
        vec_cp.start()
        each(1, at.outer, lambda step: vec_out(step).wait_send())
        scatter.complete()
        for cp in stat_cps + cond_cps:
            cp.wait_send()

        def drain(i):
            copy_a(i).wait_send()
            copy_b(i).wait_send()

        each(0, NCH, drain)
        wait_all(outs + [vec_cp])

    tab = lambda: vm((TP, 128), F32)
    flip = lambda: vm((128, TP), F32)
    pl.run_scoped(
        run,
        xa=vm((TP, wide), BF), xb=vm((TP, wide), BF), wt=vm((wide, f), BF), w1=vm((wide, 3 * f), BF), da=vm((TP, f), BF),
        dqkv=vm((TP, 3 * f), BF), lse_t=flip(), delta_t=flip(), dqt=flip(), stage=vm((wide, f), BF), xo=vm((TP, f), BF),
        go=vm((8, f), F32), g1=vm((TP, f), F32), tot=vm((TP, f), F32), acc=vm((2, CH, 2 * f), F32), st=tab(), back=tab(), st_t=flip(),
        cpart=vm((4, CP, f), F32), qkv=vm((TP, 3 * f), BF), a=vm((TP, f), BF), lse=tab(), trig=tab(), cos=tab(), low=tab(), high=tab(),
        c=vm((TP, f), BF), dcq=vm((TP, f), BF), dckv=vm((CP, 2 * f), BF), cond=vm((CP, wide), BF), sums=vm((4, 8, f), F32),
        sq=vm((8, wide), F32), vr=vm((2, 8, f), F32), vb=vm((8, f), F32), lat=vm((TP, f), BF), gc=vm((CP, f), BF),
        sem=dma((24,)), gsem=dma((2,)), s_c=dma((3,)), s_x=dma((3,)), s_v=dma((k.outer + 1,)),
    )


class Names:
    pass


def layer_kernel(n, f, pieces, front_pieces, mid_pieces, back_pieces, ahead, s_ahead, slots, *refs):
    refs = list(refs)
    take = lambda count: [refs.pop(0) for _ in range(count)]
    k = Names()
    k.at, k.f, k.wide, k.outer = Place(n), f, 4 * f, n // 2
    k.front_pieces, k.mid_pieces, k.back_pieces = front_pieces, mid_pieces, back_pieces
    k.end_spots = ((0, 2), (1, 0), (1, 3), (2, 2))
    k.lat, k.teach, k.cond, k.trig = take(4)
    k.small = take(6)
    shards = take(11)
    k.y, k.glat, k.gcond, k.vec = take(4)
    gate_out, up_out, down_out = take(3)
    square_out = take(8)
    k.full = take(8)
    mlp_full = take(3)
    k.x0, k.vecs, k.cond_full, k.teach_full, k.h1, k.st1, k.qkv, k.a, k.lse1 = take(9)
    k.x1, k.h2, k.cq, k.ckv, k.c, k.lse2, k.x2, k.h3 = take(8)
    k.res, k.squares, k.g1, k.dco, k.do, k.dcq, k.dckv, k.sums, k.part = take(9)
    k.send_a, k.recv_a, k.p1, k.p2, k.sx, k.crecv, k.vz = take(7)
    sems = [take(8) for _ in range(5)]
    free = take(5)
    k.e_sa, k.e_ra, k.e_sb, k.e_rb, k.row_sem, k.r_c, k.r_x, k.r_v = take(8)
    gather_sem = take(3)
    bufs, scatter_sem = take(5), take(8)
    k.parts = shards[8].shape[1] // f
    col = lambda j: slice(j * f, (j + 1) * f)
    made = [(shards[j], k.full[j]) for j in range(8)]
    for j in range(k.parts):
        for q in range(2):
            made.append((shards[8 + q].at[:, col(j)], mlp_full[q].at[:, col(j)]))
    made += [(shards[10].at[:, col(j)], mlp_full[2].at[:, col(j)]) for j in range(k.parts)]
    gather = ColGather(k.at, made, ahead, *gather_sem)
    sums = []
    for q, out in enumerate((gate_out, up_out, down_out)):
        sums += [(k.part.at[:, col(q * k.parts + j)], out.at[:, col(j)]) for j in range(k.parts)]
    sums += [(k.part.at[:, col(3 * k.parts + j)], square_out[j]) for j in range(8)]
    scatter = ColScatter(k.at, sums, s_ahead, slots, bufs, scatter_sem)
    red = [None]
    for j in range(5):
        red.append(RowReduce(k.at, k.send_a, k.recv_a, None, k.p1, k.p2, sems[j], free[j], red[j]))
    red = red[1:]
    k.last_sum = red[4]
    front_phase(k, gather)
    mid_phase(k, gather, red[0], red[1])
    full = pltpu.VMEM((TP, k.wide), BF)

    def back(h, hid, sg, tt, dm):
        mlp_phase(k, gather, red[2], red[3], h, hid, sg, tt, dm)
        mid_back_phase(k, scatter, red[3], red[4], h, hid, sg, tt, dm)

    pl.run_scoped(back, h=full, hid=full, sg=full, tt=full, dm=full)
    end_phase(k, scatter)


def layer_call(n, lat, teach, cond, trig, small, shards, front_pieces=12, mid_pieces=19, back_pieces=9, ahead=4, s_ahead=3, slots=5):
    f = lat.shape[1]
    wide, size, outer = 4 * f, shards[0].shape[0], n // 2
    ffl = shards[8].shape[1]
    sd = jax.ShapeDtypeStruct
    dma = pltpu.SemaphoreType.DMA
    vm = pltpu.VMEM
    half = wide // 2
    results = [sd((TP, f), BF), sd((TP, f), BF), sd((CP, f), BF), sd((8, f), F32)]
    results += [sd((size, ffl), F32)] * 3 + [sd((size, f), F32)] * 8
    between = [sd((wide, f), BF)] * 8 + [sd((wide, ffl), BF)] * 3
    rows, rows32 = sd((TP, wide), BF), sd((TP, wide), F32)
    between += [rows, sd((8, wide), F32), sd((CP, wide), BF), rows, rows, sd((TP, 128), F32), sd((TP, 3 * f), BF), sd((TP, f), BF), sd((TP, 128), F32)]
    between += [rows32, rows, sd((TP, f), BF), sd((CP, 2 * f), BF), sd((TP, f), BF), sd((TP, 128), F32), rows32, rows]
    between += [rows32, sd((8, wide), F32), rows32, rows, rows, sd((TP, f), BF), sd((CP, 2 * f), BF), sd((4, 8, wide), F32), sd((wide, 3 * ffl + 8 * f), BF)]
    pieces = 8 + 3 * ffl // f
    scratch = [
        vm((TP, half), BF), vm((TP, half), BF), vm((2, TP, half), BF), vm((2, TP, half), BF),
        vm((4, 8, TP), F32), vm((7, CP, f), BF), vm((outer + 1, 8, f), F32),
    ] + [dma((NCH,))] * 40 + [pltpu.SemaphoreType.REGULAR((NCH,))] * 5 + [dma((NCH,))] * 4 + [dma((4, 3)), dma((3,)), dma((3,)), dma((outer + 1,))]
    bufs, sems = scatter_scratch(pieces, slots, n, f, wide)
    scratch += gather_sems(pieces, n) + bufs + sems
    out = pl.pallas_call(
        functools.partial(layer_kernel, n, f, pieces, front_pieces, mid_pieces, back_pieces, ahead, s_ahead, slots),
        out_shape=results + between,
        in_specs=[hspec()] * 4 + [vspec()] * 6 + [hspec()] * 11,
        out_specs=[hspec()] * (len(results) + len(between)),
        scratch_shapes=scratch,
        compiler_params=pltpu.CompilerParams(collective_id=0, has_side_effects=True, vmem_limit_bytes=66_900_000),
        name="layer",
    )(lat, teach, cond, trig, *small, *shards)
    return out[:len(results)]


def emit_kernel(n, scale, *refs):
    refs = list(refs)
    take = lambda count: [refs.pop(0) for _ in range(count)]
    moved, grads = take(4), take(11)
    y_out, lat_out, cond_out, vec_out = take(4)
    grad_outs = take(11)
    y, lat, cond, vec, sem, vsem = take(6)
    held = take(11)
    cps = [local(src, dst, sem.at[j]) for j, (src, dst) in enumerate(zip(grads, held))]
    out_cps = [local(src, dst, sem.at[j]) for j, (src, dst) in enumerate(zip(held, grad_outs))]
    ins = [local(src, dst, vsem.at[j]) for j, (src, dst) in enumerate(zip(moved, (y, lat, cond, vec)))]
    start_all(cps + ins)
    for cp, out in zip(cps, out_cps):
        cp.wait()
        out.start()
    wait_all(ins)
    y_out[...] = y[:y_out.shape[0]]
    lat_out[...] = lat[:lat_out.shape[0]]
    cond_out[...] = cond[:cond_out.shape[0]]
    width = vec_out.shape[1]
    v = vec[...]
    rows = lax.broadcasted_iota(jnp.int32, v.shape, 0)
    turned = pltpu.roll(v, lax.rem((n - lax.axis_index("col")) * width, v.shape[1]), 1)
    vec_out[...] = jnp.where(rows == 6, v * scale, turned)[:, :width]
    wait_all(out_cps)


def emit_call(n, scale, y, lat, cond, vec, grads):
    f = y.shape[1]
    sd = jax.ShapeDtypeStruct
    return pl.pallas_call(
        functools.partial(emit_kernel, n, scale),
        out_shape=[sd((LEN, f), BF), sd((LEN, f), BF), sd((CLEN, f), BF), sd((8, f // n), F32)] + [sd(g.shape, F32) for g in grads],
        in_specs=[hspec()] * 15,
        out_specs=[vspec()] * 4 + [hspec()] * 11,
        scratch_shapes=[
            pltpu.VMEM((TP, f), BF), pltpu.VMEM((TP, f), BF), pltpu.VMEM((CP, f), BF), pltpu.VMEM((8, f), F32),
            pltpu.SemaphoreType.DMA((11,)), pltpu.SemaphoreType.DMA((4,)),
        ] + [pltpu.VMEM(g.shape, F32) for g in grads],
        compiler_params=pltpu.CompilerParams(vmem_limit_bytes=62 << 20),
        name="emit",
    )(y, lat, cond, vec, *grads)


def trig_table():
    half_size = ROT // 2
    rates = np.exp(np.arange(half_size) * (-2.0 * math.log(10000.0) / ROT))
    angles = np.arange(TP)[:, None] * rates[None, :]
    table = np.zeros((TP, 128), np.float32)
    table[:, :half_size], table[:, half_size:ROT] = np.cos(angles), np.sin(angles)
    return jnp.asarray(table)


def body(
    latents,
    conditioning,
    teacher,
    gain_attn,
    bias_attn,
    gain_cross,
    bias_cross,
    gain_mlp,
    bias_mlp,
    w_query,
    w_key,
    w_value,
    w_out,
    w_cross_query,
    w_cross_key,
    w_cross_value,
    w_cross_out,
    w_gate,
    w_up,
    w_down,
):

    F = latents.shape[1]
    wide = F * lax.axis_size("row")
    n = lax.axis_size("col")
    y, glat, gcond, vec, *grads = layer_call(
        n, latents, teacher, conditioning, trig_table(), [gain_attn, bias_attn, gain_cross, bias_cross, gain_mlp, bias_mlp],
        [w_query, w_key, w_value, w_out.T, w_cross_query, w_cross_key, w_cross_value, w_cross_out.T, w_gate, w_up, w_down.T],
    )
    outputs, glat, gcond, vec, ggate, gup, gdown, go, gco, gcq, gck, gcv, gq, gk, gv = emit_call(
        n, 1.0 / (LEN * wide * n), y, glat, gcond, vec, grads
    )
    return (
        outputs, vec[6, 0], glat, gcond, gq, gk, gv, go.T, gcq, gck, gcv, gco.T, ggate, gup, gdown.T,
        vec[0], vec[1], vec[2], vec[3], vec[4], vec[5],
    )


def solution(mesh):
    in_specs = (
        P("col", "row"),
        P("col", "row"),
        P("col", "row"),
        P("row"),
        P("row"),
        P("row"),
        P("row"),
        P("row"),
        P("row"),
        P("col", "row"),
        P("col", "row"),
        P("col", "row"),
        P("row", "col"),
        P("col", "row"),
        P("col", "row"),
        P("col", "row"),
        P("row", "col"),
        P("col", "row"),
        P("col", "row"),
        P("row", "col"),
    )
    out_specs = (
        P("col", "row"),
        P(),
        P("col", "row"),
        P("col", "row"),
        P("col", "row"),
        P("col", "row"),
        P("col", "row"),
        P("row", "col"),
        P("col", "row"),
        P("col", "row"),
        P("col", "row"),
        P("row", "col"),
        P("col", "row"),
        P("col", "row"),
        P("row", "col"),
        P(("row", "col")),
        P(("row", "col")),
        P(("row", "col")),
        P(("row", "col")),
        P(("row", "col")),
        P(("row", "col")),
    )
    return jax.shard_map(body, mesh=mesh, in_specs=in_specs, out_specs=out_specs, check_vma=False)
```

```python
import functools
import math

import jax
import jax.numpy as jnp
import numpy as np
from jax import lax
from jax.sharding import PartitionSpec as P
from jax.experimental import pallas as pl
from jax.experimental.pallas import tpu as pltpu

BF, F32 = jnp.bfloat16, jnp.float32
MESH = pl.DeviceIdType.MESH
TP = 1040
LEN = 1025
CLEN = 130
CP = 144
HEAD = 64
ROT = 32
EPSILON = 1e-06
CH = 208
NCH = TP // CH
SUB = 16


def nt(a, b):
    return lax.dot_general(a, b, (((1,), (1,)), ((), ())), preferred_element_type=F32)


def remote(src, dst, ssem, rsem, dev):
    return pltpu.make_async_remote_copy(src_ref=src, dst_ref=dst, send_sem=ssem, recv_sem=rsem, device_id=dev, device_id_type=MESH)


def tn(left, right):
    return lax.dot_general(left, right, (((0,), (0,)), ((), ())), preferred_element_type=F32)


def row_stats(x, wide):
    xc = x - jnp.sum(x, axis=1, keepdims=True) * (1.0 / wide)
    inv = lax.rsqrt(jnp.sum(xc * xc, axis=1, keepdims=True) * (1.0 / wide) + EPSILON)
    return xc * inv, inv


def rotate_lanes(u, cos, sin_low, sin_high):
    width = u.shape[-1]
    return u * cos + pltpu.roll(u, width - ROT // 2, u.ndim - 1) * sin_low + pltpu.roll(u, ROT // 2, u.ndim - 1) * sin_high


def vspec():
    return pl.BlockSpec(memory_space=pltpu.VMEM)


def hspec():
    return pl.BlockSpec(memory_space=pl.ANY)


class Place:
    def __init__(self, n):
        self.n, self.outer = n, n // 2
        self.r, self.col = lax.axis_index("row"), lax.axis_index("col")
        self.c = lax.rem(self.r, 2)
        self.o = 1 - self.c
        self.xi = lax.div(self.r, 2)
        self.sib = (self.r + 1 - 2 * self.c, self.col)
        self.par = (self.r + 2 - 4 * self.xi, self.col)
        self.diag = (self.par[0] + 1 - 2 * self.c, self.col)
        self.zo, self.yi = lax.div(self.col, 2), lax.rem(self.col, 2)
        self.ypar = (self.r, self.col + 1 - 2 * self.yi)

    def zpeer(self, step):
        return lax.rem(self.zo + step, self.outer)

    def near(self, z):
        gap = z - self.zo
        return jnp.logical_and(gap < 3, gap > -3)

    def enter(self, with_cols, diagonal=False):
        barrier = pltpu.get_barrier_semaphore()
        pl.semaphore_signal(barrier, inc=1, device_id=self.sib, device_id_type=MESH)
        pl.semaphore_signal(barrier, inc=1, device_id=self.par, device_id_type=MESH)
        count = 2
        if diagonal:
            pl.semaphore_signal(barrier, inc=1, device_id=self.diag, device_id_type=MESH)
            count += 1
        if with_cols:
            pl.semaphore_signal(barrier, inc=1, device_id=self.ypar, device_id_type=MESH)

            def greet(step, carry):
                pl.semaphore_signal(barrier, inc=1, device_id=(self.r, 2 * self.zpeer(step) + self.yi), device_id_type=MESH)
                return carry

            lax.fori_loop(1, self.outer, greet, 0)
            count += self.outer
        pl.semaphore_wait(barrier, count)


class ColGather:
    more = 8

    def __init__(self, place, pieces, ahead, ssem, rsem, lsem):
        self.at, self.pieces, self.ahead, self.ssem, self.rsem, self.lsem = place, pieces, ahead, ssem, rsem, lsem
        self.line = place.outer == 4

    def rows(self, p, j):
        size = self.pieces[p][0].shape[0]
        return self.pieces[p][1].at[pl.ds(pl.multiple_of(j * size, 16), size)]

    def local(self, p):
        return pltpu.make_async_copy(self.pieces[p][0], self.rows(p, self.at.col), self.lsem.at[p])

    def send(self, p, slot, j, to, own=False):
        src = self.pieces[p][0] if own else self.rows(p, j)
        return remote(src, self.rows(p, j), self.ssem.at[p, slot], self.rsem.at[p, j], to)

    def across(self, p):
        return self.send(p, 0, self.at.col, self.at.ypar, own=True)

    def outward(self, p, step):
        at = self.at
        return self.send(p, step, at.col, (at.r, 2 * at.zpeer(step) + at.yi), own=True)

    def onward(self, p, step):
        at = self.at
        return self.send(p, at.outer - 1 + step, 2 * at.zpeer(at.outer - step) + at.yi, at.ypar)

    def steps(self, fn, source, far=False):
        at = self.at
        if far and not self.line:
            return

        def one(step):
            if not self.line:
                fn(step)
                return
            near = at.near(at.zpeer(at.outer - step) if source else at.zpeer(step))
            pl.when(jnp.logical_not(near) if far else near)(lambda: fn(step))

        each(1, at.outer, one)

    def relay(self, p, act):
        if not self.line:
            return
        at = self.at
        for mine, source, end in ((2, 0, 3), (1, 3, 0)):
            pl.when(at.zo == mine)(lambda: act(self.send(p, at.n - 1, 2 * source + at.yi, (at.r, 2 * end + at.yi))))

    def start(self, p):
        if p < len(self.pieces):
            self.local(p).start()
            self.across(p).start()
            self.steps(lambda step: self.outward(p, step).start(), False)

    def pass_on(self, p, far):
        def one(step):
            cp = self.onward(p, step)
            cp.wait_recv()
            cp.start()

        self.steps(one, True, far)

    def started(self, p):
        return self.ahead + p + 1 + max(0, min(p - 2, self.more))

    def begin(self):
        for p in range(self.ahead):
            self.start(p)

    def advance(self, p, flush=True):
        self.pass_on(p, False)
        self.relay(p, lambda cp: cp.start())
        for later in range(self.started(p - 1), self.started(p)):
            self.start(later)
        if flush and p > 0:
            self.pass_on(p - 1, True)
        if p == len(self.pieces) - 1:
            self.pass_on(p, True)

    def finish(self, p):
        at = self.at
        self.local(p).wait()
        self.across(p).wait_send()
        self.steps(lambda step: self.outward(p, step).wait_send(), False)
        each(0, at.outer, lambda z: self.send(p, 0, 2 * z + 1 - at.yi, at.ypar).wait_recv())
        self.steps(lambda step: self.onward(p, step).wait_send(), True)
        self.steps(lambda step: self.onward(p, step).wait_send(), True, far=True)
        self.relay(p, lambda cp: cp.wait_send())


def gather_sems(pieces, n):
    return [pltpu.SemaphoreType.DMA((pieces, n)), pltpu.SemaphoreType.DMA((pieces, n)), pltpu.SemaphoreType.DMA((pieces,))]


class ColScatter:
    def __init__(self, place, pieces, ahead, slots, bufs, sems):
        self.at, self.pieces, self.ahead, self.slots = place, pieces, ahead, slots
        self.ry, self.hb, self.rz, self.rl, self.ob = bufs
        self.ls, self.sy, self.ryr, self.sz, self.rzr, self.rlr, self.os, self.credit = sems
        self.line = place.outer == 4
        self.size = self.hb.shape[2]

    def rows(self, p, j):
        return self.pieces[p][0].at[pl.ds(pl.multiple_of(j * self.size, 16), self.size)]

    def across(self, p, z):
        at = self.at
        return remote(
            self.rows(p, 2 * z + 1 - at.yi), self.ry.at[p % self.slots, z], self.sy.at[p, z], self.ryr.at[p, z], at.ypar
        )

    def own(self, p, z):
        return pltpu.make_async_copy(self.rows(p, 2 * z + self.at.yi), self.hb.at[p % 2, z], self.ls.at[p, z])

    def outward(self, p, z):
        at, s = self.at, p % self.slots
        return remote(self.ry.at[s, z], self.rz.at[s, at.zo], self.sz.at[p, z], self.rzr.at[p, at.zo], (at.r, 2 * z + at.yi))

    def detour(self, p, z):
        at, s = self.at, p % self.slots
        via = lax.div(at.zo, 3) + 1
        return remote(self.ry.at[s, z], self.rl.at[s], self.sz.at[p, z], self.rlr.at[p], (at.r, 2 * via + at.yi))

    def merging(self, z):
        zo = self.at.zo
        return jnp.logical_or(jnp.logical_and(zo == 1, z == 3), jnp.logical_and(zo == 2, z == 0))

    def arrives(self, zs):
        return self.at.near(zs)

    def blocks(self, fn):
        each(0, self.size // 48, lambda k: fn(pl.ds(pl.multiple_of(k * 48, 16), 48)))

    def begin(self):
        for p in range(self.ahead):
            self.start(p)

    def start(self, p):
        if p >= len(self.pieces):
            return
        if p >= self.slots:
            pl.semaphore_wait(self.credit.at[p - self.slots], self.at.outer)

        def one(z):
            self.across(p, z).start()
            if p < 2:
                self.own(p, z).start()

        each(0, self.at.outer, one)

    def reduce(self, p):
        at, s = self.at, p % self.slots

        def one(step):
            z = at.zpeer(step)
            self.own(p, z).wait()
            self.across(p, z).wait_recv()

            def add(rs):
                self.ry[s, z, rs] = (self.hb[p % 2, z, rs].astype(F32) + self.ry[s, z, rs].astype(F32)).astype(BF)

            self.blocks(add)

            @pl.when(z != at.zo)
            def _():
                if not self.line:
                    self.outward(p, z).start()
                    return
                near = at.near(z)
                pl.when(jnp.logical_not(near))(lambda: self.detour(p, z).start())
                pl.when(jnp.logical_and(near, jnp.logical_not(self.merging(z))))(lambda: self.outward(p, z).start())

        each(1, at.outer + 1, one)
        if p + 2 < len(self.pieces):
            each(0, at.outer, lambda z: self.own(p + 2, z).start())

    def merge(self, p):
        if not self.line:
            return
        at, s = self.at, p % self.slots
        for mine, z, origin in ((1, 3, 0), (2, 0, 3)):
            @pl.when(at.zo == mine)
            def _():
                remote(self.rl.at[s], self.rl.at[s], self.sz.at[p, z], self.rlr.at[p], at.ypar).wait_recv()

                def add(rs):
                    self.ry[s, z, rs] = (self.ry[s, z, rs].astype(F32) + self.rl[s, rs].astype(F32)).astype(BF)

                self.blocks(add)
                self.outward(p, z).start()

    def result(self, p):
        return pltpu.make_async_copy(self.ob.at[p % 2], self.pieces[p][1], self.os.at[p])

    def finish(self, p):
        at, s = self.at, p % self.slots
        if p >= 2:
            self.result(p - 2).wait()

        def first(rs):
            self.ob[p % 2, rs] = self.ry[s, at.zo, rs].astype(F32)

        self.blocks(first)

        def one(step):
            zs = at.zpeer(at.outer - step)

            def take():
                remote(self.rz.at[s, zs], self.rz.at[s, zs], self.sz.at[p, zs], self.rzr.at[p, zs], at.ypar).wait_recv()

                def add(rs):
                    self.ob[p % 2, rs] += self.rz[s, zs, rs].astype(F32)

                self.blocks(add)

            if self.line:
                pl.when(at.near(zs))(take)
            else:
                take()

        each(1, at.outer, one)
        self.result(p).start()

        def sent(z):
            self.across(p, z).wait_send()

            @pl.when(z != at.zo)
            def _():
                self.outward(p, z).wait_send()

        each(0, at.outer, sent)
        if p + self.slots < len(self.pieces):
            pl.semaphore_signal(self.credit.at[p], inc=1, device_id=at.ypar, device_id_type=MESH)
            each(
                1,
                at.outer,
                lambda step: pl.semaphore_signal(
                    self.credit.at[p], inc=1, device_id=(at.r, 2 * at.zpeer(step) + at.yi), device_id_type=MESH
                ),
            )

    def advance(self, p):
        if p < len(self.pieces):
            self.reduce(p)
        if 0 <= p - 1 < len(self.pieces):
            self.merge(p - 1)
        if 0 <= p - 2 < len(self.pieces):
            self.finish(p - 2)
        self.start(p + self.ahead)

    def complete(self):
        count = len(self.pieces)
        self.advance(count)
        self.advance(count + 1)
        for p in range(max(0, count - 2), count):
            self.result(p).wait()


def scatter_scratch(pieces, slots, n, f, rows):
    size, outer = rows // n, n // 2
    dma = pltpu.SemaphoreType.DMA
    block = lambda *lead: pltpu.VMEM(lead + (size, f), BF)
    return [
        block(slots, outer), block(2, outer), block(slots, outer), block(slots),
        pltpu.VMEM((2, size, f), F32),
    ], [
        dma((pieces, outer)), dma((pieces, outer)), dma((pieces, outer)), dma((pieces, outer)), dma((pieces, outer)),
        dma((pieces,)), dma((pieces,)), pltpu.SemaphoreType.REGULAR((pieces,)),
    ]


class RowGather:
    def __init__(self, place, pieces, ssem, rsem, lsem):
        self.at, self.pieces, self.ssem, self.rsem, self.lsem = place, pieces, ssem, rsem, lsem

    def cols(self, p, j):
        size = self.pieces[p][0].shape[1]
        return self.pieces[p][1].at[:, pl.ds(pl.multiple_of(j * size, 128), size)]

    def copies(self, p):
        at = self.at
        src, mine = self.pieces[p][0], self.cols(p, at.r)
        theirs = self.cols(p, at.par[0])
        return (
            pltpu.make_async_copy(src, mine, self.lsem.at[p]),
            remote(src, mine, self.ssem.at[p, 0], self.rsem.at[p, 0], at.sib),
            remote(src, mine, self.ssem.at[p, 1], self.rsem.at[p, 1], at.par),
            remote(theirs, theirs, self.ssem.at[p, 2], self.rsem.at[p, 2], at.sib),
        )

    def start(self, p):
        for cp in self.copies(p)[:3]:
            cp.start()

    def forward(self, p):
        local, near, far, on = self.copies(p)
        far.wait_recv()
        on.start()

    def finish(self, p):
        local, near, far, on = self.copies(p)
        local.wait()
        near.wait_recv()
        on.wait_recv()
        near.wait_send()
        far.wait_send()
        on.wait_send()


class RowReduce:
    def __init__(self, at, send_a, recv_a, acc, p1, p2, sems, free, prior):
        self.free, self.prior = free, prior
        self.at, self.send_a, self.recv_a, self.acc, self.p1, self.p2 = at, send_a, recv_a, acc, p1, p2
        self.s_a, self.r_a, self.s_b, self.r_b, self.s_c, self.r_c, self.s_d, self.r_d = sems
        self.half = p1.shape[2]

    def copy_a(self, i):
        rows = rows_of(i)
        return remote(self.send_a.at[rows], self.recv_a.at[rows], self.s_a.at[i], self.r_a.at[i], self.at.sib)

    def copy_b(self, i):
        rows, c = rows_of(i), self.at.c
        return remote(self.p1.at[c, rows], self.p2.at[c, rows], self.s_b.at[i], self.r_b.at[i], self.at.par)

    def copy_c(self, i, side):
        rows = rows_of(i)
        return remote(self.p1.at[side, rows], self.p1.at[side, rows], self.s_c.at[i], self.r_c.at[i], self.at.sib)

    def copy_d(self, i, side):
        rows = rows_of(i)
        return remote(self.p2.at[side, rows], self.p2.at[side, rows], self.s_d.at[i], self.r_d.at[i], self.at.sib)

    def partial(self, i, terms):
        half = self.half

        def side(which):
            rows = pl.ds(pl.multiple_of(which * half, 128), half)
            return sum(nt(value, w[rows]) for value, w in terms)

        self.send_a[rows_of(i)] = side(self.at.o).astype(BF)
        self.copy_a(i).start()
        self.acc[lax.rem(i, 2)] = side(self.at.c)

    def swap(self, i):
        self.copy_a(i).wait_recv()
        self.p1[self.at.c, rows_of(i)] = (self.acc[lax.rem(i, 2)] + self.recv_a[rows_of(i)].astype(F32)).astype(BF)
        if self.prior is not None:
            pl.semaphore_wait(self.prior.free.at[i], 1)
        self.copy_b(i).start()
        self.copy_c(i, self.at.c).start()

    def share(self, i):
        self.copy_b(i).wait_recv()
        self.copy_d(i, self.at.c).start()

    def ready(self, i):
        self.copy_c(i, self.at.o).wait_recv()
        self.copy_d(i, self.at.o).wait_recv()

    def total(self, rs):
        p1, p2 = self.p1, self.p2
        return jnp.concatenate(
            [p1[0, rs].astype(F32) + p2[0, rs].astype(F32), p1[1, rs].astype(F32) + p2[1, rs].astype(F32)], axis=1
        )

    def drain(self, i):
        self.copy_a(i).wait_send()
        self.copy_b(i).wait_send()
        self.copy_c(i, self.at.c).wait_send()
        self.copy_d(i, self.at.c).wait_send()
        pl.semaphore_signal(self.free.at[i], inc=1, device_id=self.at.par, device_id_type=MESH)


def rows_of(i):
    return pl.ds(pl.multiple_of(i * CH, 16), CH)


def each(low, high, fn):
    def body(i, carry):
        fn(i)
        return carry

    lax.fori_loop(low, high, body, 0)


def sub_blocks(i, fn):
    each(0, CH // SUB, lambda k: fn(k, pl.ds(pl.multiple_of(i * CH + k * SUB, SUB), SUB), pl.ds(pl.multiple_of(k * SUB, SUB), SUB)))


NEG = -1e30


def nn(a, b):
    return jnp.dot(a, b, preferred_element_type=F32)


def lanes(shape):
    return lax.broadcasted_iota(jnp.int32, shape, len(shape) - 1)


def head_mask(value, which):
    lane = lanes(value.shape)
    keep = (lane < HEAD) if which == 0 else (lane >= HEAD)
    return jnp.where(keep, value, jnp.zeros_like(value))


def attend_step(i, q_ref, q_off, k_ref, k_off, v_ref, v_off, keys, valid, out_ref, lse_ref, heads, hook=None):
    rows = rows_of(i)
    lse = jnp.zeros((CH, 128), F32)
    for pair in range(heads // 2):
        qp = q_ref[rows, q_off + 128 * pair:q_off + 128 * (pair + 1)]
        kp = k_ref[:, k_off + 128 * pair:k_off + 128 * (pair + 1)]
        vp = v_ref[:, v_off + 128 * pair:v_off + 128 * (pair + 1)]
        mixed = []
        for which in range(2):
            s = nt(head_mask(qp, which), kp)
            s = jnp.where(lanes((1, keys)) < valid, s, NEG)
            top = jnp.max(s, axis=1, keepdims=True)
            e = jnp.exp(s - top)
            total = jnp.sum(e, axis=1, keepdims=True)
            mixed.append(nn(e.astype(BF), vp) / total)
            lse = jnp.where(lanes(lse.shape) == 2 * pair + which, top + jnp.log(total), lse)
        both = jnp.where(lanes(mixed[0].shape) < HEAD, mixed[0], mixed[1])
        out_ref[rows, 128 * pair:128 * (pair + 1)] = both.astype(BF)
        if hook is not None:
            hook(pair)
    lse_ref[rows] = lse


def attend_back(q_ref, q_off, k_ref, k_off, v_ref, v_off, keys, kblock, valid, do_ref, out_ref, lse_ref, lse_t, delta_t, dqt, emit_q, emit_kv, heads, hook=None):
    queries = q_ref.shape[0]
    lse_t[...] = lse_ref[...].T
    delta = jnp.zeros((queries, 128), F32)
    for pair in range(heads // 2):
        cols = slice(128 * pair, 128 * (pair + 1))
        prod = do_ref[:, cols].astype(F32) * out_ref[:, cols].astype(F32)
        for which in range(2):
            one = jnp.sum(head_mask(prod, which), axis=1, keepdims=True)
            delta = jnp.where(lanes(delta.shape) == 2 * pair + which, one, delta)
    delta_t[...] = delta.T
    for pair in range(heads // 2):
        qc = slice(q_off + 128 * pair, q_off + 128 * (pair + 1))
        kc = slice(k_off + 128 * pair, k_off + 128 * (pair + 1))
        vc = slice(v_off + 128 * pair, v_off + 128 * (pair + 1))
        oc = slice(128 * pair, 128 * (pair + 1))
        dqt[...] = jnp.zeros_like(dqt)

        def keys_step(j, carry):
            rows = pl.ds(pl.multiple_of(j * kblock, 16), kblock)
            kb, vb = k_ref[rows, kc], v_ref[rows, vc]
            dks, dvs = [], []
            for which in range(2):
                h = 2 * pair + which
                km = head_mask(kb, which)
                p = jnp.exp(nt(km, q_ref[:, qc]) - lse_t[h:h + 1])
                if keys != valid:
                    pos = j * kblock + lax.broadcasted_iota(jnp.int32, (kblock, 1), 0)
                    p = jnp.where(pos < valid, p, 0.0)
                dp = nt(head_mask(vb, which), do_ref[:, oc])
                ds = (p * (dp - delta_t[h:h + 1])).astype(BF)
                dvs.append(nn(p.astype(BF), do_ref[:, oc]))
                dks.append(nn(ds, q_ref[:, qc]))
                dqt[...] += nn(km.T, ds)
            low = lanes(dks[0].shape) < HEAD
            emit_kv(pair, rows, jnp.where(low, dks[0], dks[1]), jnp.where(low, dvs[0], dvs[1]))
            if hook is not None:
                hook(pair, j)
            return carry

        lax.fori_loop(0, keys // kblock, keys_step, 0)
        emit_q(pair, dqt[...].T)


def rotate_lanes(u, cos, sin_low, sin_high):
    width = u.shape[-1]
    return u * cos + pltpu.roll(u, width - ROT // 2, u.ndim - 1) * sin_low + pltpu.roll(u, ROT // 2, u.ndim - 1) * sin_high


def norm_back(tot, x, prior, gain, wide):
    xh, inv = row_stats(x, wide)
    e = tot * gain
    m1 = jnp.sum(e, axis=1, keepdims=True) * (1.0 / wide)
    m2 = jnp.sum(e * xh, axis=1, keepdims=True) * (1.0 / wide)
    return prior + inv * (e - m1 - xh * m2), tot * xh


def fold(ref, at, value):
    ref[at] += value[:8] + value[8:]


def local(src, dst, sem):
    return pltpu.make_async_copy(src, dst, sem)


def start_all(copies):
    for cp in copies:
        cp.start()


def wait_all(copies):
    for cp in copies:
        cp.wait()


def pad_into(dst, src, count):
    whole = count // 16 * 16
    dst[:whole] = src[:whole]
    left = count - whole
    rows = lax.broadcasted_iota(jnp.int32, (16, dst.shape[1]), 0)
    tile = jnp.zeros((16, dst.shape[1]), F32)
    for k in range(left):
        tile = jnp.where(rows == k, src[whole + k:whole + k + 1].astype(F32), tile)
    dst[whole:whole + 16] = tile.astype(dst.dtype)


def spread_tables(trig, cos, low, high):
    half = ROT // 2
    t = trig[...]
    lane = lanes(t.shape)
    place = lax.rem(lane, HEAD)
    first, second = place < half, jnp.logical_and(place >= half, place < ROT)
    both = lambda u: jnp.where(lane < HEAD, u, pltpu.roll(u, HEAD, 1))
    shift = lambda u: pltpu.roll(u, half, 1)
    back = lambda u: pltpu.roll(u, 128 - half, 1)
    c16, s16 = both(t), both(back(t))
    cos[...] = jnp.where(first, c16, jnp.where(second, shift(c16), 1.0))
    low[...] = jnp.where(first, -s16, 0.0)
    high[...] = jnp.where(second, shift(s16), 0.0)


def front_phase(k, gather):
    at, f, wide = k.at, k.f, k.wide
    dma = pltpu.SemaphoreType.DMA

    def run(latv, teachv, condv, latp, teachp, condp, smallv, trig, cos, low, high, x, h, qkv, a, lse, st, w, vec, ssem, lsem, sem):
        ins = [local(k.lat, latv, sem.at[0]), local(k.teach, teachv, sem.at[1]), local(k.cond, condv, sem.at[2]), local(k.trig, trig, sem.at[4])]
        start_all(ins)
        rowg = RowGather(at, [(latp, k.x0), (smallv, k.vecs), (condp, k.cond_full), (teachp, k.teach_full)], ssem, k.row_sem, lsem)
        ins[0].wait()
        pad_into(latp, latv, LEN)
        smallv[...] = jnp.zeros_like(smallv)
        for j in range(6):
            smallv[j, :] = k.small[j][...]
        at.enter(True, diagonal=True)
        rowg.start(0)
        rowg.start(1)
        gather.begin()
        wait_all(ins[1:3])
        pad_into(condp, condv, CLEN)
        pad_into(teachp, teachv, LEN)
        ins[3].wait()
        spread_tables(trig, cos, low, high)
        gather.advance(0)
        rowg.forward(0)
        rowg.forward(1)
        gather.advance(1)
        rowg.finish(0)
        rowg.finish(1)
        more = [local(k.x0, x, sem.at[0]), local(k.vecs, vec, sem.at[1])]
        start_all(more)
        rowg.start(2)
        rowg.start(3)
        wait_all(more)

        def norm(b):
            rows = pl.ds(pl.multiple_of(b * SUB, SUB), SUB)
            v = x[rows].astype(F32)
            mean = jnp.sum(v, axis=1, keepdims=True) * (1.0 / wide)
            xc = v - mean
            inv = lax.rsqrt(jnp.sum(xc * xc, axis=1, keepdims=True) * (1.0 / wide) + EPSILON)
            h[rows] = (xc * inv * vec[0:1] + vec[1:2]).astype(BF)
            st[rows] = jnp.where(lanes((SUB, 128)) == 2, mean, inv)

        each(0, TP // SUB, norm)
        outs = [local(h, k.h1, sem.at[2]), local(st, k.st1, sem.at[3])]
        start_all(outs)
        gather.advance(2)
        rowg.forward(2)
        fetch = lambda p: local(gather.pieces[p][1], w.at[p % 2], sem.at[4 + p % 2])
        gather.finish(0)
        fetch(0).start()
        for part in range(3):
            fetch(part).wait()
            gather.advance(3 + part)
            if part < 2:
                gather.finish(part + 1)
                fetch(part + 1).start()

            def project(i):
                rows = rows_of(i)
                c, lo, hi = cos[rows], low[rows], high[rows]
                res = nn(h[rows], w[part % 2])
                for pair in range(f // 128):
                    u = res[:, pair * 128:(pair + 1) * 128]
                    if part < 2:
                        u = rotate_lanes(u, c, lo, hi).astype(BF)
                    else:
                        u = u.astype(BF)
                    if part == 0:
                        u = u * HEAD ** (-0.5)
                    qkv[rows, part * f + pair * 128:part * f + (pair + 1) * 128] = u

            each(0, NCH, project)

        def attend(i):
            def hook(pair):
                for p in range(6, k.front_pieces):
                    pl.when(i * 3 + pair == (p - 6) * 15 // (k.front_pieces - 6))(lambda: gather.advance(p))

            attend_step(i, qkv, 0, qkv, f, qkv, 2 * f, TP, LEN, a, lse, f // HEAD, hook)

        each(0, NCH, attend)
        last = [local(qkv, k.qkv, sem.at[0]), local(a, k.a, sem.at[1]), local(lse, k.lse1, sem.at[6])]
        start_all(last)
        rowg.forward(3)
        rowg.finish(2)
        rowg.finish(3)
        wait_all(outs + last)

    vm = pltpu.VMEM
    pl.run_scoped(
        run,
        latv=vm((LEN, f), BF), teachv=vm((LEN, f), BF), condv=vm((CLEN, f), BF), latp=vm((TP, f), BF), teachp=vm((TP, f), BF),
        condp=vm((CP, f), BF), smallv=vm((8, f), F32), trig=vm((TP, 128), F32), cos=vm((TP, 128), F32), low=vm((TP, 128), F32),
        high=vm((TP, 128), F32), x=vm((TP, wide), BF), h=vm((TP, wide), BF), qkv=vm((TP, 3 * f), BF), a=vm((TP, f), BF),
        lse=vm((TP, 128), F32), st=vm((TP, 128), F32), w=vm((2, wide, f), BF), vec=vm((8, wide), F32),
        ssem=dma((4, 3)), lsem=dma((4,)), sem=dma((7,)),
    )


def mid_phase(k, gather, first, second):
    at, f, wide = k.at, k.f, k.wide
    dma, vm = pltpu.SemaphoreType.DMA, pltpu.VMEM
    slots = list(range(k.front_pieces, k.mid_pieces))

    def run(a, x0, x, low, wo, wq, wk, wv, wc, cq, ckv, c, lse, cond, vec, acc, sem, osem, esem):
        first.acc, second.acc = acc, acc
        for p in range(3, 8):
            gather.finish(p)
        loads = [
            local(src, dst, sem.at[j])
            for j, (src, dst) in enumerate(
                ((k.a, a), (k.full[3], wo), (k.full[5], wk), (k.full[6], wv), (k.cond_full, cond), (k.x0, x0), (k.full[4], wq), (k.full[7], wc), (k.vecs, vec))
            )
        ]
        start_all(loads)
        wait_all(loads[:2])

        def project(i):
            first.partial(i, [(a[rows_of(i)], wo)])
            pl.when(i > 0)(lambda: first.swap(i - 1))

        each(0, NCH, project)
        first.swap(NCH - 1)
        wait_all(loads[2:])
        ckv[:, :f] = nn(cond[...], wk[...]).astype(BF)
        ckv[:, f:] = nn(cond[...], wv[...]).astype(BF)

        def outs(i, main, lowest, which):
            return [
                local(x.at[rows_of(i)], main.at[rows_of(i)], osem.at[which, 2 * i]),
                local(low.at[rows_of(i)], lowest.at[rows_of(i)], osem.at[which, 2 * i + 1]),
            ]

        def hook(slot, base):
            for j, p in enumerate(slots):
                spot = j * 2 * NCH // len(slots)
                if base <= spot < base + NCH:
                    pl.when(slot == spot - base)(lambda: gather.advance(p))

        def cross(i):
            first.ready(i)

            def block(b, rs, ls):
                v = x0[rs].astype(F32) + first.total(rs)
                x[rs] = v
                low[rs] = (row_stats(v, wide)[0] * vec[2:3] + vec[3:4]).astype(BF)

            sub_blocks(i, block)
            start_all(outs(i, k.x1, k.h2, 0))
            rows = rows_of(i)
            cq[rows] = nn(low[rows], wq[...]).astype(BF) * HEAD ** (-0.5)
            attend_step(i, cq, 0, ckv, 0, ckv, f, CP, CLEN, c, lse, f // HEAD)
            first.drain(i)
            second.partial(i, [(c[rows], wc)])
            pl.when(i > 0)(lambda: second.swap(i - 1))

        def step(i):
            first.share(i)
            pl.when(i > 0)(lambda: cross(i - 1))
            hook(i, 0)

        each(0, NCH, step)
        cross(NCH - 1)
        second.swap(NCH - 1)
        ends = [local(cq, k.cq, esem.at[0]), local(ckv, k.ckv, esem.at[1]), local(c, k.c, esem.at[2]), local(lse, k.lse2, esem.at[3])]
        start_all(ends)

        def last(i):
            second.ready(i)
            wait_all(outs(i, k.x1, k.h2, 0))

            def block(b, rs, ls):
                v = x[rs] + second.total(rs)
                x[rs] = v
                low[rs] = (row_stats(v, wide)[0] * vec[4:5] + vec[5:6]).astype(BF)

            sub_blocks(i, block)
            start_all(outs(i, k.x2, k.h3, 1))

        def step_two(i):
            second.share(i)
            pl.when(i > 0)(lambda: last(i - 1))
            hook(i, NCH)

        each(0, NCH, step_two)
        last(NCH - 1)

        def end(i):
            second.drain(i)
            wait_all(outs(i, k.x2, k.h3, 1))

        each(0, NCH, end)
        wait_all(ends)

    weight = lambda: vm((wide, f), BF)
    pl.run_scoped(
        run,
        a=vm((TP, f), BF), x0=vm((TP, wide), BF), x=vm((TP, wide), F32), low=vm((TP, wide), BF), wo=weight(), wq=weight(), wk=weight(),
        wv=weight(), wc=weight(), cq=vm((TP, f), BF), ckv=vm((CP, 2 * f), BF), c=vm((TP, f), BF), lse=vm((TP, 128), F32),
        cond=vm((CP, wide), BF), vec=vm((8, wide), F32), acc=vm((2, CH, wide // 2), F32), sem=dma((9,)), osem=dma((2, 2 * NCH)), esem=dma((4,)),
    )


def mlp_phase(k, gather, red, nxt, h, hid, sg, tt, dm):
    at, f, wide = k.at, k.f, k.wide
    dma, vm = pltpu.SemaphoreType.DMA, pltpu.VMEM
    parts = k.parts
    col = lambda j: slice(j * f, (j + 1) * f)
    own = pl.ds(pl.multiple_of(at.r * f, 128), f)

    def run(wg, wu, wd, acc, xbuf, tbuf, sq, sem, wsem, xsem, tsem, rsem, ysem):
        red.acc, nxt.acc = acc, acc
        hcp = local(k.h3, h, sem.at[0])
        hcp.start()
        sq[...] = jnp.zeros_like(sq)

        def slot_in(i):
            s = lax.rem(i, 2)
            return [local(k.x2.at[rows_of(i)], xbuf.at[s], xsem.at[s]), local(k.teach_full.at[rows_of(i)], tbuf.at[s], tsem.at[s])]

        for i in range(2):
            start_all(slot_in(i))
        pending = list(range(k.mid_pieces, len(gather.pieces)))

        def fetch(p):
            q, j = (p - 8) % 2 if p < 16 else 2, (p - 8) // 2 if p < 16 else p - 16
            return local(gather.pieces[p][1], (wg, wu, wd)[q].at[:, col(j)], wsem.at[p - 8])

        done = [8]

        def bring(upto):
            while done[0] <= upto:
                while pending and pending[0] <= done[0] + 1:
                    gather.advance(pending.pop(0))
                gather.finish(done[0])
                fetch(done[0]).start()
                done[0] += 1

        bring(9)
        hcp.wait()
        for j in range(parts):
            if j < parts - 1:
                bring(11 + 2 * j)
            fetch(8 + 2 * j).wait()
            fetch(9 + 2 * j).wait()

            def hidden(i):
                rows = rows_of(i)
                gate = nn(h[rows], wg[:, col(j)])
                up = nn(h[rows], wu[:, col(j)])
                sig = jax.nn.sigmoid(gate)
                act = gate * sig
                hid[rows, col(j)] = (act * up).astype(BF)
                sg[rows, col(j)] = act.astype(BF)
                tt[rows, col(j)] = (up * sig * (1.0 + gate * (1.0 - sig))).astype(BF)

            each(0, NCH, hidden)
            if pending:
                gather.advance(pending.pop(0))
        bring(15 + parts)
        for j in range(parts):
            fetch(16 + j).wait()

        def project(i):
            red.partial(i, [(hid[rows_of(i)], wd)])
            pl.when(i > 0)(lambda: red.swap(i - 1))

        each(0, NCH, project)
        red.swap(NCH - 1)

        def outs_of(i):
            s = lax.rem(i, 2)
            return [local(xbuf.at[s], k.res.at[rows_of(i)], rsem.at[s]), local(tbuf.at[s, :, own], k.y.at[rows_of(i)], ysem.at[s])]

        def finish(i):
            s = lax.rem(i, 2)
            red.ready(i)

            @pl.when(i >= 1)
            def _():
                wait_all(outs_of(i - 1))
                pl.when(i < NCH - 1)(lambda: start_all(slot_in(i + 1)))

            wait_all(slot_in(i))

            def block(b, rs, ls):
                y = xbuf[s, ls] + red.total(rs)
                pos = i * CH + b * SUB + lax.broadcasted_iota(jnp.int32, (SUB, wide), 0)
                res = jnp.where(pos < LEN, y - tbuf[s, ls].astype(F32), 0.0)
                xbuf[s, ls] = res
                dm[rs] = res.astype(BF)
                tbuf[s, ls] = y.astype(BF)
                sq_ = res * res
                sq[...] += sq_[:8] + sq_[8:]

            sub_blocks(i, block)
            start_all(outs_of(i))
            rows = rows_of(i)
            for j in range(parts):
                dh = nn(dm[rows], wd[:, col(j)])
                tt[rows, col(j)] = (dh * tt[rows, col(j)].astype(F32)).astype(BF)
                sg[rows, col(j)] = (dh * sg[rows, col(j)].astype(F32)).astype(BF)
            red.drain(i)
            nxt.partial(i, [(tt[rows], wg), (sg[rows], wu)])
            pl.when(i > 0)(lambda: nxt.swap(i - 1))

        def step(i):
            red.share(i)
            pl.when(i > 0)(lambda: finish(i - 1))

        each(0, NCH, step)
        finish(NCH - 1)
        nxt.swap(NCH - 1)
        scp = local(sq, k.squares, sem.at[0])
        scp.start()
        wait_all(outs_of(NCH - 1))
        scp.wait()

    weight = lambda: vm((wide, parts * f), BF)
    pl.run_scoped(
        run,
        wg=weight(), wu=weight(), wd=weight(), acc=vm((2, CH, wide // 2), F32), xbuf=vm((2, CH, wide), F32), tbuf=vm((2, CH, wide), BF),
        sq=vm((8, wide), F32), sem=dma((1,)), wsem=dma((3 * parts,)), xsem=dma((2,)), tsem=dma((2,)),
        rsem=dma((2,)), ysem=dma((2,)),
    )


class Grads:
    def __init__(self, part, stage, sem, f):
        self.part, self.stage, self.sem, self.f = part, stage, sem, f

    def copy(self, p):
        return local(self.stage, self.part.at[:, p * self.f:(p + 1) * self.f], self.sem.at[p % 2])

    def make(self, p, left, right):
        wide = left.shape[1]

        def one(j):
            cols = pl.ds(pl.multiple_of(j * 512, 128), 512)
            self.stage[cols] = tn(left[:, cols], right()).astype(BF)

        each(0, wide // 512, one)
        self.copy(p).start()


def mid_back_phase(k, scatter, first, second, h, hid, sg, tt, dm):
    at, f, wide = k.at, k.f, k.wide
    dma, vm = pltpu.SemaphoreType.DMA, pltpu.VMEM

    def run(g, low, xs, wc, wq, dkv, dc, cq, ckv, c, lse, dcq, sums, vec, acc, stage, sem, xsem, osem, gsem):
        second.acc = acc
        grads = Grads(k.part, stage, gsem, f)
        rest = [
            local(src, dst, sem.at[j])
            for j, (src, dst) in enumerate(((k.res, g), (k.full[7], wc), (k.full[4], wq), (k.cq, cq), (k.ckv, ckv), (k.c, c), (k.lse2, lse), (k.vecs, vec)))
        ]
        start_all(rest)

        def stream(src, i, s):
            return local(src.at[rows_of(i)], xs.at[s], xsem.at[s])

        stream(k.x2, 0, 0).start()
        stream(k.x2, 1, 1).start()
        sums[...] = jnp.zeros_like(sums)
        dkv[...] = jnp.zeros_like(dkv)

        def make(p):
            q, j = p // 4, p % 4
            left, right = ((h, tt), (h, sg), (dm, hid))[q]
            grads.make(p, left, lambda: right[:, j * f:(j + 1) * f])

        for p in range(2):
            make(p)
            grads.copy(p).wait()
            scatter.start(p)
        wait_all(rest)

        def hook(slot, base):
            for p in range(base + 2, base + 2 + NCH):
                @pl.when(slot == p - 2 - base)
                def _():
                    make(p)
                    grads.copy(p).wait()
                    if p < scatter.ahead:
                        scatter.start(p)

            for p in range(k.back_pieces):
                spot = p * 2 * NCH // k.back_pieces + 1
                if base <= spot < base + NCH:
                    pl.when(slot == spot - base)(lambda: scatter.advance(p))

        def low_out(i, which):
            return local(low.at[lax.rem(i + which * NCH, 2)], (k.dco, k.do)[which].at[rows_of(i)], osem.at[which, i])

        def g_out(i):
            return local(g.at[rows_of(i)], k.g1.at[rows_of(i)], osem.at[2, i])

        valid = lambda: lax.broadcasted_iota(jnp.int32, (CP, 1), 0) < CLEN

        def cross(i):
            first.ready(i)
            s = lax.rem(i, 2)
            stream(k.x2, i, s).wait()
            pl.when(i >= 2)(lambda: low_out(i - 2, 0).wait())

            def block(b, rs, ls):
                tot = first.total(rs)
                new, dx = norm_back(tot, xs[s, ls], g[rs], vec[4:5], wide)
                g[rs] = new
                low[s, ls] = new.astype(BF)
                fold(sums, 0, dx)
                fold(sums, 1, tot)

            sub_blocks(i, block)
            pl.when(i < NCH - 2)(lambda: stream(k.x2, i + 2, s).start())
            pl.when(i >= NCH - 2)(lambda: stream(k.x1, i + 2 - NCH, s).start())
            low_out(i, 0).start()
            rows = rows_of(i)
            dc[...] = nn(low[s], wc[...]).astype(BF)
            lse_t = lse[rows].T
            delta = jnp.zeros((CH, 128), F32)
            for pair in range(f // 128):
                cols = slice(128 * pair, 128 * (pair + 1))
                prod = dc[:, cols].astype(F32) * c[rows, cols].astype(F32)
                for which in range(2):
                    one = jnp.sum(head_mask(prod, which), axis=1, keepdims=True)
                    delta = jnp.where(lanes(delta.shape) == 2 * pair + which, one, delta)
            delta_t = delta.T
            for pair in range(f // 128):
                cols = slice(128 * pair, 128 * (pair + 1))
                vcols = slice(f + 128 * pair, f + 128 * (pair + 1))
                kb, vb, qc, doc = ckv[:, cols], ckv[:, vcols], cq[rows, cols], dc[:, cols]
                dks, dvs, dqt = [], [], None
                for which in range(2):
                    hd = 2 * pair + which
                    km = head_mask(kb, which)
                    p = jnp.where(valid(), jnp.exp(nt(km, qc) - lse_t[hd:hd + 1]), 0.0)
                    dp = nt(head_mask(vb, which), doc)
                    ds = (p * (dp - delta_t[hd:hd + 1])).astype(BF)
                    dvs.append(nn(p.astype(BF), doc))
                    dks.append(nn(ds, qc))
                    part = nn(km.T, ds)
                    dqt = part if dqt is None else dqt + part
                left = lanes(dks[0].shape) < HEAD
                dkv[:, cols] += jnp.where(left, dks[0], dks[1])
                dkv[:, vcols] += jnp.where(left, dvs[0], dvs[1])
                dcq[rows, cols] = (dqt.T * HEAD ** (-0.5)).astype(BF)
            first.drain(i)
            second.partial(i, [(dcq[rows], wq)])
            pl.when(i > 0)(lambda: second.swap(i - 1))

        def step(i):
            first.share(i)
            pl.when(i > 0)(lambda: cross(i - 1))
            hook(i, 0)

        each(0, NCH, step)
        cross(NCH - 1)
        second.swap(NCH - 1)
        ckv[...] = dkv[...].astype(BF)

        def last(i):
            second.ready(i)
            s = lax.rem(i + NCH, 2)
            stream(k.x1, i, s).wait()
            pl.when(i < 2)(lambda: low_out(NCH - 2 + i, 0).wait())
            pl.when(i >= 2)(lambda: low_out(i - 2, 1).wait())

            def block(b, rs, ls):
                tot = second.total(rs)
                new, dx = norm_back(tot, xs[s, ls], g[rs], vec[2:3], wide)
                g[rs] = new
                low[s, ls] = new.astype(BF)
                fold(sums, 2, dx)
                fold(sums, 3, tot)

            sub_blocks(i, block)
            pl.when(i < NCH - 2)(lambda: stream(k.x1, i + 2, s).start())
            low_out(i, 1).start()
            g_out(i).start()

        def step_two(i):
            second.share(i)
            pl.when(i > 0)(lambda: last(i - 1))
            hook(i, NCH)

        each(0, NCH, step_two)
        last(NCH - 1)
        ends = [local(dcq, k.dcq, sem.at[0]), local(ckv, k.dckv, sem.at[1]), local(sums, k.sums, sem.at[2])]
        start_all(ends)

        def end(i):
            second.drain(i)
            pl.when(i >= NCH - 2)(lambda: low_out(i, 1).wait())
            g_out(i).wait()

        each(0, NCH, end)
        wait_all(ends)

    pl.run_scoped(
        run,
        g=vm((TP, wide), F32), low=vm((2, CH, wide), BF), xs=vm((2, CH, wide), F32), wc=vm((wide, f), BF), wq=vm((wide, f), BF),
        dkv=vm((CP, 2 * f), F32), dc=vm((CH, f), BF), cq=vm((TP, f), BF), ckv=vm((CP, 2 * f), BF), c=vm((TP, f), BF),
        lse=vm((TP, 128), F32), dcq=vm((TP, f), BF), sums=vm((4, 8, wide), F32), vec=vm((8, wide), F32), acc=vm((2, CH, wide // 2), F32),
        stage=vm((wide, f), BF), sem=dma((8,)), xsem=dma((2,)), osem=dma((3, NCH)), gsem=dma((2,)),
    )


def end_phase(k, scatter):
    at, f, wide = k.at, k.f, k.wide
    dma, vm = pltpu.SemaphoreType.DMA, pltpu.VMEM
    r, c_, o = at.r, at.c, at.o
    own = pl.ds(pl.multiple_of(r * f, 128), f)
    send_a, recv_a = k.send_a, k.recv_a
    send_b, recv_b = k.p1.at[0, :, :f], k.p2.at[0, :, :f]

    def run(xa, xb, wt, w1, da, dqkv, lse_t, delta_t, dqt, stage, xo, go, g1, tot, acc, st, back, st_t, cpart, qkv, a, lse, trig,
            cos, low, high, c, dcq, dckv, cond, sums, sq, vr, vb, lat, gc, sem, gsem, s_c, s_x, s_v):
        grads = Grads(k.part, stage, gsem, f)
        names = {}

        def load(name, src, dst):
            names[name] = local(src, dst, sem.at[len(names)])
            names[name].start()

        load("do", k.do, xa)
        load("wo", k.full[3], wt)
        load("a", k.a, a)
        load("qkv", k.qkv, qkv)
        load("lse", k.lse1, lse)
        load("trig", k.trig, trig)
        load("h2", k.h2, xb)
        load("c", k.c, c)
        load("dcq", k.dcq, dcq)
        load("dckv", k.dckv, dckv)
        load("cond", k.cond_full, cond)
        rest = ["st", "xo", "go", "g1", "sums", "sq"]
        for name, src, dst in (
            ("st", k.st1, st), ("xo", k.x0.at[:, own], xo), ("go", k.vecs.at[:, own], go), ("g1", k.g1.at[:, own], g1),
            ("sums", k.sums.at[:, :, own], sums), ("sq", k.squares, sq),
        ):
            load(name, src, dst)
        for j in range(3):
            load(f"w{j}", k.full[j], w1.at[:, j * f:(j + 1) * f])
            rest.append(f"w{j}")

        def ready(*which):
            for name in which:
                names[name].wait()

        def make(p, left, right):
            grads.make(p, left, right)
            grads.copy(p).wait()

        ready("do", "wo", "a")

        def project_da(i):
            da[rows_of(i)] = nn(xa[rows_of(i)], wt[...]).astype(BF)

        each(0, NCH, project_da)
        make(12, xa, lambda: a[...])
        again = local(k.dco, xa, sem.at[0])
        again.start()
        wck_cp = local(k.full[5], wt, sem.at[1])
        wck_cp.start()
        nxt = k.back_pieces
        scatter.advance(nxt)
        nxt = nxt + 1
        ready("h2", "c", "dcq", "dckv", "cond")
        again.wait()
        make(13, xa, lambda: c[...])
        make(14, xb, lambda: dcq[...])
        h1_cp = local(k.h1, xb, sem.at[0])
        h1_cp.start()
        make(15, cond, lambda: dckv[:, :f])
        make(16, cond, lambda: dckv[:, f:])
        ready("qkv", "lse", "trig")
        spread_tables(trig, cos, low, high)

        def emit_q(pair, dq):
            dqkv[:, 128 * pair:128 * (pair + 1)] = rotate_lanes(dq * HEAD ** (-0.5), cos[...], -low[...], -high[...]).astype(BF)

        def emit_kv(pair, rows, dk, dv):
            dqkv[rows, f + 128 * pair:f + 128 * (pair + 1)] = rotate_lanes(dk, cos[rows], -low[rows], -high[rows]).astype(BF)
            dqkv[rows, 2 * f + 128 * pair:2 * f + 128 * (pair + 1)] = dv.astype(BF)


        def hook(pair, j):
            for step, spot in enumerate(k.end_spots):
                if spot[0] == pair:
                    pl.when(j == spot[1])(lambda: scatter.advance(nxt + step))

        attend_back(qkv, 0, qkv, f, qkv, 2 * f, TP, CH, LEN, da, a, lse, lse_t, delta_t, dqt, emit_q, emit_kv, f // HEAD, hook)
        nxt = nxt + len(k.end_spots)

        h1_cp.wait()
        for j in range(3):
            make(17 + j, xb, lambda: dqkv[:, j * f:(j + 1) * f])
        scatter.advance(nxt)

        wck_cp.wait()
        for j in range(4):
            cpart[j] = nt(dckv[:, :f], wt[j * f:(j + 1) * f])
        wcv_cp = local(k.full[6], wt, sem.at[1])
        wcv_cp.start()
        scatter.advance(nxt + 1)
        wcv_cp.wait()
        crecv = k.crecv
        for j in range(4):
            crecv[j] = (cpart[j] + nt(dckv[:, f:], wt[j * f:(j + 1) * f])).astype(BF)
        peers = (at.sib, at.par, at.diag)
        cond_cps = [remote(crecv.at[peers[j][0]], crecv.at[4 + j], s_c.at[j], k.r_c.at[j], peers[j]) for j in range(3)]
        start_all(cond_cps)
        ready(*rest)

        wblock = lambda j: w1[pl.ds(pl.multiple_of(j * f, 128), f)]

        def copy_a(i):
            return remote(send_a.at[rows_of(i)], recv_a.at[rows_of(i)], k.e_sa.at[i], k.e_ra.at[i], at.sib)

        def copy_b(i):
            return remote(send_b.at[rows_of(i)], recv_b.at[rows_of(i)], k.e_sb.at[i], k.e_rb.at[i], at.par)

        def swap(i):
            copy_a(i).wait_recv()
            both = acc[lax.rem(i, 2)] + recv_a[rows_of(i)].astype(F32)
            left, right = both[:, :f], both[:, f:]
            tot[rows_of(i)] = jnp.where(at.xi == 0, left, right)
            send_b[rows_of(i)] = jnp.where(at.xi == 0, right, left).astype(BF)
            pl.semaphore_wait(k.last_sum.free.at[i], 1)
            copy_b(i).start()

        def project(i):
            y = dqkv[rows_of(i)]
            send_a[rows_of(i), :f] = nt(y, wblock(o)).astype(BF)
            send_a[rows_of(i), f:] = nt(y, wblock(2 + o)).astype(BF)
            copy_a(i).start()
            acc[lax.rem(i, 2), :, :f] = nt(y, wblock(c_))
            acc[lax.rem(i, 2), :, f:] = nt(y, wblock(2 + c_))
            pl.when(i > 0)(lambda: swap(i - 1))

        each(0, NCH, project)
        swap(NCH - 1)
        vr[...] = jnp.zeros_like(vr)
        scatter.advance(nxt + 2)

        def sums_of(i):
            copy_b(i).wait_recv()

            def block(b, rs, ls):
                t = tot[rs] + recv_b[rs].astype(F32)
                tot[rs] = t
                own_st = st[rs]
                mean, inv = own_st[:, 2:3], own_st[:, 3:4]
                xh = (xo[rs].astype(F32) - mean) * inv
                e = t * go[0:1]
                lane = lanes((SUB, 128))
                first = jnp.sum(e, axis=1, keepdims=True)
                cross = jnp.sum(e * xh, axis=1, keepdims=True)
                back[rs] = jnp.where(lane == 0, first, cross)
                fold(vr, 0, t * xh)
                fold(vr, 1, t)

            sub_blocks(i, block)

        each(0, NCH, sums_of)
        sx = k.sx
        st_t[...] = back[...].T
        sx[0] = st_t[:8]
        stat_cps = [remote(sx.at[0], sx.at[1 + j], s_x.at[j], k.r_x.at[j], peers[j]) for j in range(3)]
        start_all(stat_cps)
        total = lambda x: jnp.sum(x, axis=0, keepdims=True)
        error = jnp.sum(total(sq[...]), axis=1, keepdims=True)
        vb[0:1] = total(vr[0])
        vb[1:2] = total(vr[1])
        vb[2:3] = total(sums[2])
        vb[3:4] = total(sums[3])
        vb[4:5] = total(sums[0])
        vb[5:6] = total(sums[1])
        vb[6:8] = jnp.broadcast_to(error, (2, f))
        vz = k.vz
        pair_cp = remote(vb, vz.at[at.outer], s_v.at[at.outer], k.r_v.at[at.outer], at.ypar)
        pair_cp.start()
        scatter.advance(nxt + 3)
        for cp in cond_cps:
            cp.wait_recv()
        gc[...] = (crecv[r].astype(F32) + crecv[4].astype(F32) + crecv[5].astype(F32) + crecv[6].astype(F32)).astype(BF)
        for cp in stat_cps:
            cp.wait_recv()
        st_t[:8] = sx[0] + sx[1] + sx[2] + sx[3]
        back[...] = st_t[...].T
        pair_cp.wait()
        vz[at.zo] = vb[...] + vz[at.outer]

        def vec_out(step):
            return remote(vz.at[at.zo], vz.at[at.zo], s_v.at[step], k.r_v.at[at.zo], (r, 2 * at.zpeer(step) + at.yi))

        each(1, at.outer, lambda step: vec_out(step).start())

        def last(i):
            def block(b, rs, ls):
                e = tot[rs] * go[0:1]
                row_sums, own_st = back[rs], st[rs]
                first, cross = row_sums[:, 0:1] * (1.0 / wide), row_sums[:, 1:2] * (1.0 / wide)
                mean, inv = own_st[:, 2:3], own_st[:, 3:4]
                xh = (xo[rs].astype(F32) - mean) * inv
                lat[rs] = (g1[rs] + inv * (e - first - xh * cross)).astype(BF)

            sub_blocks(i, block)

        each(0, NCH, last)
        outs = [local(lat, k.glat, sem.at[0]), local(gc, k.gcond, sem.at[1])]
        start_all(outs)
        for p in range(nxt + 4, len(scatter.pieces)):
            scatter.advance(p)
        vb[...] = vz[at.zo]

        def vec_in(step):
            zs = at.zpeer(at.outer - step)
            remote(vz.at[zs], vz.at[zs], s_v.at[step], k.r_v.at[zs], at.ypar).wait_recv()
            vb[...] += vz[zs]

        each(1, at.outer, vec_in)
        vec_cp = local(vb, k.vec, sem.at[2])
        vec_cp.start()
        each(1, at.outer, lambda step: vec_out(step).wait_send())
        scatter.complete()
        for cp in stat_cps + cond_cps:
            cp.wait_send()

        def drain(i):
            copy_a(i).wait_send()
            copy_b(i).wait_send()

        each(0, NCH, drain)
        wait_all(outs + [vec_cp])

    tab = lambda: vm((TP, 128), F32)
    flip = lambda: vm((128, TP), F32)
    pl.run_scoped(
        run,
        xa=vm((TP, wide), BF), xb=vm((TP, wide), BF), wt=vm((wide, f), BF), w1=vm((wide, 3 * f), BF), da=vm((TP, f), BF),
        dqkv=vm((TP, 3 * f), BF), lse_t=flip(), delta_t=flip(), dqt=flip(), stage=vm((wide, f), BF), xo=vm((TP, f), BF),
        go=vm((8, f), F32), g1=vm((TP, f), F32), tot=vm((TP, f), F32), acc=vm((2, CH, 2 * f), F32), st=tab(), back=tab(), st_t=flip(),
        cpart=vm((4, CP, f), F32), qkv=vm((TP, 3 * f), BF), a=vm((TP, f), BF), lse=tab(), trig=tab(), cos=tab(), low=tab(), high=tab(),
        c=vm((TP, f), BF), dcq=vm((TP, f), BF), dckv=vm((CP, 2 * f), BF), cond=vm((CP, wide), BF), sums=vm((4, 8, f), F32),
        sq=vm((8, wide), F32), vr=vm((2, 8, f), F32), vb=vm((8, f), F32), lat=vm((TP, f), BF), gc=vm((CP, f), BF),
        sem=dma((24,)), gsem=dma((2,)), s_c=dma((3,)), s_x=dma((3,)), s_v=dma((k.outer + 1,)),
    )


class Names:
    pass


def layer_kernel(n, f, pieces, front_pieces, mid_pieces, back_pieces, ahead, s_ahead, slots, *refs):
    refs = list(refs)
    take = lambda count: [refs.pop(0) for _ in range(count)]
    k = Names()
    k.at, k.f, k.wide, k.outer = Place(n), f, 4 * f, n // 2
    k.front_pieces, k.mid_pieces, k.back_pieces = front_pieces, mid_pieces, back_pieces
    k.end_spots = ((0, 2), (1, 0), (1, 3), (2, 2))
    k.lat, k.teach, k.cond, k.trig = take(4)
    k.small = take(6)
    shards = take(11)
    k.y, k.glat, k.gcond, k.vec = take(4)
    gate_out, up_out, down_out = take(3)
    square_out = take(8)
    k.full = take(8)
    mlp_full = take(3)
    k.x0, k.vecs, k.cond_full, k.teach_full, k.h1, k.st1, k.qkv, k.a, k.lse1 = take(9)
    k.x1, k.h2, k.cq, k.ckv, k.c, k.lse2, k.x2, k.h3 = take(8)
    k.res, k.squares, k.g1, k.dco, k.do, k.dcq, k.dckv, k.sums, k.part = take(9)
    k.send_a, k.recv_a, k.p1, k.p2, k.sx, k.crecv, k.vz = take(7)
    sems = [take(8) for _ in range(5)]
    free = take(5)
    k.e_sa, k.e_ra, k.e_sb, k.e_rb, k.row_sem, k.r_c, k.r_x, k.r_v = take(8)
    gather_sem = take(3)
    bufs, scatter_sem = take(5), take(8)
    k.parts = shards[8].shape[1] // f
    col = lambda j: slice(j * f, (j + 1) * f)
    made = [(shards[j], k.full[j]) for j in range(8)]
    for j in range(k.parts):
        for q in range(2):
            made.append((shards[8 + q].at[:, col(j)], mlp_full[q].at[:, col(j)]))
    made += [(shards[10].at[:, col(j)], mlp_full[2].at[:, col(j)]) for j in range(k.parts)]
    gather = ColGather(k.at, made, ahead, *gather_sem)
    sums = []
    for q, out in enumerate((gate_out, up_out, down_out)):
        sums += [(k.part.at[:, col(q * k.parts + j)], out.at[:, col(j)]) for j in range(k.parts)]
    sums += [(k.part.at[:, col(3 * k.parts + j)], square_out[j]) for j in range(8)]
    scatter = ColScatter(k.at, sums, s_ahead, slots, bufs, scatter_sem)
    red = [None]
    for j in range(5):
        red.append(RowReduce(k.at, k.send_a, k.recv_a, None, k.p1, k.p2, sems[j], free[j], red[j]))
    red = red[1:]
    k.last_sum = red[4]
    front_phase(k, gather)
    mid_phase(k, gather, red[0], red[1])
    full = pltpu.VMEM((TP, k.wide), BF)

    def back(h, hid, sg, tt, dm):
        mlp_phase(k, gather, red[2], red[3], h, hid, sg, tt, dm)
        mid_back_phase(k, scatter, red[3], red[4], h, hid, sg, tt, dm)

    pl.run_scoped(back, h=full, hid=full, sg=full, tt=full, dm=full)
    end_phase(k, scatter)


def layer_call(n, lat, teach, cond, trig, small, shards, front_pieces=12, mid_pieces=18, back_pieces=9, ahead=4, s_ahead=3, slots=5):
    f = lat.shape[1]
    wide, size, outer = 4 * f, shards[0].shape[0], n // 2
    ffl = shards[8].shape[1]
    sd = jax.ShapeDtypeStruct
    dma = pltpu.SemaphoreType.DMA
    vm = pltpu.VMEM
    half = wide // 2
    results = [sd((TP, f), BF), sd((TP, f), BF), sd((CP, f), BF), sd((8, f), F32)]
    results += [sd((size, ffl), F32)] * 3 + [sd((size, f), F32)] * 8
    between = [sd((wide, f), BF)] * 8 + [sd((wide, ffl), BF)] * 3
    rows, rows32 = sd((TP, wide), BF), sd((TP, wide), F32)
    between += [rows, sd((8, wide), F32), sd((CP, wide), BF), rows, rows, sd((TP, 128), F32), sd((TP, 3 * f), BF), sd((TP, f), BF), sd((TP, 128), F32)]
    between += [rows32, rows, sd((TP, f), BF), sd((CP, 2 * f), BF), sd((TP, f), BF), sd((TP, 128), F32), rows32, rows]
    between += [rows32, sd((8, wide), F32), rows32, rows, rows, sd((TP, f), BF), sd((CP, 2 * f), BF), sd((4, 8, wide), F32), sd((wide, 3 * ffl + 8 * f), BF)]
    pieces = 8 + 3 * ffl // f
    scratch = [
        vm((TP, half), BF), vm((TP, half), BF), vm((2, TP, half), BF), vm((2, TP, half), BF),
        vm((4, 8, TP), F32), vm((7, CP, f), BF), vm((outer + 1, 8, f), F32),
    ] + [dma((NCH,))] * 40 + [pltpu.SemaphoreType.REGULAR((NCH,))] * 5 + [dma((NCH,))] * 4 + [dma((4, 3)), dma((3,)), dma((3,)), dma((outer + 1,))]
    bufs, sems = scatter_scratch(pieces, slots, n, f, wide)
    scratch += gather_sems(pieces, n) + bufs + sems
    out = pl.pallas_call(
        functools.partial(layer_kernel, n, f, pieces, front_pieces, mid_pieces, back_pieces, ahead, s_ahead, slots),
        out_shape=results + between,
        in_specs=[hspec()] * 4 + [vspec()] * 6 + [hspec()] * 11,
        out_specs=[hspec()] * (len(results) + len(between)),
        scratch_shapes=scratch,
        compiler_params=pltpu.CompilerParams(collective_id=0, has_side_effects=True, vmem_limit_bytes=66_900_000),
        name="layer",
    )(lat, teach, cond, trig, *small, *shards)
    return out[:len(results)]


def emit_kernel(n, scale, *refs):
    refs = list(refs)
    take = lambda count: [refs.pop(0) for _ in range(count)]
    moved, grads = take(4), take(11)
    y_out, lat_out, cond_out, vec_out = take(4)
    grad_outs = take(11)
    y, lat, cond, vec, sem, vsem = take(6)
    held = take(11)
    cps = [local(src, dst, sem.at[j]) for j, (src, dst) in enumerate(zip(grads, held))]
    out_cps = [local(src, dst, sem.at[j]) for j, (src, dst) in enumerate(zip(held, grad_outs))]
    ins = [local(src, dst, vsem.at[j]) for j, (src, dst) in enumerate(zip(moved, (y, lat, cond, vec)))]
    start_all(cps + ins)
    for cp, out in zip(cps, out_cps):
        cp.wait()
        out.start()
    wait_all(ins)
    y_out[...] = y[:y_out.shape[0]]
    lat_out[...] = lat[:lat_out.shape[0]]
    cond_out[...] = cond[:cond_out.shape[0]]
    width = vec_out.shape[1]
    v = vec[...]
    rows = lax.broadcasted_iota(jnp.int32, v.shape, 0)
    turned = pltpu.roll(v, lax.rem((n - lax.axis_index("col")) * width, v.shape[1]), 1)
    vec_out[...] = jnp.where(rows == 6, v * scale, turned)[:, :width]
    wait_all(out_cps)


def emit_call(n, scale, y, lat, cond, vec, grads):
    f = y.shape[1]
    sd = jax.ShapeDtypeStruct
    return pl.pallas_call(
        functools.partial(emit_kernel, n, scale),
        out_shape=[sd((LEN, f), BF), sd((LEN, f), BF), sd((CLEN, f), BF), sd((8, f // n), F32)] + [sd(g.shape, F32) for g in grads],
        in_specs=[hspec()] * 15,
        out_specs=[vspec()] * 4 + [hspec()] * 11,
        scratch_shapes=[
            pltpu.VMEM((TP, f), BF), pltpu.VMEM((TP, f), BF), pltpu.VMEM((CP, f), BF), pltpu.VMEM((8, f), F32),
            pltpu.SemaphoreType.DMA((11,)), pltpu.SemaphoreType.DMA((4,)),
        ] + [pltpu.VMEM(g.shape, F32) for g in grads],
        compiler_params=pltpu.CompilerParams(vmem_limit_bytes=62 << 20),
        name="emit",
    )(y, lat, cond, vec, *grads)


def trig_table():
    half_size = ROT // 2
    rates = np.exp(np.arange(half_size) * (-2.0 * math.log(10000.0) / ROT))
    angles = np.arange(TP)[:, None] * rates[None, :]
    table = np.zeros((TP, 128), np.float32)
    table[:, :half_size], table[:, half_size:ROT] = np.cos(angles), np.sin(angles)
    return jnp.asarray(table)


def body(
    latents,
    conditioning,
    teacher,
    gain_attn,
    bias_attn,
    gain_cross,
    bias_cross,
    gain_mlp,
    bias_mlp,
    w_query,
    w_key,
    w_value,
    w_out,
    w_cross_query,
    w_cross_key,
    w_cross_value,
    w_cross_out,
    w_gate,
    w_up,
    w_down,
):

    F = latents.shape[1]
    wide = F * lax.axis_size("row")
    n = lax.axis_size("col")
    y, glat, gcond, vec, *grads = layer_call(
        n, latents, teacher, conditioning, trig_table(), [gain_attn, bias_attn, gain_cross, bias_cross, gain_mlp, bias_mlp],
        [w_query, w_key, w_value, w_out.T, w_cross_query, w_cross_key, w_cross_value, w_cross_out.T, w_gate, w_up, w_down.T],
    )
    outputs, glat, gcond, vec, ggate, gup, gdown, go, gco, gcq, gck, gcv, gq, gk, gv = emit_call(
        n, 1.0 / (LEN * wide * n), y, glat, gcond, vec, grads
    )
    return (
        outputs, vec[6, 0], glat, gcond, gq, gk, gv, go.T, gcq, gck, gcv, gco.T, ggate, gup, gdown.T,
        vec[0], vec[1], vec[2], vec[3], vec[4], vec[5],
    )


def solution(mesh):
    in_specs = (
        P("col", "row"),
        P("col", "row"),
        P("col", "row"),
        P("row"),
        P("row"),
        P("row"),
        P("row"),
        P("row"),
        P("row"),
        P("col", "row"),
        P("col", "row"),
        P("col", "row"),
        P("row", "col"),
        P("col", "row"),
        P("col", "row"),
        P("col", "row"),
        P("row", "col"),
        P("col", "row"),
        P("col", "row"),
        P("row", "col"),
    )
    out_specs = (
        P("col", "row"),
        P(),
        P("col", "row"),
        P("col", "row"),
        P("col", "row"),
        P("col", "row"),
        P("col", "row"),
        P("row", "col"),
        P("col", "row"),
        P("col", "row"),
        P("col", "row"),
        P("row", "col"),
        P("col", "row"),
        P("col", "row"),
        P("row", "col"),
        P(("row", "col")),
        P(("row", "col")),
        P(("row", "col")),
        P(("row", "col")),
        P(("row", "col")),
        P(("row", "col")),
    )
    return jax.shard_map(body, mesh=mesh, in_specs=in_specs, out_specs=out_specs, check_vma=False)
```
